32 devices in a mesh: shot: 8 (over y, x, core), rcv: 4 (over z).
Axes of the slice: x: 2, y: 2, z: 4, core: 2. Of those that a mesh axis runs over, the one named last changes fastest.
Arguments:
- traces: bfloat16 [256, 512, 256], P('shot', 'rcv'), may hold values from -6 to 6
- shift_index: int32 [256, 512], P('shot', 'rcv'), may hold values from 0 to 63
- deconv: float32 [256, 64], P('shot'), may hold values from -0.75 to 0.75
- focal_start: bfloat16 [8, 512, 256], P(None, 'rcv'), may hold values from -6 to 6
- onset_source: int32 [8, 256], P('rcv', 'shot'), may hold values from 32 to 128
- onset_receiver: int32 [8, 512], P('shot', 'rcv'), may hold values from 32 to 128
Outputs:
- upgoing_first: float32 [8, 256, 256], P('rcv', 'shot')
- downgoing: float32 [8, 512, 256], P('shot', 'rcv')
- upgoing_second: float32 [8, 256, 256], P('rcv', 'shot')
The draws below stay inside these ranges and needn't reach their ends.
All inputs are finite; a program needn't handle non-finite values.
Results may differ from the reference program's by a relative error of at most 0.028.
Values may be sent and summed in bfloat16 or wider, within the bound.
No kernel may reach another device: no remote copies, remote signals or barrier semaphores. Data moves between devices by JAX's collectives and lax.ppermute only.
A program may use at most 64 MiB of HBM per device.

```python
import math
import jax
import jax.numpy as jnp
from jax import lax

NT = 256
NF = 128
TAPS = 64
KSHIFT = 64
S_DEV = 32
R_DEV = 128
S = 256
NR = 512
FOC = 8


def place_ends(values, rng, smallest, high):
    longest = values.shape.index(max(values.shape))
    spots = []
    for shift in (0, 1):
        where = [jax.random.randint(jax.random.fold_in(rng, axis), (), 0, length) for axis, length in enumerate(values.shape)]
        where[longest] = (where[longest] + shift) % values.shape[longest]
        spots.append(tuple(where))
    return values.at[spots[0]].set(smallest).at[spots[1]].set(high)


def levels(key, shape, shards, least, high):
    def one(position, parts):
        draws = jax.random.uniform(jax.random.fold_in(jax.random.fold_in(key, 6), position), (parts,), jnp.float32, least / len(shards), high / len(shards))
        return jnp.repeat(jnp.exp(draws), shape[position] // parts).reshape((-1,) + (1,) * (len(shape) - position - 1))

    level = one(*shards[0])
    for cut in shards[1:]:
        level = level * one(*cut)
    return level


def normal_values(stream_key, dims, spread, reach, cuts=(), kind=jnp.bfloat16):
    array = spread * jax.random.normal(stream_key, dims, jnp.float32)
    if cuts:
        array = array * levels(stream_key, dims, cuts, -0.22, 0.18)
    return jnp.clip(array, -reach, reach).astype(kind)


def setup_inputs(seed: int = 0) -> dict:
    splits = jax.random.split(jax.random.key(seed), 7)
    return {
        "traces": normal_values(splits[0], (S, NR, NT), 1.0, 6.0, ((0, 8), (1, 4))),
        "shift_index": place_ends(jax.random.randint(splits[1], (S, NR), 0, KSHIFT), jax.random.fold_in(splits[1], 1), 0, KSHIFT - 1).astype(jnp.int32),
        "deconv": normal_values(splits[2], (S, TAPS), 0.125, 0.75, ((0, 8),), jnp.float32),
        "focal_start": normal_values(splits[3], (FOC, NR, NT), 1.0, 6.0, ((1, 4),)),
        "onset_source": place_ends(jax.random.randint(splits[4], (FOC, S), NT // 8, NT // 2 + 1), jax.random.fold_in(splits[4], 1), NT // 8, (NT // 2 + 1) - 1).astype(jnp.int32),
        "onset_receiver": place_ends(jax.random.randint(splits[5], (FOC, NR), NT // 8, NT // 2 + 1), jax.random.fold_in(splits[5], 1), NT // 8, (NT // 2 + 1) - 1).astype(jnp.int32),
    }


exact_mode = lax.Precision.HIGHEST

def delay_table(tap_count, kind_count):
    tap_index = jnp.arange(tap_count, dtype=jnp.float32)
    fraction = jnp.arange(kind_count, dtype=jnp.float32) * (tap_count / (4.0 * kind_count))
    offset = tap_index[None, :] - 0.375 * tap_count - fraction[:, None]
    window = 0.5 - 0.5 * jnp.cos(2.0 * math.pi * (tap_index + 0.5) / tap_count)
    return jnp.sinc(offset) * window[None, :]

def half_spectrum(signal):
    full_spec = jnp.fft.rfft(signal, n=NT, axis=-1)[..., :NF]
    return (jnp.real(full_spec), jnp.imag(full_spec))

def back_to_time(real_part, imag_part):
    nyquist = jnp.zeros(real_part.shape[:-1] + (NT // 2 + 1 - NF,), real_part.dtype)
    full_spec = jnp.concatenate([real_part, nyquist], axis=-1) + 1j * jnp.concatenate([imag_part, nyquist], axis=-1)
    return jnp.fft.irfft(full_spec, n=NT, axis=-1)

def time_mute(signal, onset):
    sample_index = jnp.arange(NT, dtype=jnp.int32)
    folded = jnp.minimum(sample_index, NT - sample_index)
    return jnp.where(folded[None, None, :] < onset[:, :, None], signal, 0.0)

def reference(traces, shift_index, deconv, focal_start, onset_source, onset_receiver):
    gain_factor = 1.0 / math.sqrt(NT * NR)
    taps_re, taps_im = half_spectrum(delay_table(TAPS, KSHIFT))
    wave_re, wave_im = half_spectrum(deconv)
    start_re, start_im = half_spectrum(focal_start.astype(jnp.float32))
    start_re = start_re.astype(jnp.bfloat16)
    start_im = start_im.astype(jnp.bfloat16)
    blocks = S // S_DEV
    groups = NR // R_DEV
    trace_blocks = traces.reshape(blocks, S_DEV, NR, NT)
    index_blocks = shift_index.reshape(blocks, S_DEV, NR)
    wave_re_blocks = wave_re.reshape(blocks, S_DEV, NF)
    wave_im_blocks = wave_im.reshape(blocks, S_DEV, NF)
    onset_blocks = onset_source.reshape(FOC, blocks, S_DEV).transpose(1, 0, 2)

    def matrix_block(trace_block, index_block, wave_real, wave_imag):
        raw_re, raw_im = half_spectrum(trace_block.astype(jnp.float32))
        delay_re = taps_re[index_block]
        delay_im = taps_im[index_block]
        first_re = raw_re * delay_re - raw_im * delay_im
        first_im = raw_re * delay_im + raw_im * delay_re
        wave_r = wave_real[:, None, :]
        wave_i = wave_imag[:, None, :]
        refl_re = (first_re * wave_r - first_im * wave_i) * gain_factor
        refl_im = (first_re * wave_i + first_im * wave_r) * gain_factor
        return (refl_re.astype(jnp.bfloat16), refl_im.astype(jnp.bfloat16))

    def forward_apply(mat_re, mat_im, vec_re, vec_im):

        def product_term(left_op, right_op):
            left_f = left_op.astype(jnp.float32).reshape(-1, groups, R_DEV, NF)
            right_f = right_op.astype(jnp.float32).reshape(FOC, groups, R_DEV, NF)
            return jnp.einsum('sbdf,pbdf->bpsf', left_f, right_f, precision=exact_mode)
        real_part = product_term(mat_re, vec_re) - product_term(mat_im, vec_im)
        imag_part = product_term(mat_re, vec_im) + product_term(mat_im, vec_re)

        def settle(partial_value):
            return lax.optimization_barrier(jnp.sum(lax.optimization_barrier(partial_value.astype(jnp.bfloat16)).astype(jnp.float32), axis=0))
        return (settle(real_part), settle(imag_part))

    def adjoint_apply(mat_re, mat_im, echo_re, echo_im):

        def product_term(left_op, right_op):
            return jnp.einsum('sdf,psf->pdf', left_op.astype(jnp.float32), right_op.astype(jnp.float32), precision=exact_mode)
        real_part = product_term(mat_re, echo_re) + product_term(mat_im, echo_im)
        imag_part = product_term(mat_re, echo_im) - product_term(mat_im, echo_re)
        return (real_part, imag_part)

    def first_pass(carried, inputs):
        trace_block, index_block, wave_real, wave_imag, onset_block = inputs
        mat_re, mat_im = matrix_block(trace_block, index_block, wave_real, wave_imag)
        sum_re, sum_im = forward_apply(mat_re, mat_im, start_re, start_im)
        minus_block = time_mute(back_to_time(sum_re, sum_im), onset_block)
        echo_re, echo_im = half_spectrum(minus_block)
        echo_re = echo_re.astype(jnp.bfloat16)
        echo_im = echo_im.astype(jnp.bfloat16)
        adj_re, adj_im = adjoint_apply(mat_re, mat_im, echo_re, echo_im)
        return ((carried[0] + adj_re, carried[1] + adj_im), minus_block)
    zero_sums = jnp.zeros((FOC, NR, NF), jnp.float32)
    scan_inputs = (trace_blocks, index_blocks, wave_re_blocks, wave_im_blocks, onset_blocks)
    (adjoint_re, adjoint_im), minus_blocks = lax.scan(first_pass, (zero_sums, zero_sums), scan_inputs)
    upgoing_first = minus_blocks.transpose(1, 0, 2, 3).reshape(FOC, S, NT)
    downgoing = focal_start.astype(jnp.float32) + time_mute(back_to_time(adjoint_re, adjoint_im), onset_receiver)
    plus_re, plus_im = half_spectrum(downgoing)
    plus_re = plus_re.astype(jnp.bfloat16)
    plus_im = plus_im.astype(jnp.bfloat16)

    def second_pass(carried, inputs):
        trace_block, index_block, wave_real, wave_imag, onset_block = inputs
        mat_re, mat_im = matrix_block(trace_block, index_block, wave_real, wave_imag)
        sum_re, sum_im = forward_apply(mat_re, mat_im, plus_re, plus_im)
        return (carried, time_mute(back_to_time(sum_re, sum_im), onset_block))
    unused, second_blocks = lax.scan(second_pass, jnp.zeros((), jnp.float32), scan_inputs)
    upgoing_second = second_blocks.transpose(1, 0, 2, 3).reshape(FOC, S, NT)
    return (upgoing_first, downgoing, upgoing_second)
```

```python
import functools
import math

import jax
import jax.numpy as jnp
import numpy as np
from jax import lax
from jax.experimental import pallas as pl
from jax.experimental.pallas import tpu as pltpu
from jax.sharding import PartitionSpec as P

NT = 256
NF = 128
TAPS = 64
KSHIFT = 64
LANES = 128
GROUP = 8
NG = NF // GROUP

F32 = jnp.float32
BF16 = jnp.bfloat16
NN = (((1,), (0,)), ((), ()))
NT_DIMS = (((1,), (1,)), ((), ()))


def make_tables(source_local):
    sample = np.arange(NT)
    bins = np.arange(NF)
    angles = 2.0 * np.pi / NT * (bins[:, None] * sample[None, :] % NT)
    forward = np.concatenate([np.cos(angles), -np.sin(angles)], axis=0)
    weights = np.where(bins == 0, 1.0, 2.0) / NT
    inverse = (forward * np.concatenate([weights, weights])[:, None]).T
    tap = np.arange(TAPS, dtype=np.float64)
    fraction = np.arange(KSHIFT) * (TAPS / (4.0 * KSHIFT))
    offset = tap[None, :] - 0.375 * TAPS - fraction[:, None]
    window = 0.5 - 0.5 * np.cos(2.0 * np.pi * (tap + 0.5) / TAPS)
    tap_spec = forward[:, :TAPS] @ (np.sinc(offset) * window[None, :]).T
    tap_high = jnp.asarray(tap_spec, F32).astype(BF16)
    tap_low = (jnp.asarray(tap_spec, F32) - tap_high.astype(F32)).astype(BF16)
    width = source_local * GROUP
    source_of = np.arange(width) // GROUP
    blocks = LANES // source_local
    pick = (source_of[:, None] == np.arange(source_local)[None, :]).astype(np.float64)
    gather = np.tile(pick, (1, blocks))
    spread = np.zeros((blocks, LANES, width))
    for block in range(blocks):
        spread[block, block * source_local : (block + 1) * source_local] = pick.T
    return dict(
        forward=jnp.asarray(forward, F32).astype(BF16),
        inverse=jnp.asarray(inverse, F32).astype(BF16),
        taps=jnp.concatenate([tap_high, tap_low], axis=1),
        gather=jnp.asarray(gather, F32).astype(BF16),
        spread=jnp.asarray(spread, F32).astype(BF16),
    )


def mm(left, right, dims=NN):
    return lax.dot_general(left, right, dims, preferred_element_type=F32)


def interleave(first, second):
    width = first.shape[-1]
    pair = jnp.stack(
        [first.reshape(NG, GROUP, width), second.reshape(NG, GROUP, width)], axis=1
    )
    return pair.reshape(NG, 2 * GROUP, width)


def same_bin(rows, lanes):
    row = lax.broadcasted_iota(jnp.int32, (rows, lanes), 0)
    lane = lax.broadcasted_iota(jnp.int32, (rows, lanes), 1)
    return (row % GROUP) == (lane % GROUP)


def store_vector(vector_ref, slot, first, second):
    first_re, first_im = first[:NF], first[NF:]
    second_re, second_im = second[:NF], second[NF:]
    receivers = first.shape[-1]
    re = interleave(first_re, second_re)
    im = interleave(first_im, second_im)
    vector_ref[:, 0, slot, :, :receivers] = re.astype(BF16)
    vector_ref[:, 0, slot, :, receivers:] = (-im).astype(BF16)
    vector_ref[:, 1, slot, :, :receivers] = im.astype(BF16)
    vector_ref[:, 1, slot, :, receivers:] = re.astype(BF16)


def apply_matrix(matrix_ref, vector_ref, gather, store):
    pairs = vector_ref.shape[2]
    rows = 2 * pairs * 2 * GROUP
    width = matrix_ref.shape[1] * matrix_ref.shape[2]
    diagonal = same_bin(rows, width)
    block_of = lax.broadcasted_iota(jnp.int32, (pairs, GROUP, LANES), 2) // (LANES // 4)

    def one(group):
        vector = vector_ref[group].reshape(rows, vector_ref.shape[-1])
        matrix = matrix_ref[group].reshape(width, matrix_ref.shape[-1])
        full = mm(vector, matrix, NT_DIMS)
        kept = jnp.where(diagonal, full, 0.0).astype(BF16)
        spread = mm(kept, gather).reshape(2, pairs, 2, GROUP, LANES)
        low = jnp.where(block_of == 0, spread[0, :, 0], spread[0, :, 1])
        high = jnp.where(block_of == 2, spread[1, :, 0], spread[1, :, 1])
        return jnp.where(block_of < 2, low, high)

    for couple in range(NG // 2):
        both = jnp.concatenate([one(2 * couple), one(2 * couple + 1)], axis=1)
        store(couple * 2 * GROUP, both.astype(BF16))


def build_kernel(
    gain, index_ref, traces_ref, shift_ref, deconv_ref, focal_ref, onset_ref,
    forward_ref, taps_ref, gather_ref, matrix_ref, sum_ref, vector_ref,
):
    sources, receivers = shift_ref.shape
    pairs = focal_ref.shape[0] // 2
    forward = forward_ref[...]
    taps = taps_ref[...]
    deconv = deconv_ref[...]
    deconv_high = deconv.astype(BF16)
    deconv_low = (deconv - deconv_high.astype(F32)).astype(BF16)
    head = forward[:, :TAPS]
    wave = (mm(head, deconv_high, NT_DIMS) + mm(head, deconv_low, NT_DIMS)) * gain
    kinds = lax.broadcasted_iota(jnp.int32, (KSHIFT, receivers), 0)

    for couple in range(sources // 2):
        signals = traces_ref[2 * couple : 2 * couple + 2].reshape(2 * receivers, NT)
        raw = mm(forward, signals, NT_DIMS)
        hot = jnp.concatenate(
            [
                (kinds == shift_ref[2 * couple + half : 2 * couple + half + 1, :]).astype(F32)
                for half in range(2)
            ],
            axis=1,
        ).astype(BF16)
        delay = mm(taps, jnp.concatenate([hot, hot], axis=0))
        parts = []
        for half in range(2):
            lanes = slice(half * receivers, (half + 1) * receivers)
            raw_re, raw_im = raw[:NF, lanes], raw[NF:, lanes]
            delay_re, delay_im = delay[:NF, lanes], delay[NF:, lanes]
            column = slice(2 * couple + half, 2 * couple + half + 1)
            wave_re, wave_im = wave[:NF, column], wave[NF:, column]
            first_re = raw_re * delay_re - raw_im * delay_im
            first_im = raw_re * delay_im + raw_im * delay_re
            parts.append(
                (
                    first_re * wave_re - first_im * wave_im,
                    first_re * wave_im + first_im * wave_re,
                )
            )
        matrix_ref[:, couple, :, :receivers] = interleave(parts[0][0], parts[1][0]).astype(BF16)
        matrix_ref[:, couple, :, receivers:] = interleave(parts[0][1], parts[1][1]).astype(BF16)

    for pair in range(pairs):
        first = mm(forward, focal_ref[2 * pair], NT_DIMS)
        second = mm(forward, focal_ref[2 * pair + 1], NT_DIMS)
        store_vector(vector_ref, pair, first, second)

    def store(row, value):
        for pair in range(pairs):
            sum_ref[pair * NF + row : pair * NF + row + 2 * GROUP, :] = value[pair]

    apply_matrix(matrix_ref, vector_ref, gather_ref[...], store)
    rcv_index = index_ref[1]
    own = onset_ref[...].astype(F32)
    own = jnp.concatenate([own[0:1], own[1:2]] * 2, axis=1)
    own = jnp.broadcast_to(own, (2 * GROUP, LANES))
    row = lax.broadcasted_iota(jnp.int32, own.shape, 0)
    lane = lax.broadcasted_iota(jnp.int32, own.shape, 1)
    here = (row == rcv_index // 2) & (lane // (LANES // 2) == rcv_index % 2)
    sum_ref[pairs * NF :, :] = jnp.where(here, own, 0.0).astype(BF16)


def split_halves(first, second):
    lane = lax.broadcasted_iota(jnp.int32, first.shape, 1)
    low = lane < LANES // 2
    re = jnp.where(low, first, pltpu.roll(second, LANES // 2, 1))
    im = jnp.where(low, pltpu.roll(first, LANES // 2, 1), second)
    return jnp.concatenate([re, im], axis=0)


def mute(signal, onset):
    sample = lax.broadcasted_iota(jnp.int32, signal.shape, 0)
    folded = jnp.minimum(sample, NT - sample).astype(F32)
    return jnp.where(folded < onset, signal, 0.0)


def adjoint_kernel(
    index_ref, mine_ref, other_ref, matrix_ref, forward_ref, inverse_ref, spread_ref,
    keep_ref, send_ref, field_ref, vector_ref,
):
    shot_index = index_ref[0]
    rcv_index = index_ref[1]
    core = shot_index % 2
    chip = shot_index // 2
    pairs = keep_ref.shape[0]
    receivers = matrix_ref.shape[-1] // 2
    sources = 2 * matrix_ref.shape[1]
    width = sources * GROUP
    forward = forward_ref[...]
    inverse = inverse_ref[...]
    onsets = mine_ref[pairs * NF :, :].astype(F32) + other_ref[pairs * NF :, :].astype(F32)
    diagonal = same_bin(NF, width)
    owned = jnp.zeros((NT, LANES), F32)

    for couple in range(pairs // 2):
        rows = slice(2 * couple * NF, 2 * (couple + 1) * NF)
        total = mine_ref[rows, :].astype(F32) + other_ref[rows, :].astype(F32)
        spectra = split_halves(total[:NF], total[NF:]).astype(BF16)
        signal = mute(mm(inverse, spectra), onsets[couple : couple + 1, :])
        owned = jnp.where(rcv_index // 2 == couple, signal, owned)
        echo = mm(forward, signal.astype(BF16)).astype(BF16)
        for half in range(2):
            slot = (2 * couple + half) ^ chip
            for part in range(2):
                values = echo[part * NF : (part + 1) * NF]
                kept, sent = (
                    jnp.where(diagonal, mm(values, spread_ref[2 * half + which]), 0.0)
                    for which in (core, 1 - core)
                )
                vector_ref[:, part, slot] = interleave(kept, sent).astype(BF16)

    owned = jnp.where(rcv_index % 2 == 1, pltpu.roll(owned, LANES // 2, 1), owned)
    flipped = jnp.transpose(owned)[: LANES // 2]
    field_ref[...] = flipped.reshape(field_ref.shape)

    def one(group):
        vector = vector_ref[group].reshape(2 * pairs * 2 * GROUP, width)
        matrix = matrix_ref[group].reshape(width, 2 * receivers)
        full = mm(vector, matrix).reshape(2, pairs, 2, GROUP, 2 * receivers)
        re = full[0, ..., :receivers] + full[1, ..., receivers:]
        im = full[1, ..., :receivers] - full[0, ..., receivers:]
        return re, im

    for couple in range(NG // 2):
        even = one(2 * couple)
        odd = one(2 * couple + 1)
        for part in range(2):
            both = jnp.concatenate([even[part], odd[part]], axis=2).astype(BF16)
            row = part * NF + couple * 2 * GROUP
            keep_ref[:, row : row + 2 * GROUP, :] = both[:, 0]
            send_ref[:, row : row + 2 * GROUP, :] = both[:, 1]


def downgoing_kernel(index_ref, *refs):
    parts = refs[:-6]
    focal_ref, onset_ref, forward_ref, inverse_ref, field_ref, plus_ref = refs[-6:]
    total = parts[0][...].astype(F32)
    for part in parts[1:]:
        total = total + part[...].astype(F32)
    onset = onset_ref[...].astype(F32)
    signal = mute(mm(inverse_ref[...], total.astype(BF16)), onset)
    field = focal_ref[0].astype(F32) + jnp.transpose(signal)
    field_ref[0] = field
    plus_ref[...] = mm(forward_ref[...], field.astype(BF16), NT_DIMS).astype(BF16)


def second_kernel(index_ref, near_ref, far_ref, matrix_ref, gather_ref, sum_ref, vector_ref):
    shot_index = index_ref[0]
    rcv_index = index_ref[1]
    core = shot_index % 2
    chip = shot_index // 2
    pairs = near_ref.shape[0]
    for distance in range(pairs):
        slot = (chip ^ distance) ^ rcv_index
        near = near_ref[distance].astype(F32)
        far = far_ref[distance].astype(F32)
        store_vector(
            vector_ref, slot, jnp.where(core == 0, near, far), jnp.where(core == 0, far, near)
        )

    def store(row, value):
        sum_ref[:, row : row + 2 * GROUP, :] = value

    apply_matrix(matrix_ref, vector_ref, gather_ref[...], store)


def final_kernel(*refs):
    parts = refs[:-3]
    onset_ref, inverse_ref, field_ref = refs[-3:]
    total = parts[0][...].astype(F32)
    for part in parts[1:]:
        total = total + part[...].astype(F32)
    spectra = split_halves(total, total).astype(BF16)
    onset = onset_ref[...].astype(F32)
    onset = jnp.concatenate([onset[0:1], onset[1:2]] * 2, axis=1)
    signal = mute(mm(inverse_ref[...], spectra), onset)
    field_ref[...] = jnp.transpose(signal)[: LANES // 2].reshape(field_ref.shape)


def vmem(count):
    return [pl.BlockSpec(memory_space=pltpu.VMEM) for _ in range(count)]


def smem():
    return [pl.BlockSpec(memory_space=pltpu.SMEM)]


def call(kernel, name, out_shape, in_specs, scratch=()):
    many = isinstance(out_shape, (tuple, list))
    return pl.pallas_call(
        kernel,
        name=name,
        out_shape=out_shape,
        in_specs=in_specs,
        out_specs=vmem(len(out_shape)) if many else vmem(1)[0],
        scratch_shapes=list(scratch),
        compiler_params=pltpu.CompilerParams(vmem_limit_bytes=40 << 20),
    )


def exchange(value, axis, distance):
    count = lax.axis_size(axis)
    return lax.ppermute(value, axis, [(place, place ^ distance) for place in range(count)])


def add_rounded(left, right):
    return (left.astype(F32) + right.astype(F32)).astype(BF16)


def body(traces, shift_index, deconv, focal_start, onset_source, onset_receiver):
    shot_count = lax.axis_size("shot")
    rcv_count = lax.axis_size("rcv")
    sources, receivers, _ = traces.shape
    focal_total = focal_start.shape[0]
    pairs = focal_total // 2
    assert onset_source.shape[0] == 2 and pairs == rcv_count
    assert focal_total == shot_count and 4 * sources == LANES and receivers == LANES
    gain = 1.0 / math.sqrt(NT * receivers * rcv_count)
    tables = make_tables(sources)
    index = jnp.stack([lax.axis_index("shot"), lax.axis_index("rcv")]).astype(jnp.int32)
    shape = jax.ShapeDtypeStruct
    vector = pltpu.VMEM((NG, 2, pairs, 2 * GROUP, 2 * receivers), BF16)

    matrix, partial = call(
        functools.partial(build_kernel, gain),
        "build",
        (
            shape((NG, sources // 2, 2 * GROUP, 2 * receivers), BF16),
            shape((pairs * NF + 2 * GROUP, LANES), BF16),
        ),
        smem() + vmem(8),
        [vector],
    )(
        index, traces, shift_index, deconv, focal_start, onset_source,
        tables["forward"], tables["taps"], tables["gather"],
    )

    distance = 1
    mine, other = partial, exchange(partial, "rcv", 1)
    while 2 * distance < rcv_count:
        distance *= 2
        mine = add_rounded(mine, other)
        other = exchange(mine, "rcv", distance)

    keep, send, upgoing_first = call(
        adjoint_kernel,
        "adjoint",
        (
            shape((pairs, 2 * NF, receivers), BF16),
            shape((pairs, 2 * NF, receivers), BF16),
            shape((2, sources, NT), F32),
        ),
        smem() + vmem(6),
        [pltpu.VMEM((NG, 2, pairs, 2 * GROUP, sources * GROUP), BF16)],
    )(index, mine, other, matrix, tables["forward"], tables["inverse"], tables["spread"])

    keep = add_rounded(keep, exchange(send, "shot", 1))
    parts = [keep[0]]
    for distance in range(1, pairs):
        parts.append(exchange(keep[distance], "shot", 2 * distance))

    downgoing, plus = pl.pallas_call(
        downgoing_kernel,
        name="downgoing",
        out_shape=(shape((1, receivers, NT), F32), shape((2 * NF, receivers), BF16)),
        grid_spec=pltpu.PrefetchScalarGridSpec(
            num_scalar_prefetch=1,
            grid=(1,),
            in_specs=[pl.BlockSpec((2 * NF, receivers), lambda i, s: (0, 0)) for _ in parts]
            + [
                pl.BlockSpec((1, receivers, NT), lambda i, s: (s[0], 0, 0)),
                pl.BlockSpec((1, receivers), lambda i, s: (0, 0)),
                pl.BlockSpec((2 * NF, NT), lambda i, s: (0, 0)),
                pl.BlockSpec((NT, 2 * NF), lambda i, s: (0, 0)),
            ],
            out_specs=[
                pl.BlockSpec((1, receivers, NT), lambda i, s: (0, 0, 0)),
                pl.BlockSpec((2 * NF, receivers), lambda i, s: (0, 0)),
            ],
        ),
    )(index, *parts, focal_start, onset_receiver, tables["forward"], tables["inverse"])

    near = [plus]
    for distance in range(1, pairs):
        near.append(exchange(plus, "shot", 2 * distance))
    near = jnp.stack(near)
    far = exchange(near, "shot", 1)

    second = call(
        second_kernel,
        "second",
        shape((pairs, NF, LANES), BF16),
        smem() + vmem(4),
        [vector],
    )(index, near, far, matrix, tables["gather"])

    parts = [second[0]]
    for distance in range(1, rcv_count):
        parts.append(exchange(second[distance], "rcv", distance))
    upgoing_second = call(
        final_kernel, "final", shape((2, sources, NT), F32), vmem(len(parts) + 2)
    )(*parts, onset_source, tables["inverse"])
    return (upgoing_first, downgoing, upgoing_second)


def solution(mesh):
    placed = (
        P("shot", "rcv", None),
        P("shot", "rcv"),
        P("shot", None),
        P(None, "rcv", None),
        P("rcv", "shot"),
        P("shot", "rcv"),
    )
    return jax.shard_map(
        body,
        mesh=mesh,
        in_specs=placed,
        out_specs=(P("rcv", "shot", None), P("shot", "rcv", None), P("rcv", "shot", None)),
        check_vma=False,
    )
```

```python
import functools
import math

import jax
import jax.numpy as jnp
import numpy as np
from jax import lax
from jax.experimental import pallas as pl
from jax.experimental.pallas import tpu as pltpu
from jax.sharding import PartitionSpec as P

NT = 256
NF = 128
TAPS = 64
KSHIFT = 64
LANES = 128
GROUP = 8
NG = NF // GROUP

F32 = jnp.float32
BF16 = jnp.bfloat16
NN = (((1,), (0,)), ((), ()))
NT_DIMS = (((1,), (1,)), ((), ()))


def make_tables(source_local):
    sample = np.arange(NT)
    bins = np.arange(NF)
    angles = 2.0 * np.pi / NT * (bins[:, None] * sample[None, :] % NT)
    forward = np.concatenate([np.cos(angles), -np.sin(angles)], axis=0)
    weights = np.where(bins == 0, 1.0, 2.0) / NT
    inverse = (forward * np.concatenate([weights, weights])[:, None]).T
    tap = np.arange(TAPS, dtype=np.float64)
    fraction = np.arange(KSHIFT) * (TAPS / (4.0 * KSHIFT))
    offset = tap[None, :] - 0.375 * TAPS - fraction[:, None]
    window = 0.5 - 0.5 * np.cos(2.0 * np.pi * (tap + 0.5) / TAPS)
    tap_spec = forward[:, :TAPS] @ (np.sinc(offset) * window[None, :]).T
    width = source_local * GROUP
    source_of = np.arange(width) // GROUP
    blocks = LANES // source_local
    pick = (source_of[:, None] == np.arange(source_local)[None, :]).astype(np.float64)
    gather = np.tile(pick, (1, blocks))
    spread = np.zeros((blocks, LANES, width))
    for block in range(blocks):
        spread[block, block * source_local : (block + 1) * source_local] = pick.T
    return dict(
        forward=jnp.asarray(forward, F32).astype(BF16),
        inverse=jnp.asarray(inverse, F32).astype(BF16),
        taps=jnp.asarray(np.tile(tap_spec, (1, LANES // KSHIFT)), F32),
        gather=jnp.asarray(gather, F32).astype(BF16),
        spread=jnp.asarray(spread, F32).astype(BF16),
    )


def mm(left, right, dims=NN):
    return lax.dot_general(left, right, dims, preferred_element_type=F32)


def interleave(first, second):
    width = first.shape[-1]
    pair = jnp.stack(
        [first.reshape(NG, GROUP, width), second.reshape(NG, GROUP, width)], axis=1
    )
    return pair.reshape(NG, 2 * GROUP, width)


def same_bin(rows, lanes):
    row = lax.broadcasted_iota(jnp.int32, (rows, lanes), 0)
    lane = lax.broadcasted_iota(jnp.int32, (rows, lanes), 1)
    return (row % GROUP) == (lane % GROUP)


def store_vector(vector_ref, place, re, im):
    receivers = re.shape[-1]
    vector_ref[:, place, :, :receivers] = interleave(re, im).astype(BF16)
    vector_ref[:, place, :, receivers:] = interleave(-im, re).astype(BF16)


def unpack(spectra_ref):
    receivers = spectra_ref.shape[-1]
    values = spectra_ref[...].astype(F32).reshape(NG, 2, GROUP, receivers)
    return values[:, 0].reshape(NF, receivers), values[:, 1].reshape(NF, receivers)


def apply_matrix(matrix_ref, vector_ref, kept_ref, gather, store):
    pairs = vector_ref.shape[1] // 2
    rows = 2 * pairs * 2 * GROUP
    width = matrix_ref.shape[1] * matrix_ref.shape[2]
    diagonal = same_bin(rows, width)
    block_of = lax.broadcasted_iota(jnp.int32, (pairs, GROUP, LANES), 2) // (LANES // 4)

    for group in range(NG):
        vector = vector_ref[group].reshape(rows, vector_ref.shape[-1])
        matrix = matrix_ref[group].reshape(width, matrix_ref.shape[-1])
        full = mm(vector, matrix, NT_DIMS)
        kept_ref[group * rows : (group + 1) * rows, :] = jnp.where(diagonal, full, 0.0).astype(BF16)

    for couple in range(NG // 2):
        kept = kept_ref[couple * 2 * rows : (couple + 1) * 2 * rows, :]
        spread = mm(kept, gather).reshape(2, pairs, 2, 2, GROUP, LANES)
        both = []
        for one in range(2):
            real = jnp.where(block_of == 0, spread[one, :, 0, 0], spread[one, :, 1, 0])
            imag = jnp.where(block_of == 2, spread[one, :, 0, 1], spread[one, :, 1, 1])
            both.append(jnp.where(block_of < 2, real, imag))
        store(couple * 2 * GROUP, jnp.concatenate(both, axis=1).astype(BF16))


def build_kernel(
    gain, index_ref, traces_hbm, shift_hbm, deconv_hbm, focal_hbm, onset_hbm,
    forward_hbm, taps_hbm, gather_hbm, matrix_ref, sum_ref, own_ref,
    vector_ref, kept_ref, traces_ref, shift_ref, deconv_ref, focal_ref, onset_ref,
    forward_ref, taps_ref, gather_ref, trace_sem, small_sem, delay_ref,
):
    sources, receivers = shift_ref.shape
    pairs = focal_ref.shape[0] // 2
    small = [
        pltpu.make_async_copy(source, target, small_sem.at[place])
        for place, (source, target) in enumerate(
            [
                (forward_hbm, forward_ref),
                (deconv_hbm, deconv_ref),
                (focal_hbm, focal_ref),
                (taps_hbm, taps_ref),
                (shift_hbm, shift_ref),
                (gather_hbm, gather_ref),
                (onset_hbm, onset_ref),
            ]
        )
    ]
    chunks = trace_sem.shape[0]
    step = sources // chunks
    large = [
        pltpu.make_async_copy(
            traces_hbm.at[pl.ds(chunk * step, step)],
            traces_ref.at[pl.ds(chunk * step, step)],
            trace_sem.at[chunk],
        )
        for chunk in range(chunks)
    ]
    for copy in small[:5] + large + small[5:]:
        copy.start()
    small[0].wait()
    small[1].wait()
    forward = forward_ref[...]
    deconv = deconv_ref[...]
    deconv_high = deconv.astype(BF16)
    deconv_low = (deconv - deconv_high.astype(F32)).astype(BF16)
    head = forward_ref[:, :TAPS]
    wave = (mm(head, deconv_high, NT_DIMS) + mm(head, deconv_low, NT_DIMS)) * gain
    wave_high = wave.astype(BF16)
    wave_low = (wave - wave_high.astype(F32)).astype(BF16)
    wave_both = jnp.concatenate([wave_high, wave_low], axis=1)
    small[3].wait()
    taps = taps_ref[...]
    owner = lax.broadcasted_iota(jnp.int32, (2 * sources, 2 * LANES), 0) % sources
    place = lax.broadcasted_iota(jnp.int32, (2 * sources, 2 * LANES), 1) // KSHIFT
    zeros = jnp.zeros((KSHIFT, receivers), F32)
    kinds = lax.broadcasted_iota(jnp.int32, (KSHIFT, receivers), 0)
    for quad in range(sources // 4):
        spread = mm(wave_both, (owner == place + 4 * quad).astype(F32).astype(BF16))
        for couple in range(2):
            lanes = slice(couple * LANES, (couple + 1) * LANES)
            wave_re, wave_im = spread[:NF, lanes], spread[NF:, lanes]
            taps_re, taps_im = taps[:NF], taps[NF:]
            delay_re = taps_re * wave_re - taps_im * wave_im
            delay_im = taps_re * wave_im + taps_im * wave_re
            delay_ref[2 * quad + couple] = jnp.concatenate([delay_re, delay_im], axis=0).astype(BF16)

    small[2].wait()
    own_ref[...] = focal_ref[index_ref[0]]
    for place in range(2 * pairs):
        spectra = mm(forward, focal_ref[place], NT_DIMS)
        store_vector(vector_ref, place, spectra[:NF], spectra[NF:])

    small[4].wait()
    for couple in range(sources // 2):
        if (2 * couple) % step == 0:
            large[2 * couple // step].wait()
        signals = traces_ref[2 * couple : 2 * couple + 2].reshape(2 * receivers, NT)
        raw = mm(forward, signals, NT_DIMS)
        hot = [
            (kinds == shift_ref[2 * couple + half : 2 * couple + half + 1, :]).astype(F32)
            for half in range(2)
        ]
        hot = jnp.concatenate(
            [
                jnp.concatenate([hot[0], zeros], axis=1),
                jnp.concatenate([zeros, hot[1]], axis=1),
            ],
            axis=0,
        ).astype(BF16)
        delay = mm(delay_ref[couple], hot)
        re = raw[:NF] * delay[:NF] - raw[NF:] * delay[NF:]
        im = raw[:NF] * delay[NF:] + raw[NF:] * delay[:NF]
        matrix_ref[:, couple, :, :receivers] = interleave(
            re[:, :receivers], re[:, receivers:]
        ).astype(BF16)
        matrix_ref[:, couple, :, receivers:] = interleave(
            im[:, :receivers], im[:, receivers:]
        ).astype(BF16)

    def store(row, value):
        for pair in range(pairs):
            sum_ref[pair * NF + row : pair * NF + row + 2 * GROUP, :] = value[pair]

    small[5].wait()
    small[6].wait()
    apply_matrix(matrix_ref, vector_ref, kept_ref, gather_ref[...], store)
    rcv_index = index_ref[1]
    own = onset_ref[...].astype(F32)
    own = jnp.concatenate([own[0:1], own[1:2]] * 2, axis=1)
    own = jnp.broadcast_to(own, (2 * GROUP, LANES))
    row = lax.broadcasted_iota(jnp.int32, own.shape, 0)
    lane = lax.broadcasted_iota(jnp.int32, own.shape, 1)
    here = (row == rcv_index // 2) & (lane // (LANES // 2) == rcv_index % 2)
    sum_ref[pairs * NF :, :] = jnp.where(here, own, 0.0).astype(BF16)


def split_halves(first, second):
    lane = lax.broadcasted_iota(jnp.int32, first.shape, 1)
    low = lane < LANES // 2
    re = jnp.where(low, first, pltpu.roll(second, LANES // 2, 1))
    im = jnp.where(low, pltpu.roll(first, LANES // 2, 1), second)
    return jnp.concatenate([re, im], axis=0)


def mute(signal, onset):
    sample = lax.broadcasted_iota(jnp.int32, signal.shape, 0)
    folded = jnp.minimum(sample, NT - sample).astype(F32)
    return jnp.where(folded < onset, signal, 0.0)


def adjoint_kernel(
    index_ref, mine_ref, other_ref, matrix_ref, forward_ref, inverse_ref, spread_ref, *refs
):
    field_ref, vector_ref, echo_ref = refs[-3:]
    pairs = (len(refs) - 3) // 2
    keep_refs, send_refs = refs[:pairs], refs[pairs : 2 * pairs]
    shot_index = index_ref[0]
    rcv_index = index_ref[1]
    core = shot_index % 2
    chip = shot_index // 2
    receivers = matrix_ref.shape[-1] // 2
    sources = 2 * matrix_ref.shape[1]
    width = sources * GROUP
    forward = forward_ref[...]
    inverse = inverse_ref[...]
    onsets = mine_ref[pairs * NF :, :].astype(F32) + other_ref[pairs * NF :, :].astype(F32)
    owned = jnp.zeros((NT, LANES), F32)

    for couple in range(pairs // 2):
        rows = slice(2 * couple * NF, 2 * (couple + 1) * NF)
        total = mine_ref[rows, :].astype(F32) + other_ref[rows, :].astype(F32)
        spectra = split_halves(total[:NF], total[NF:]).astype(BF16)
        signal = mute(mm(inverse, spectra), onsets[couple : couple + 1, :])
        owned = jnp.where(rcv_index // 2 == couple, signal, owned)
        echo_ref[couple] = mm(forward, signal.astype(BF16)).astype(BF16)

    diagonal = same_bin(2 * NF, width)
    for half in range(2):
        table_kept = spread_ref[2 * half + core]
        table_sent = spread_ref[2 * half + 1 - core]
        for couple in range(pairs // 2):
            slot = (2 * couple + half) ^ chip
            values = echo_ref[couple]
            kept = jnp.where(diagonal, mm(values, table_kept), 0.0)
            sent = jnp.where(diagonal, mm(values, table_sent), 0.0)
            for part in range(2):
                rows = slice(part * NF, (part + 1) * NF)
                vector_ref[:, part, slot] = interleave(kept[rows], sent[rows]).astype(BF16)

    owned = jnp.where(rcv_index % 2 == 1, pltpu.roll(owned, LANES // 2, 1), owned)
    flipped = jnp.transpose(owned)[: LANES // 2]
    field_ref[...] = flipped.reshape(field_ref.shape)

    def one(group):
        vector = vector_ref[group].reshape(2 * pairs * 2 * GROUP, width)
        matrix = matrix_ref[group].reshape(width, 2 * receivers)
        full = mm(vector, matrix).reshape(2, pairs, 2, GROUP, 2 * receivers)
        re = full[0, ..., :receivers] + full[1, ..., receivers:]
        im = full[1, ..., :receivers] - full[0, ..., receivers:]
        return re, im

    for couple in range(NG // 2):
        even = one(2 * couple)
        odd = one(2 * couple + 1)
        for part in range(2):
            both = jnp.concatenate([even[part], odd[part]], axis=2).astype(BF16)
            row = part * NF + couple * 2 * GROUP
            for slot in range(pairs):
                keep_refs[slot][row : row + 2 * GROUP, :] = both[slot, 0]
                send_refs[slot][row : row + 2 * GROUP, :] = both[slot, 1]


def downgoing_kernel(*refs):
    parts = refs[:-6]
    focal_ref, onset_ref, forward_ref, inverse_ref, field_ref, plus_ref = refs[-6:]
    total = parts[0][...].astype(F32)
    for part in parts[1:]:
        total = total + part[...].astype(F32)
    onset = onset_ref[...].astype(F32)
    signal = mute(mm(inverse_ref[...], total.astype(BF16)), onset)
    field = focal_ref[...].astype(F32) + jnp.transpose(signal)
    field_ref[0] = field
    spectra = mm(forward_ref[...], field.astype(BF16), NT_DIMS)
    plus_ref[...] = interleave(spectra[:NF], spectra[NF:]).astype(BF16)


def second_kernel(pairs, index_ref, *refs):
    near_refs, far_refs = refs[:pairs], refs[pairs : 2 * pairs]
    matrix_ref, gather_ref = refs[2 * pairs : 2 * pairs + 2]
    sum_refs = refs[2 * pairs + 2 : -2]
    vector_ref, kept_ref = refs[-2:]
    shot_index = index_ref[0]
    rcv_index = index_ref[1]
    core = shot_index % 2
    chip = shot_index // 2
    for distance in range(pairs):
        slot = (chip ^ distance) ^ rcv_index
        store_vector(vector_ref, 2 * slot + core, *unpack(near_refs[distance]))
        store_vector(vector_ref, 2 * slot + 1 - core, *unpack(far_refs[distance]))

    def store(row, value):
        for slot in range(pairs):
            sum_refs[slot][row : row + 2 * GROUP, :] = value[slot]

    apply_matrix(matrix_ref, vector_ref, kept_ref, gather_ref[...], store)


def final_kernel(*refs):
    parts = refs[:-3]
    onset_ref, inverse_ref, field_ref = refs[-3:]
    total = parts[0][...].astype(F32)
    for part in parts[1:]:
        total = total + part[...].astype(F32)
    spectra = split_halves(total, total).astype(BF16)
    onset = onset_ref[...].astype(F32)
    onset = jnp.concatenate([onset[0:1], onset[1:2]] * 2, axis=1)
    signal = mute(mm(inverse_ref[...], spectra), onset)
    field_ref[...] = jnp.transpose(signal)[: LANES // 2].reshape(field_ref.shape)


def vmem(count):
    return [pl.BlockSpec(memory_space=pltpu.VMEM) for _ in range(count)]


def smem():
    return [pl.BlockSpec(memory_space=pltpu.SMEM)]


def hbm(count):
    return [pl.BlockSpec(memory_space=pltpu.HBM) for _ in range(count)]


def call(kernel, name, out_shape, in_specs, scratch=()):
    many = isinstance(out_shape, (tuple, list))
    return pl.pallas_call(
        kernel,
        name=name,
        out_shape=out_shape,
        in_specs=in_specs,
        out_specs=vmem(len(out_shape)) if many else vmem(1)[0],
        scratch_shapes=list(scratch),
        compiler_params=pltpu.CompilerParams(vmem_limit_bytes=40 << 20),
    )


def exchange(value, axis, distance):
    count = lax.axis_size(axis)
    return lax.ppermute(value, axis, [(place, place ^ distance) for place in range(count)])


def add_rounded(left, right):
    return (left.astype(F32) + right.astype(F32)).astype(BF16)


def body(traces, shift_index, deconv, focal_start, onset_source, onset_receiver):
    shot_count = lax.axis_size("shot")
    rcv_count = lax.axis_size("rcv")
    sources, receivers, _ = traces.shape
    focal_total = focal_start.shape[0]
    pairs = focal_total // 2
    assert onset_source.shape[0] == 2 and pairs == rcv_count
    assert focal_total == shot_count and 4 * sources == LANES and receivers == LANES
    gain = 1.0 / math.sqrt(NT * receivers * rcv_count)
    tables = make_tables(sources)
    index = jnp.stack([lax.axis_index("shot"), lax.axis_index("rcv")]).astype(jnp.int32)
    shape = jax.ShapeDtypeStruct
    vector = pltpu.VMEM((NG, 2 * pairs, 2 * GROUP, 2 * receivers), BF16)
    kept = pltpu.VMEM((NG * 2 * pairs * 2 * GROUP, sources * GROUP), BF16)

    def buffer(value):
        return pltpu.VMEM(value.shape, value.dtype)

    inputs = (
        traces, shift_index, deconv, focal_start, onset_source,
        tables["forward"], tables["taps"], tables["gather"],
    )
    matrix, partial, focal_own = call(
        functools.partial(build_kernel, gain),
        "build",
        (
            shape((NG, sources // 2, 2 * GROUP, 2 * receivers), BF16),
            shape((pairs * NF + 2 * GROUP, LANES), BF16),
            shape((receivers, NT), BF16),
        ),
        smem() + hbm(len(inputs)),
        [vector, kept]
        + [buffer(value) for value in inputs]
        + [pltpu.SemaphoreType.DMA((4,)), pltpu.SemaphoreType.DMA((7,))]
        + [pltpu.VMEM((sources // 2, 2 * NF, LANES), BF16)],
    )(index, *inputs)

    distance = 1
    mine, other = partial, exchange(partial, "rcv", 1)
    while 2 * distance < rcv_count:
        distance *= 2
        mine = add_rounded(mine, other)
        other = exchange(mine, "rcv", distance)

    field = shape((2 * NF, receivers), BF16)
    *blocks, upgoing_first = call(
        adjoint_kernel,
        "adjoint",
        [field] * (2 * pairs) + [shape((2, sources, NT), F32)],
        smem() + vmem(6),
        [
            pltpu.VMEM((NG, 2, pairs, 2 * GROUP, sources * GROUP), BF16),
            pltpu.VMEM((pairs // 2, 2 * NF, LANES), BF16),
        ],
    )(index, mine, other, matrix, tables["forward"], tables["inverse"], tables["spread"])

    parts = []
    for distance in reversed(range(pairs)):
        block = add_rounded(blocks[distance], exchange(blocks[pairs + distance], "shot", 1))
        parts.append(exchange(block, "shot", 2 * distance) if distance else block)

    downgoing, plus = call(
        downgoing_kernel,
        "downgoing",
        (
            shape((1, receivers, NT), F32),
            shape((NG, 2 * GROUP, receivers), BF16),
        ),
        vmem(pairs + 4),
    )(*parts, focal_own, onset_receiver, tables["forward"], tables["inverse"])

    near = [plus]
    for distance in range(1, pairs):
        near.append(exchange(plus, "shot", 2 * distance))
    far = [exchange(value, "shot", 1) for value in near]

    parts = call(
        functools.partial(second_kernel, pairs),
        "second",
        [shape((NF, LANES), BF16)] * pairs,
        smem() + vmem(2 * pairs + 2),
        [vector, kept],
    )(index, *near, *far, matrix, tables["gather"])

    parts = [parts[0]] + [
        exchange(parts[distance], "rcv", distance) for distance in range(1, rcv_count)
    ]
    upgoing_second = call(
        final_kernel, "final", shape((2, sources, NT), F32), vmem(len(parts) + 2)
    )(*parts, onset_source, tables["inverse"])
    return (upgoing_first, downgoing, upgoing_second)


def solution(mesh):
    placed = (
        P("shot", "rcv", None),
        P("shot", "rcv"),
        P("shot", None),
        P(None, "rcv", None),
        P("rcv", "shot"),
        P("shot", "rcv"),
    )
    return jax.shard_map(
        body,
        mesh=mesh,
        in_specs=placed,
        out_specs=(P("rcv", "shot", None), P("shot", "rcv", None), P("rcv", "shot", None)),
        check_vma=False,
    )
```

```python
import functools
import math

import jax
import jax.numpy as jnp
import numpy as np
from jax import lax
from jax.experimental import pallas as pl
from jax.experimental.pallas import tpu as pltpu
from jax.sharding import PartitionSpec as P

NT = 256
NF = 128
TAPS = 64
KSHIFT = 64
LANES = 128
GROUP = 8
NG = NF // GROUP

F32 = jnp.float32
BF16 = jnp.bfloat16
NN = (((1,), (0,)), ((), ()))
NT_DIMS = (((1,), (1,)), ((), ()))


def make_tables(source_local):
    sample = np.arange(NT)
    bins = np.arange(NF)
    angles = 2.0 * np.pi / NT * (bins[:, None] * sample[None, :] % NT)
    forward = np.concatenate([np.cos(angles), -np.sin(angles)], axis=0)
    weights = np.where(bins == 0, 1.0, 2.0) / NT
    inverse = (forward * np.concatenate([weights, weights])[:, None]).T
    tap = np.arange(TAPS, dtype=np.float64)
    fraction = np.arange(KSHIFT) * (TAPS / (4.0 * KSHIFT))
    offset = tap[None, :] - 0.375 * TAPS - fraction[:, None]
    window = 0.5 - 0.5 * np.cos(2.0 * np.pi * (tap + 0.5) / TAPS)
    tap_spec = forward[:, :TAPS] @ (np.sinc(offset) * window[None, :]).T
    width = source_local * GROUP
    source_of = np.arange(width) // GROUP
    blocks = LANES // source_local
    pick = (source_of[:, None] == np.arange(source_local)[None, :]).astype(np.float64)
    gather = np.tile(pick, (1, blocks))
    spread = np.zeros((blocks, LANES, width))
    for block in range(blocks):
        spread[block, block * source_local : (block + 1) * source_local] = pick.T
    return dict(
        forward=jnp.asarray(forward, F32).astype(BF16),
        inverse=jnp.asarray(inverse, F32).astype(BF16),
        taps=jnp.asarray(np.tile(tap_spec, (1, LANES // KSHIFT)), F32),
        gather=jnp.asarray(gather, F32).astype(BF16),
        spread=jnp.asarray(spread, F32).astype(BF16),
    )


def mm(left, right, dims=NN):
    return lax.dot_general(left, right, dims, preferred_element_type=F32)


def interleave(first, second):
    width = first.shape[-1]
    pair = jnp.stack(
        [first.reshape(NG, GROUP, width), second.reshape(NG, GROUP, width)], axis=1
    )
    return pair.reshape(NG, 2 * GROUP, width)


def same_bin(rows, lanes):
    row = lax.broadcasted_iota(jnp.int32, (rows, lanes), 0)
    lane = lax.broadcasted_iota(jnp.int32, (rows, lanes), 1)
    return (row % GROUP) == (lane % GROUP)


def store_vector(vector_ref, place, re, im):
    receivers = re.shape[-1]
    vector_ref[:, place, :, :receivers] = interleave(re, im).astype(BF16)
    vector_ref[:, place, :, receivers:] = interleave(-im, re).astype(BF16)


def unpack(spectra_ref):
    receivers = spectra_ref.shape[-1]
    values = spectra_ref[...].astype(F32).reshape(NG, 2, GROUP, receivers)
    return values[:, 0].reshape(NF, receivers), values[:, 1].reshape(NF, receivers)


def apply_matrix(matrix_ref, vector_ref, kept_ref, gather, store):
    pairs = vector_ref.shape[1] // 2
    rows = 2 * pairs * 2 * GROUP
    width = matrix_ref.shape[1] * matrix_ref.shape[2]
    diagonal = same_bin(rows, width)
    block_of = lax.broadcasted_iota(jnp.int32, (pairs, GROUP, LANES), 2) // (LANES // 4)

    for group in range(NG):
        vector = vector_ref[group].reshape(rows, vector_ref.shape[-1])
        matrix = matrix_ref[group].reshape(width, matrix_ref.shape[-1])
        full = mm(vector, matrix, NT_DIMS)
        kept_ref[group * rows : (group + 1) * rows, :] = jnp.where(diagonal, full, 0.0).astype(BF16)

    for couple in range(NG // 2):
        kept = kept_ref[couple * 2 * rows : (couple + 1) * 2 * rows, :]
        spread = mm(kept, gather).reshape(2, pairs, 2, 2, GROUP, LANES)
        both = []
        for one in range(2):
            real = jnp.where(block_of == 0, spread[one, :, 0, 0], spread[one, :, 1, 0])
            imag = jnp.where(block_of == 2, spread[one, :, 0, 1], spread[one, :, 1, 1])
            both.append(jnp.where(block_of < 2, real, imag))
        store(couple * 2 * GROUP, jnp.concatenate(both, axis=1).astype(BF16))


def build_kernel(
    gain, index_ref, traces_hbm, shift_hbm, deconv_hbm, focal_hbm, onset_hbm,
    forward_hbm, taps_hbm, gather_hbm, matrix_ref, sum_ref, own_ref,
    vector_ref, kept_ref, traces_ref, shift_ref, deconv_ref, focal_ref, onset_ref,
    forward_ref, taps_ref, gather_ref, trace_sem, small_sem, delay_ref,
):
    sources, receivers = shift_ref.shape
    pairs = focal_ref.shape[0] // 2
    small = [
        pltpu.make_async_copy(source, target, small_sem.at[place])
        for place, (source, target) in enumerate(
            [
                (forward_hbm, forward_ref),
                (deconv_hbm, deconv_ref),
                (focal_hbm, focal_ref),
                (taps_hbm, taps_ref),
                (shift_hbm, shift_ref),
                (gather_hbm, gather_ref),
                (onset_hbm, onset_ref),
            ]
        )
    ]
    chunks = trace_sem.shape[0]
    step = sources // chunks
    large = [
        pltpu.make_async_copy(
            traces_hbm.at[pl.ds(chunk * step, step)],
            traces_ref.at[pl.ds(chunk * step, step)],
            trace_sem.at[chunk],
        )
        for chunk in range(chunks)
    ]
    for copy in small[:5] + large + small[5:]:
        copy.start()
    small[0].wait()
    small[1].wait()
    forward = forward_ref[...]
    deconv = deconv_ref[...]
    deconv_high = deconv.astype(BF16)
    deconv_low = (deconv - deconv_high.astype(F32)).astype(BF16)
    head = forward_ref[:, :TAPS]
    wave = (mm(head, deconv_high, NT_DIMS) + mm(head, deconv_low, NT_DIMS)) * gain
    wave_high = wave.astype(BF16)
    wave_low = (wave - wave_high.astype(F32)).astype(BF16)
    wave_both = jnp.concatenate([wave_high, wave_low], axis=1)
    small[3].wait()
    taps = taps_ref[...]
    owner = lax.broadcasted_iota(jnp.int32, (2 * sources, 2 * LANES), 0) % sources
    place = lax.broadcasted_iota(jnp.int32, (2 * sources, 2 * LANES), 1) // KSHIFT
    zeros = jnp.zeros((KSHIFT, receivers), F32)
    kinds = lax.broadcasted_iota(jnp.int32, (KSHIFT, receivers), 0)
    for quad in range(sources // 4):
        spread = mm(wave_both, (owner == place + 4 * quad).astype(F32).astype(BF16))
        for couple in range(2):
            lanes = slice(couple * LANES, (couple + 1) * LANES)
            wave_re, wave_im = spread[:NF, lanes], spread[NF:, lanes]
            taps_re, taps_im = taps[:NF], taps[NF:]
            delay_re = taps_re * wave_re - taps_im * wave_im
            delay_im = taps_re * wave_im + taps_im * wave_re
            delay_ref[2 * quad + couple] = jnp.concatenate([delay_re, delay_im], axis=0).astype(BF16)

    small[2].wait()
    own_ref[...] = focal_ref[index_ref[0]]
    for place in range(2 * pairs):
        spectra = mm(forward, focal_ref[place], NT_DIMS)
        store_vector(vector_ref, place, spectra[:NF], spectra[NF:])

    small[4].wait()
    for couple in range(sources // 2):
        if (2 * couple) % step == 0:
            large[2 * couple // step].wait()
        signals = traces_ref[2 * couple : 2 * couple + 2].reshape(2 * receivers, NT)
        raw = mm(forward, signals, NT_DIMS)
        hot = [
            (kinds == shift_ref[2 * couple + half : 2 * couple + half + 1, :]).astype(F32)
            for half in range(2)
        ]
        hot = jnp.concatenate(
            [
                jnp.concatenate([hot[0], zeros], axis=1),
                jnp.concatenate([zeros, hot[1]], axis=1),
            ],
            axis=0,
        ).astype(BF16)
        delay = mm(delay_ref[couple], hot)
        re = raw[:NF] * delay[:NF] - raw[NF:] * delay[NF:]
        im = raw[:NF] * delay[NF:] + raw[NF:] * delay[:NF]
        matrix_ref[:, couple, :, :receivers] = interleave(
            re[:, :receivers], re[:, receivers:]
        ).astype(BF16)
        matrix_ref[:, couple, :, receivers:] = interleave(
            im[:, :receivers], im[:, receivers:]
        ).astype(BF16)

    def store(row, value):
        for pair in range(pairs):
            sum_ref[pair * NF + row : pair * NF + row + 2 * GROUP, :] = value[pair]

    small[5].wait()
    small[6].wait()
    apply_matrix(matrix_ref, vector_ref, kept_ref, gather_ref[...], store)
    rcv_index = index_ref[1]
    own = onset_ref[...].astype(F32)
    own = jnp.concatenate([own[0:1], own[1:2]] * 2, axis=1)
    own = jnp.broadcast_to(own, (2 * GROUP, LANES))
    row = lax.broadcasted_iota(jnp.int32, own.shape, 0)
    lane = lax.broadcasted_iota(jnp.int32, own.shape, 1)
    here = (row == rcv_index // 2) & (lane // (LANES // 2) == rcv_index % 2)
    sum_ref[pairs * NF :, :] = jnp.where(here, own, 0.0).astype(BF16)


def split_halves(first, second):
    lane = lax.broadcasted_iota(jnp.int32, first.shape, 1)
    low = lane < LANES // 2
    re = jnp.where(low, first, pltpu.roll(second, LANES // 2, 1))
    im = jnp.where(low, pltpu.roll(first, LANES // 2, 1), second)
    return jnp.concatenate([re, im], axis=0)


def mute(signal, onset):
    sample = lax.broadcasted_iota(jnp.int32, signal.shape, 0)
    folded = jnp.minimum(sample, NT - sample).astype(F32)
    return jnp.where(folded < onset, signal, 0.0)


def adjoint_kernel(
    index_ref, mine_ref, other_ref, matrix_ref, forward_ref, inverse_ref, spread_ref, *refs
):
    field_ref, vector_ref, echo_ref = refs[-3:]
    pairs = (len(refs) - 3) // 2
    keep_refs, send_refs = refs[:pairs], refs[pairs : 2 * pairs]
    shot_index = index_ref[0]
    rcv_index = index_ref[1]
    core = shot_index % 2
    chip = shot_index // 2
    receivers = matrix_ref.shape[-1] // 2
    sources = 2 * matrix_ref.shape[1]
    width = sources * GROUP
    forward = forward_ref[...]
    inverse = inverse_ref[...]
    onsets = mine_ref[pairs * NF :, :].astype(F32) + other_ref[pairs * NF :, :].astype(F32)
    owned = jnp.zeros((NT, LANES), F32)

    for couple in range(pairs // 2):
        rows = slice(2 * couple * NF, 2 * (couple + 1) * NF)
        total = mine_ref[rows, :].astype(F32) + other_ref[rows, :].astype(F32)
        spectra = split_halves(total[:NF], total[NF:]).astype(BF16)
        signal = mute(mm(inverse, spectra), onsets[couple : couple + 1, :])
        owned = jnp.where(rcv_index // 2 == couple, signal, owned)
        echo_ref[couple] = mm(forward, signal.astype(BF16)).astype(BF16)

    diagonal = same_bin(2 * NF, width)
    for half in range(2):
        table_kept = spread_ref[2 * half + core]
        table_sent = spread_ref[2 * half + 1 - core]
        for couple in range(pairs // 2):
            slot = (2 * couple + half) ^ chip
            values = echo_ref[couple]
            kept = jnp.where(diagonal, mm(values, table_kept), 0.0)
            sent = jnp.where(diagonal, mm(values, table_sent), 0.0)
            for part in range(2):
                rows = slice(part * NF, (part + 1) * NF)
                vector_ref[:, part, slot] = interleave(kept[rows], sent[rows]).astype(BF16)

    owned = jnp.where(rcv_index % 2 == 1, pltpu.roll(owned, LANES // 2, 1), owned)
    flipped = jnp.transpose(owned)[: LANES // 2]
    field_ref[...] = flipped.reshape(field_ref.shape)

    def one(group):
        vector = vector_ref[group].reshape(2 * pairs * 2 * GROUP, width)
        matrix = matrix_ref[group].reshape(width, 2 * receivers)
        full = mm(vector, matrix).reshape(2, pairs, 2, GROUP, 2 * receivers)
        re = full[0, ..., :receivers] + full[1, ..., receivers:]
        im = full[1, ..., :receivers] - full[0, ..., receivers:]
        return re, im

    for couple in range(NG // 2):
        even = one(2 * couple)
        odd = one(2 * couple + 1)
        for part in range(2):
            both = jnp.concatenate([even[part], odd[part]], axis=2).astype(BF16)
            row = part * NF + couple * 2 * GROUP
            for slot in range(pairs):
                keep_refs[slot][row : row + 2 * GROUP, :] = both[slot, 0]
                send_refs[slot][row : row + 2 * GROUP, :] = both[slot, 1]


def downgoing_kernel(*refs):
    parts = refs[:-6]
    focal_ref, onset_ref, forward_ref, inverse_ref, field_ref, plus_ref = refs[-6:]
    total = parts[0][...].astype(F32)
    for part in parts[1:]:
        total = total + part[...].astype(F32)
    onset = onset_ref[...].astype(F32)
    signal = mute(mm(inverse_ref[...], total.astype(BF16)), onset)
    field = focal_ref[...].astype(F32) + jnp.transpose(signal)
    field_ref[0] = field
    spectra = mm(forward_ref[...], field.astype(BF16), NT_DIMS)
    plus_ref[...] = interleave(spectra[:NF], spectra[NF:]).astype(BF16)


def second_kernel(pairs, index_ref, *refs):
    near_refs, far_refs = refs[:pairs], refs[pairs : 2 * pairs]
    matrix_ref, gather_ref = refs[2 * pairs : 2 * pairs + 2]
    sum_refs = refs[2 * pairs + 2 : -2]
    vector_ref, kept_ref = refs[-2:]
    shot_index = index_ref[0]
    rcv_index = index_ref[1]
    core = shot_index % 2
    chip = shot_index // 2
    for distance in range(pairs):
        slot = (chip ^ distance) ^ rcv_index
        store_vector(vector_ref, 2 * slot + core, *unpack(near_refs[distance]))
        store_vector(vector_ref, 2 * slot + 1 - core, *unpack(far_refs[distance]))

    def store(row, value):
        for slot in range(pairs):
            sum_refs[slot][row : row + 2 * GROUP, :] = value[slot]

    apply_matrix(matrix_ref, vector_ref, kept_ref, gather_ref[...], store)


def final_kernel(*refs):
    parts = refs[:-3]
    onset_ref, inverse_ref, field_ref = refs[-3:]
    total = parts[0][...].astype(F32)
    for part in parts[1:]:
        total = total + part[...].astype(F32)
    spectra = split_halves(total, total).astype(BF16)
    onset = onset_ref[...].astype(F32)
    onset = jnp.concatenate([onset[0:1], onset[1:2]] * 2, axis=1)
    signal = mute(mm(inverse_ref[...], spectra), onset)
    field_ref[...] = jnp.transpose(signal)[: LANES // 2].reshape(field_ref.shape)


def vmem(count):
    return [pl.BlockSpec(memory_space=pltpu.VMEM) for _ in range(count)]


def smem():
    return [pl.BlockSpec(memory_space=pltpu.SMEM)]


def hbm(count):
    return [pl.BlockSpec(memory_space=pltpu.HBM) for _ in range(count)]


def call(kernel, name, out_shape, in_specs, scratch=()):
    many = isinstance(out_shape, (tuple, list))
    return pl.pallas_call(
        kernel,
        name=name,
        out_shape=out_shape,
        in_specs=in_specs,
        out_specs=vmem(len(out_shape)) if many else vmem(1)[0],
        scratch_shapes=list(scratch),
        compiler_params=pltpu.CompilerParams(vmem_limit_bytes=40 << 20),
    )


def exchange(value, axis, distance):
    count = lax.axis_size(axis)
    return lax.ppermute(value, axis, [(place, place ^ distance) for place in range(count)])


def add_rounded(left, right):
    return (left.astype(F32) + right.astype(F32)).astype(BF16)


def body(traces, shift_index, deconv, focal_start, onset_source, onset_receiver):
    shot_count = lax.axis_size("shot")
    rcv_count = lax.axis_size("rcv")
    sources, receivers, _ = traces.shape
    focal_total = focal_start.shape[0]
    pairs = focal_total // 2
    assert onset_source.shape[0] == 2 and pairs == rcv_count
    assert focal_total == shot_count and 4 * sources == LANES and receivers == LANES
    gain = 1.0 / math.sqrt(NT * receivers * rcv_count)
    tables = make_tables(sources)
    index = jnp.stack([lax.axis_index("shot"), lax.axis_index("rcv")]).astype(jnp.int32)
    shape = jax.ShapeDtypeStruct
    vector = pltpu.VMEM((NG, 2 * pairs, 2 * GROUP, 2 * receivers), BF16)
    kept = pltpu.VMEM((NG * 2 * pairs * 2 * GROUP, sources * GROUP), BF16)

    def buffer(value):
        return pltpu.VMEM(value.shape, value.dtype)

    inputs = (
        traces, shift_index, deconv, focal_start, onset_source,
        tables["forward"], tables["taps"], tables["gather"],
    )
    matrix, partial, focal_own = call(
        functools.partial(build_kernel, gain),
        "build",
        (
            shape((NG, sources // 2, 2 * GROUP, 2 * receivers), BF16),
            shape((pairs * NF + 2 * GROUP, LANES), BF16),
            shape((receivers, NT), BF16),
        ),
        smem() + hbm(len(inputs)),
        [vector, kept]
        + [buffer(value) for value in inputs]
        + [pltpu.SemaphoreType.DMA((4,)), pltpu.SemaphoreType.DMA((7,))]
        + [pltpu.VMEM((sources // 2, 2 * NF, LANES), BF16)],
    )(index, *[pltpu.with_memory_space_constraint(value, pltpu.HBM) for value in inputs])

    distance = 1
    mine, other = partial, exchange(partial, "rcv", 1)
    while 2 * distance < rcv_count:
        distance *= 2
        mine = add_rounded(mine, other)
        other = exchange(mine, "rcv", distance)

    field = shape((2 * NF, receivers), BF16)
    *blocks, upgoing_first = call(
        adjoint_kernel,
        "adjoint",
        [field] * (2 * pairs) + [shape((2, sources, NT), F32)],
        smem() + vmem(6),
        [
            pltpu.VMEM((NG, 2, pairs, 2 * GROUP, sources * GROUP), BF16),
            pltpu.VMEM((pairs // 2, 2 * NF, LANES), BF16),
        ],
    )(index, mine, other, matrix, tables["forward"], tables["inverse"], tables["spread"])

    parts = []
    for distance in reversed(range(pairs)):
        block = add_rounded(blocks[distance], exchange(blocks[pairs + distance], "shot", 1))
        parts.append(exchange(block, "shot", 2 * distance) if distance else block)

    downgoing, plus = call(
        downgoing_kernel,
        "downgoing",
        (
            shape((1, receivers, NT), F32),
            shape((NG, 2 * GROUP, receivers), BF16),
        ),
        vmem(pairs + 4),
    )(*parts, focal_own, onset_receiver, tables["forward"], tables["inverse"])

    near = [plus]
    for distance in range(1, pairs):
        near.append(exchange(plus, "shot", 2 * distance))
    far = [exchange(value, "shot", 1) for value in near]

    parts = call(
        functools.partial(second_kernel, pairs),
        "second",
        [shape((NF, LANES), BF16)] * pairs,
        smem() + vmem(2 * pairs + 2),
        [vector, kept],
    )(index, *near, *far, matrix, tables["gather"])

    parts = [parts[0]] + [
        exchange(parts[distance], "rcv", distance) for distance in range(1, rcv_count)
    ]
    upgoing_second = call(
        final_kernel, "final", shape((2, sources, NT), F32), vmem(len(parts) + 2)
    )(*parts, onset_source, tables["inverse"])
    return (upgoing_first, downgoing, upgoing_second)


def solution(mesh):
    placed = (
        P("shot", "rcv", None),
        P("shot", "rcv"),
        P("shot", None),
        P(None, "rcv", None),
        P("rcv", "shot"),
        P("shot", "rcv"),
    )
    return jax.shard_map(
        body,
        mesh=mesh,
        in_specs=placed,
        out_specs=(P("rcv", "shot", None), P("shot", "rcv", None), P("rcv", "shot", None)),
        check_vma=False,
    )
```

```python
import functools
import math

import jax
import jax.numpy as jnp
import numpy as np
from jax import lax
from jax.experimental import pallas as pl
from jax.experimental.pallas import tpu as pltpu
from jax.sharding import PartitionSpec as P

NT = 256
NF = 128
TAPS = 64
KSHIFT = 64
LANES = 128
GROUP = 8
NG = NF // GROUP

F32 = jnp.float32
BF16 = jnp.bfloat16
NN = (((1,), (0,)), ((), ()))
NT_DIMS = (((1,), (1,)), ((), ()))


def make_tables(source_local):
    sample = np.arange(NT)
    bins = np.arange(NF)
    angles = 2.0 * np.pi / NT * (bins[:, None] * sample[None, :] % NT)
    forward = np.concatenate([np.cos(angles), -np.sin(angles)], axis=0)
    weights = np.where(bins == 0, 1.0, 2.0) / NT
    inverse = (forward * np.concatenate([weights, weights])[:, None]).T
    tap = np.arange(TAPS, dtype=np.float64)
    fraction = np.arange(KSHIFT) * (TAPS / (4.0 * KSHIFT))
    offset = tap[None, :] - 0.375 * TAPS - fraction[:, None]
    window = 0.5 - 0.5 * np.cos(2.0 * np.pi * (tap + 0.5) / TAPS)
    tap_spec = forward[:, :TAPS] @ (np.sinc(offset) * window[None, :]).T
    return dict(
        forward=jnp.asarray(forward, F32).astype(BF16),
        inverse=jnp.asarray(inverse, F32).astype(BF16),
        taps=jnp.asarray(np.tile(tap_spec, (1, LANES // KSHIFT)), F32),
        gather=gather_table(source_local),
        gather_half=gather_table(source_local // 2),
        spread=spread_table(source_local // 2),
    )


def gather_table(sources):
    source_of = np.arange(sources * GROUP) // GROUP
    pick = source_of[:, None] == np.arange(sources)[None, :]
    return jnp.asarray(np.tile(pick, (1, LANES // sources)), F32).astype(BF16)


def spread_table(sources):
    pick = (np.arange(sources * GROUP)[None, :] // GROUP == np.arange(sources)[:, None]).astype(
        np.float32
    )
    blocks = LANES // sources
    table = np.zeros((2, blocks // 2, blocks, sources, 2, sources * GROUP), np.float32)
    for core in range(2):
        for pair in range(blocks // 2):
            table[core, pair, 2 * pair + core, :, 0] = pick
            table[core, pair, 2 * pair + 1 - core, :, 1] = pick
    table = table.reshape(2, blocks // 2, LANES, 2 * sources * GROUP)
    return jnp.asarray(table, F32).astype(BF16)


def mm(left, right, dims=NN):
    return lax.dot_general(left, right, dims, preferred_element_type=F32)


def interleave(first, second):
    width = first.shape[-1]
    pair = jnp.stack(
        [first.reshape(NG, GROUP, width), second.reshape(NG, GROUP, width)], axis=1
    )
    return pair.reshape(NG, 2 * GROUP, width)


def same_bin(rows, lanes):
    row = lax.broadcasted_iota(jnp.int32, (rows, lanes), 0)
    lane = lax.broadcasted_iota(jnp.int32, (rows, lanes), 1)
    return (row % GROUP) == (lane % GROUP)


def store_vector(vector_ref, place, re, im):
    receivers = re.shape[-1]
    vector_ref[:, place, :, :receivers] = interleave(re, im).astype(BF16)
    vector_ref[:, place, :, receivers:] = interleave(-im, re).astype(BF16)


def unpack(spectra_ref):
    receivers = spectra_ref.shape[-1]
    values = spectra_ref[...].astype(F32).reshape(NG, 2, GROUP, receivers)
    return values[:, 0].reshape(NF, receivers), values[:, 1].reshape(NF, receivers)


def apply_matrix(matrix_refs, vector_ref, kept_ref, gather, store):
    fields = vector_ref.shape[1]
    rows = fields * 2 * GROUP
    half = matrix_refs[0].shape[1] * matrix_refs[0].shape[2]
    width = half * len(matrix_refs)
    blocks = LANES // (width // GROUP)
    members = blocks // 2
    sets = fields // members
    diagonal = same_bin(rows, width)
    block_of = lax.broadcasted_iota(jnp.int32, (sets, GROUP, LANES), 2) // (LANES // blocks)

    for group in range(NG):
        vector = vector_ref[group].reshape(rows, vector_ref.shape[-1])
        matrix = [ref[group].reshape(half, ref.shape[-1]) for ref in matrix_refs]
        matrix = matrix[0] if len(matrix) == 1 else jnp.concatenate(matrix, axis=0)
        full = mm(vector, matrix, NT_DIMS)
        kept_ref[group * rows : (group + 1) * rows, :] = jnp.where(diagonal, full, 0.0).astype(BF16)

    for couple in range(NG // 2):
        kept = kept_ref[couple * 2 * rows : (couple + 1) * 2 * rows, :]
        spread = mm(kept, gather).reshape(2, sets, members, 2, GROUP, LANES)
        both = []
        for one in range(2):
            value = spread[one, :, 0, 0]
            for block in range(1, blocks):
                term = spread[one, :, block % members, block // members]
                value = jnp.where(block_of == block, term, value)
            both.append(value)
        store(couple * 2 * GROUP, jnp.concatenate(both, axis=1).astype(BF16))


def make_delays(first, count, forward_ref, deconv_ref, taps_ref, gain, delay_ref):
    deconv = deconv_ref[...]
    sources = deconv.shape[0]
    deconv_high = deconv.astype(BF16)
    deconv_low = (deconv - deconv_high.astype(F32)).astype(BF16)
    head = forward_ref[:, :TAPS]
    wave = (mm(head, deconv_high, NT_DIMS) + mm(head, deconv_low, NT_DIMS)) * gain
    wave_high = wave.astype(BF16)
    wave_low = (wave - wave_high.astype(F32)).astype(BF16)
    wave_both = jnp.concatenate([wave_high, wave_low], axis=1)
    taps = taps_ref[...]
    taps_re, taps_im = taps[:NF], taps[NF:]
    owner = lax.broadcasted_iota(jnp.int32, (2 * sources, 2 * LANES), 0) % sources
    place = lax.broadcasted_iota(jnp.int32, (2 * sources, 2 * LANES), 1) // KSHIFT
    for quad in range(count // 4):
        spread = mm(wave_both, (owner == place + (first + 4 * quad)).astype(F32).astype(BF16))
        for couple in range(2):
            lanes = slice(couple * LANES, (couple + 1) * LANES)
            wave_re, wave_im = spread[:NF, lanes], spread[NF:, lanes]
            delay_re = taps_re * wave_re - taps_im * wave_im
            delay_im = taps_re * wave_im + taps_im * wave_re
            delay_ref[2 * quad + couple] = jnp.concatenate([delay_re, delay_im], axis=0).astype(BF16)


def make_matrix(first, couple, forward, traces_ref, shift_ref, delay_ref, matrix_ref):
    receivers = shift_ref.shape[1]
    source = first + 2 * couple
    zeros = jnp.zeros((KSHIFT, receivers), F32)
    kinds = lax.broadcasted_iota(jnp.int32, (KSHIFT, receivers), 0)
    signals = traces_ref[2 * couple : 2 * couple + 2].reshape(2 * receivers, NT)
    raw = mm(forward, signals, NT_DIMS)
    hot = [
        (kinds == shift_ref[source + half : source + half + 1, :]).astype(F32)
        for half in range(2)
    ]
    hot = jnp.concatenate(
        [jnp.concatenate([hot[0], zeros], axis=1), jnp.concatenate([zeros, hot[1]], axis=1)],
        axis=0,
    ).astype(BF16)
    delay = mm(delay_ref[couple], hot)
    re = raw[:NF] * delay[:NF] - raw[NF:] * delay[NF:]
    im = raw[:NF] * delay[NF:] + raw[NF:] * delay[:NF]
    matrix_ref[:, couple, :, :receivers] = interleave(
        re[:, :receivers], re[:, receivers:]
    ).astype(BF16)
    matrix_ref[:, couple, :, receivers:] = interleave(
        im[:, :receivers], im[:, receivers:]
    ).astype(BF16)


def make_sums(first, rcv_index, matrix_ref, vector_ref, kept_ref, gather, onset_ref, sum_ref):
    half = 2 * matrix_ref.shape[1]
    sets = vector_ref.shape[1] // (LANES // half // 2)

    def store(row, value):
        for one in range(sets):
            sum_ref[one * NF + row : one * NF + row + 2 * GROUP, :] = value[one]

    apply_matrix([matrix_ref], vector_ref, kept_ref, gather, store)
    own = onset_ref[...].astype(F32)[:, first : first + half]
    turns = LANES // (2 * half)
    own = jnp.concatenate([own[0:1], own[1:2]] * turns, axis=1)
    own = jnp.broadcast_to(own, (2 * GROUP, LANES))
    row = lax.broadcasted_iota(jnp.int32, own.shape, 0)
    lane = lax.broadcasted_iota(jnp.int32, own.shape, 1)
    here = (row == rcv_index // turns) & (lane // (2 * half) == rcv_index % turns)
    sum_ref[sets * NF :, :] = jnp.where(here, own, 0.0).astype(BF16)


def first_kernel(
    gain, index_ref, traces_hbm, shift_hbm, deconv_hbm, focal_hbm, onset_hbm,
    forward_hbm, taps_hbm, gather_hbm, matrix_ref, sum_ref, own_ref, vector_ref,
    kept_ref, traces_ref, shift_ref, deconv_ref, focal_ref, onset_ref,
    forward_ref, taps_ref, gather_ref, trace_sem, small_sem, delay_ref,
):
    half = traces_ref.shape[0]
    fields = focal_ref.shape[0]
    small = [
        pltpu.make_async_copy(source, target, small_sem.at[place])
        for place, (source, target) in enumerate(
            [
                (forward_hbm, forward_ref),
                (deconv_hbm, deconv_ref),
                (taps_hbm, taps_ref),
                (focal_hbm, focal_ref),
                (shift_hbm, shift_ref),
                (gather_hbm, gather_ref),
                (onset_hbm, onset_ref),
            ]
        )
    ]
    chunks = trace_sem.shape[0]
    step = half // chunks
    large = [
        pltpu.make_async_copy(
            traces_hbm.at[pl.ds(chunk * step, step)],
            traces_ref.at[pl.ds(chunk * step, step)],
            trace_sem.at[chunk],
        )
        for chunk in range(chunks)
    ]
    for copy in small[:5] + large + small[5:]:
        copy.start()
    for copy in small[:3]:
        copy.wait()
    make_delays(0, half, forward_ref, deconv_ref, taps_ref, gain, delay_ref)
    forward = forward_ref[...]
    small[3].wait()
    own_ref[...] = focal_ref[index_ref[0]]
    for place in range(fields):
        spectra = mm(forward, focal_ref[place], NT_DIMS)
        store_vector(vector_ref, place, spectra[:NF], spectra[NF:])
    small[4].wait()
    for couple in range(half // 2):
        if (2 * couple) % step == 0:
            large[2 * couple // step].wait()
        make_matrix(0, couple, forward, traces_ref, shift_ref, delay_ref, matrix_ref)
    small[5].wait()
    small[6].wait()
    make_sums(
        0, index_ref[1], matrix_ref, vector_ref, kept_ref, gather_ref[...], onset_ref, sum_ref
    )


def rest_kernel(
    gain, index_ref, traces_ref, shift_ref, deconv_ref, onset_ref, forward_ref, taps_ref,
    gather_ref, vector_ref, matrix_ref, sum_ref, kept_ref, delay_ref,
):
    half = traces_ref.shape[0] // 2
    make_delays(half, half, forward_ref, deconv_ref, taps_ref, gain, delay_ref)
    forward = forward_ref[...]
    upper = traces_ref.at[pl.ds(half, half)]
    for couple in range(half // 2):
        make_matrix(half, couple, forward, upper, shift_ref, delay_ref, matrix_ref)
    make_sums(
        half, index_ref[1], matrix_ref, vector_ref, kept_ref, gather_ref[...], onset_ref, sum_ref
    )


def split_halves(first, second):
    lane = lax.broadcasted_iota(jnp.int32, first.shape, 1)
    low = lane < LANES // 2
    re = jnp.where(low, first, pltpu.roll(second, LANES // 2, 1))
    im = jnp.where(low, pltpu.roll(first, LANES // 2, 1), second)
    return jnp.concatenate([re, im], axis=0)


def mute(signal, onset):
    sample = lax.broadcasted_iota(jnp.int32, signal.shape, 0)
    folded = jnp.minimum(sample, NT - sample).astype(F32)
    return jnp.where(folded < onset, signal, 0.0)


def mute_half(index_ref, mine_ref, other_ref, forward, inverse, spread_ref, vector_ref):
    shot_index = index_ref[0]
    rcv_index = index_ref[1]
    core = shot_index % 2
    chip = shot_index // 2
    width = vector_ref.shape[-1]
    half = width // GROUP
    blocks = LANES // half
    sets = (mine_ref.shape[0] - 2 * GROUP) // NF
    turns = blocks // 2
    onsets = mine_ref[sets * NF :, :].astype(F32) + other_ref[sets * NF :, :].astype(F32)
    owned = jnp.zeros((NT, LANES), F32)
    diagonal = same_bin(2 * NF, 2 * width)
    for couple in range(sets // 2):
        rows = slice(2 * couple * NF, 2 * (couple + 1) * NF)
        total = mine_ref[rows, :].astype(F32) + other_ref[rows, :].astype(F32)
        spectra = split_halves(total[:NF], total[NF:]).astype(BF16)
        signal = mute(mm(inverse, spectra), onsets[couple : couple + 1, :])
        owned = jnp.where(rcv_index // turns == couple, signal, owned)
        echo = mm(forward, signal.astype(BF16)).astype(BF16)
        for pair in range(blocks // 2):
            slot = (couple * (blocks // 2) + pair) ^ chip
            wide = jnp.where(diagonal, mm(echo, spread_ref[core, pair]), 0.0)
            for part in range(2):
                rows = slice(part * NF, (part + 1) * NF)
                vector_ref[:, part, slot] = interleave(
                    wide[rows, :width], wide[rows, width:]
                ).astype(BF16)
    turn = (turns - rcv_index % turns) % turns
    owned = pltpu.roll(owned, turn * (2 * half), 1)
    return jnp.transpose(owned)[: 2 * half].reshape(2, half, NT)


def mute_kernel(
    index_ref, mine_ref, other_ref, forward_ref, inverse_ref, spread_ref, vector_ref, field_ref
):
    field_ref[...] = mute_half(
        index_ref, mine_ref, other_ref, forward_ref[...], inverse_ref[...], spread_ref, vector_ref
    )


def adjoint_kernel(
    index_ref, mine_ref, other_ref, forward_ref, inverse_ref, spread_ref,
    lower_ref, field_half_ref, first_ref, rest_ref, *refs
):
    field_ref, upper_ref = refs[-2:]
    pairs = (len(refs) - 2) // 2
    keep_refs, send_refs = refs[:pairs], refs[pairs : 2 * pairs]
    receivers = first_ref.shape[-1] // 2
    width = lower_ref.shape[-1]
    half = width // GROUP
    field_ref[:, :half] = field_half_ref[...]
    field_ref[:, half:] = mute_half(
        index_ref, mine_ref, other_ref, forward_ref[...], inverse_ref[...], spread_ref, upper_ref
    )

    def one(group):
        rows = 2 * pairs * 2 * GROUP
        vector = jnp.concatenate(
            [ref[group].reshape(rows, width) for ref in (lower_ref, upper_ref)], axis=1
        )
        matrix = jnp.concatenate(
            [ref[group].reshape(width, 2 * receivers) for ref in (first_ref, rest_ref)], axis=0
        )
        full = mm(vector, matrix).reshape(2, pairs, 2, GROUP, 2 * receivers)
        re = full[0, ..., :receivers] + full[1, ..., receivers:]
        im = full[1, ..., :receivers] - full[0, ..., receivers:]
        return re, im

    for couple in range(NG // 2):
        even = one(2 * couple)
        odd = one(2 * couple + 1)
        for part in range(2):
            both = jnp.concatenate([even[part], odd[part]], axis=2).astype(BF16)
            row = part * NF + couple * 2 * GROUP
            for slot in range(pairs):
                keep_refs[slot][row : row + 2 * GROUP, :] = both[slot, 0]
                send_refs[slot][row : row + 2 * GROUP, :] = both[slot, 1]


def downgoing_kernel(*refs):
    parts = refs[:-6]
    focal_ref, onset_ref, forward_ref, inverse_ref, field_ref, plus_ref = refs[-6:]
    total = parts[0][...].astype(F32)
    for part in parts[1:]:
        total = total + part[...].astype(F32)
    onset = onset_ref[...].astype(F32)
    signal = mute(mm(inverse_ref[...], total.astype(BF16)), onset)
    field = focal_ref[...].astype(F32) + jnp.transpose(signal)
    field_ref[0] = field
    spectra = mm(forward_ref[...], field.astype(BF16), NT_DIMS)
    plus_ref[...] = interleave(spectra[:NF], spectra[NF:]).astype(BF16)


def second_kernel(pairs, index_ref, *refs):
    near_refs, far_refs = refs[:pairs], refs[pairs : 2 * pairs]
    first_ref, rest_ref, gather_ref = refs[2 * pairs : 2 * pairs + 3]
    sum_refs = refs[2 * pairs + 3 : -2]
    vector_ref, kept_ref = refs[-2:]
    shot_index = index_ref[0]
    rcv_index = index_ref[1]
    core = shot_index % 2
    chip = shot_index // 2
    for distance in range(pairs):
        slot = (chip ^ distance) ^ rcv_index
        store_vector(vector_ref, 2 * slot + core, *unpack(near_refs[distance]))
        store_vector(vector_ref, 2 * slot + 1 - core, *unpack(far_refs[distance]))

    def store(row, value):
        for slot in range(pairs):
            sum_refs[slot][row : row + 2 * GROUP, :] = value[slot]

    apply_matrix([first_ref, rest_ref], vector_ref, kept_ref, gather_ref[...], store)


def final_kernel(*refs):
    parts = refs[:-3]
    onset_ref, inverse_ref, field_ref = refs[-3:]
    total = parts[0][...].astype(F32)
    for part in parts[1:]:
        total = total + part[...].astype(F32)
    spectra = split_halves(total, total).astype(BF16)
    onset = onset_ref[...].astype(F32)
    onset = jnp.concatenate([onset[0:1], onset[1:2]] * 2, axis=1)
    signal = mute(mm(inverse_ref[...], spectra), onset)
    field_ref[...] = jnp.transpose(signal)[: LANES // 2].reshape(field_ref.shape)


def vmem(count):
    return [pl.BlockSpec(memory_space=pltpu.VMEM) for _ in range(count)]


def smem():
    return [pl.BlockSpec(memory_space=pltpu.SMEM)]


def hbm(count):
    return [pl.BlockSpec(memory_space=pltpu.HBM) for _ in range(count)]


def call(kernel, name, out_shape, in_specs, scratch=(), work=1.0e9):
    many = isinstance(out_shape, (tuple, list))
    return pl.pallas_call(
        kernel,
        name=name,
        out_shape=out_shape,
        in_specs=in_specs,
        out_specs=vmem(len(out_shape)) if many else vmem(1)[0],
        scratch_shapes=list(scratch),
        compiler_params=pltpu.CompilerParams(vmem_limit_bytes=40 << 20),
        cost_estimate=pl.CostEstimate(flops=int(work), bytes_accessed=1 << 20, transcendentals=0),
    )


def exchange(value, axis, distance):
    count = lax.axis_size(axis)
    return lax.ppermute(value, axis, [(place, place ^ distance) for place in range(count)])


def add_rounded(left, right):
    return (left.astype(F32) + right.astype(F32)).astype(BF16)


def body(traces, shift_index, deconv, focal_start, onset_source, onset_receiver):
    shot_count = lax.axis_size("shot")
    rcv_count = lax.axis_size("rcv")
    sources, receivers, _ = traces.shape
    focal_total = focal_start.shape[0]
    pairs = focal_total // 2
    assert onset_source.shape[0] == 2 and pairs == rcv_count
    assert focal_total == shot_count and 4 * sources == LANES and receivers == LANES
    gain = 1.0 / math.sqrt(NT * receivers * rcv_count)
    tables = make_tables(sources)
    index = jnp.stack([lax.axis_index("shot"), lax.axis_index("rcv")]).astype(jnp.int32)
    shape = jax.ShapeDtypeStruct
    half = sources // 2
    sets = focal_total // (LANES // half // 2)
    vector = shape((NG, focal_total, 2 * GROUP, 2 * receivers), BF16)
    half_matrix = shape((NG, half // 2, 2 * GROUP, 2 * receivers), BF16)
    half_sums = shape((sets * NF + 2 * GROUP, LANES), BF16)
    half_kept = pltpu.VMEM((NG * focal_total * 2 * GROUP, half * GROUP), BF16)
    half_delays = pltpu.VMEM((half // 2, 2 * NF, LANES), BF16)
    assert sets % 2 == 0 and rcv_count <= 2 * GROUP * (LANES // half // 2)

    def buffer(value):
        return pltpu.VMEM(value.shape, value.dtype)

    inputs = (
        traces, shift_index, deconv, focal_start, onset_source,
        tables["forward"], tables["taps"], tables["gather_half"],
    )
    first, first_sum, focal_own, start = call(
        functools.partial(first_kernel, gain),
        "first",
        (half_matrix, half_sums, shape((receivers, NT), BF16), vector),
        smem() + hbm(len(inputs)),
        [half_kept, pltpu.VMEM((half, receivers, NT), BF16)]
        + [buffer(value) for value in inputs[1:]]
        + [pltpu.SemaphoreType.DMA((2,)), pltpu.SemaphoreType.DMA((7,)), half_delays],
        work=4.0e9,
    )(index, *[pltpu.with_memory_space_constraint(value, pltpu.HBM) for value in inputs])
    rest, rest_sum = call(
        functools.partial(rest_kernel, gain),
        "rest",
        (half_matrix, half_sums),
        smem() + vmem(8),
        [half_kept, half_delays],
        work=3.0e9,
    )(
        index, traces, shift_index, deconv, onset_source,
        tables["forward"], tables["taps"], tables["gather_half"], start,
    )

    mine = [first_sum, rest_sum]
    other = [exchange(value, "rcv", 1) for value in mine]
    distance = 1
    while 2 * distance < rcv_count:
        distance *= 2
        mine = [add_rounded(left, right) for left, right in zip(mine, other)]
        other = [exchange(value, "rcv", distance) for value in mine]

    echo = shape((NG, 2, pairs, 2 * GROUP, half * GROUP), BF16)
    shared = (tables["forward"], tables["inverse"], tables["spread"])
    lower, field_half = call(
        mute_kernel,
        "mute",
        (echo, shape((2, half, NT), F32)),
        smem() + vmem(5),
        work=1.0e9,
    )(index, mine[0], other[0], *shared)

    field = shape((2 * NF, receivers), BF16)
    *blocks, upgoing_first = call(
        adjoint_kernel,
        "adjoint",
        [field] * (2 * pairs) + [shape((2, sources, NT), F32)],
        smem() + vmem(9),
        [buffer(echo)],
        work=2.0e9,
    )(index, mine[1], other[1], *shared, lower, field_half, first, rest)

    parts = []
    for distance in reversed(range(pairs)):
        block = add_rounded(blocks[distance], exchange(blocks[pairs + distance], "shot", 1))
        parts.append(exchange(block, "shot", 2 * distance) if distance else block)

    downgoing, plus = call(
        downgoing_kernel,
        "downgoing",
        (
            shape((1, receivers, NT), F32),
            shape((NG, 2 * GROUP, receivers), BF16),
        ),
        vmem(pairs + 4),
    )(*parts, focal_own, onset_receiver, tables["forward"], tables["inverse"])

    near = [plus]
    for distance in range(1, pairs):
        near.append(exchange(plus, "shot", 2 * distance))
    far = [exchange(value, "shot", 1) for value in near]

    parts = call(
        functools.partial(second_kernel, pairs),
        "second",
        [shape((NF, LANES), BF16)] * pairs,
        smem() + vmem(2 * pairs + 3),
        [buffer(vector), pltpu.VMEM((NG * focal_total * 2 * GROUP, sources * GROUP), BF16)],
    )(index, *near, *far, first, rest, tables["gather"])

    parts = [parts[0]] + [
        exchange(parts[distance], "rcv", distance) for distance in range(1, rcv_count)
    ]
    upgoing_second = call(
        final_kernel, "final", shape((2, sources, NT), F32), vmem(len(parts) + 2)
    )(*parts, onset_source, tables["inverse"])
    return (upgoing_first, downgoing, upgoing_second)


def solution(mesh):
    placed = (
        P("shot", "rcv", None),
        P("shot", "rcv"),
        P("shot", None),
        P(None, "rcv", None),
        P("rcv", "shot"),
        P("shot", "rcv"),
    )
    return jax.shard_map(
        body,
        mesh=mesh,
        in_specs=placed,
        out_specs=(P("rcv", "shot", None), P("shot", "rcv", None), P("rcv", "shot", None)),
        check_vma=False,
    )
```

```python
import functools
import math

import jax
import jax.numpy as jnp
import numpy as np
from jax import lax
from jax.experimental import pallas as pl
from jax.experimental.pallas import tpu as pltpu
from jax.sharding import PartitionSpec as P

NT = 256
NF = 128
TAPS = 64
KSHIFT = 64
LANES = 128
GROUP = 8
NG = NF // GROUP

F32 = jnp.float32
BF16 = jnp.bfloat16
NN = (((1,), (0,)), ((), ()))
NT_DIMS = (((1,), (1,)), ((), ()))


def make_tables(source_local):
    sample = np.arange(NT)
    bins = np.arange(NF)
    angles = 2.0 * np.pi / NT * (bins[:, None] * sample[None, :] % NT)
    forward = np.concatenate([np.cos(angles), -np.sin(angles)], axis=0)
    weights = np.where(bins == 0, 1.0, 2.0) / NT
    inverse = (forward * np.concatenate([weights, weights])[:, None]).T
    tap = np.arange(TAPS, dtype=np.float64)
    fraction = np.arange(KSHIFT) * (TAPS / (4.0 * KSHIFT))
    offset = tap[None, :] - 0.375 * TAPS - fraction[:, None]
    window = 0.5 - 0.5 * np.cos(2.0 * np.pi * (tap + 0.5) / TAPS)
    tap_spec = forward[:, :TAPS] @ (np.sinc(offset) * window[None, :]).T
    return dict(
        forward=jnp.asarray(forward, F32).astype(BF16),
        inverse=jnp.asarray(inverse, F32).astype(BF16),
        taps=jnp.asarray(np.tile(tap_spec, (1, LANES // KSHIFT)), F32),
        gather=gather_table(source_local),
        gather_half=gather_table(source_local // 2),
        spread=spread_table(source_local // 2),
    )


def gather_table(sources):
    source_of = np.arange(sources * GROUP) // GROUP
    pick = source_of[:, None] == np.arange(sources)[None, :]
    return jnp.asarray(np.tile(pick, (1, LANES // sources)), F32).astype(BF16)


def spread_table(sources):
    pick = (np.arange(sources * GROUP)[None, :] // GROUP == np.arange(sources)[:, None]).astype(
        np.float32
    )
    blocks = LANES // sources
    table = np.zeros((2, blocks // 2, blocks, sources, 2, sources * GROUP), np.float32)
    for core in range(2):
        for pair in range(blocks // 2):
            table[core, pair, 2 * pair + core, :, 0] = pick
            table[core, pair, 2 * pair + 1 - core, :, 1] = pick
    table = table.reshape(2, blocks // 2, LANES, 2 * sources * GROUP)
    return jnp.asarray(table, F32).astype(BF16)


def mm(left, right, dims=NN):
    return lax.dot_general(left, right, dims, preferred_element_type=F32)


def interleave(first, second):
    width = first.shape[-1]
    pair = jnp.stack(
        [first.reshape(NG, GROUP, width), second.reshape(NG, GROUP, width)], axis=1
    )
    return pair.reshape(NG, 2 * GROUP, width)


def same_bin(rows, lanes):
    row = lax.broadcasted_iota(jnp.int32, (rows, lanes), 0)
    lane = lax.broadcasted_iota(jnp.int32, (rows, lanes), 1)
    return (row % GROUP) == (lane % GROUP)


def store_vector(vector_ref, place, re, im):
    receivers = re.shape[-1]
    vector_ref[:, place, :, :receivers] = interleave(re, im).astype(BF16)
    vector_ref[:, place, :, receivers:] = interleave(-im, re).astype(BF16)


def unpack(spectra_ref):
    receivers = spectra_ref.shape[-1]
    values = spectra_ref[...].astype(F32).reshape(NG, 2, GROUP, receivers)
    return values[:, 0].reshape(NF, receivers), values[:, 1].reshape(NF, receivers)


def apply_matrix(matrix_refs, vector_ref, kept_ref, gather, store):
    fields = vector_ref.shape[1]
    rows = fields * 2 * GROUP
    half = matrix_refs[0].shape[1] * matrix_refs[0].shape[2]
    width = half * len(matrix_refs)
    blocks = LANES // (width // GROUP)
    members = blocks // 2
    sets = fields // members
    diagonal = same_bin(rows, width)
    block_of = lax.broadcasted_iota(jnp.int32, (sets, GROUP, LANES), 2) // (LANES // blocks)

    for group in range(NG):
        vector = vector_ref[group].reshape(rows, vector_ref.shape[-1])
        matrix = [ref[group].reshape(half, ref.shape[-1]) for ref in matrix_refs]
        matrix = matrix[0] if len(matrix) == 1 else jnp.concatenate(matrix, axis=0)
        full = mm(vector, matrix, NT_DIMS)
        kept_ref[group * rows : (group + 1) * rows, :] = jnp.where(diagonal, full, 0.0).astype(BF16)

    for couple in range(NG // 2):
        kept = kept_ref[couple * 2 * rows : (couple + 1) * 2 * rows, :]
        spread = mm(kept, gather).reshape(2, sets, members, 2, GROUP, LANES)
        both = []
        for one in range(2):
            value = spread[one, :, 0, 0]
            for block in range(1, blocks):
                term = spread[one, :, block % members, block // members]
                value = jnp.where(block_of == block, term, value)
            both.append(value)
        store(couple * 2 * GROUP, jnp.concatenate(both, axis=1).astype(BF16))


def make_delays(first, count, forward_ref, deconv_ref, taps_ref, gain, delay_ref):
    deconv = deconv_ref[...]
    sources = deconv.shape[0]
    deconv_high = deconv.astype(BF16)
    deconv_low = (deconv - deconv_high.astype(F32)).astype(BF16)
    head = forward_ref[:, :TAPS]
    wave = (mm(head, deconv_high, NT_DIMS) + mm(head, deconv_low, NT_DIMS)) * gain
    wave_high = wave.astype(BF16)
    wave_low = (wave - wave_high.astype(F32)).astype(BF16)
    wave_both = jnp.concatenate([wave_high, wave_low], axis=1)
    taps = taps_ref[...]
    taps_re, taps_im = taps[:NF], taps[NF:]
    owner = lax.broadcasted_iota(jnp.int32, (2 * sources, 2 * LANES), 0) % sources
    place = lax.broadcasted_iota(jnp.int32, (2 * sources, 2 * LANES), 1) // KSHIFT
    for quad in range(count // 4):
        spread = mm(wave_both, (owner == place + (first + 4 * quad)).astype(F32).astype(BF16))
        for couple in range(2):
            lanes = slice(couple * LANES, (couple + 1) * LANES)
            wave_re, wave_im = spread[:NF, lanes], spread[NF:, lanes]
            delay_re = taps_re * wave_re - taps_im * wave_im
            delay_im = taps_re * wave_im + taps_im * wave_re
            delay_ref[2 * quad + couple] = jnp.concatenate([delay_re, delay_im], axis=0).astype(BF16)


def make_matrix(first, couple, forward, traces_ref, shift_ref, delay_ref, matrix_ref):
    receivers = shift_ref.shape[1]
    source = first + 2 * couple
    zeros = jnp.zeros((KSHIFT, receivers), F32)
    kinds = lax.broadcasted_iota(jnp.int32, (KSHIFT, receivers), 0)
    signals = traces_ref[2 * couple : 2 * couple + 2].reshape(2 * receivers, NT)
    raw = mm(forward, signals, NT_DIMS)
    hot = [
        (kinds == shift_ref[source + half : source + half + 1, :]).astype(F32)
        for half in range(2)
    ]
    hot = jnp.concatenate(
        [jnp.concatenate([hot[0], zeros], axis=1), jnp.concatenate([zeros, hot[1]], axis=1)],
        axis=0,
    ).astype(BF16)
    delay = mm(delay_ref[couple], hot)
    re = raw[:NF] * delay[:NF] - raw[NF:] * delay[NF:]
    im = raw[:NF] * delay[NF:] + raw[NF:] * delay[:NF]
    matrix_ref[:, couple, :, :receivers] = interleave(
        re[:, :receivers], re[:, receivers:]
    ).astype(BF16)
    matrix_ref[:, couple, :, receivers:] = interleave(
        im[:, :receivers], im[:, receivers:]
    ).astype(BF16)


def make_sums(first, rcv_index, matrix_ref, vector_ref, kept_ref, gather, onset_ref, sum_ref):
    half = 2 * matrix_ref.shape[1]
    sets = vector_ref.shape[1] // (LANES // half // 2)

    def store(row, value):
        for one in range(sets):
            sum_ref[one * NF + row : one * NF + row + 2 * GROUP, :] = value[one]

    apply_matrix([matrix_ref], vector_ref, kept_ref, gather, store)
    own = onset_ref[...].astype(F32)[:, first : first + half]
    turns = LANES // (2 * half)
    own = jnp.concatenate([own[0:1], own[1:2]] * turns, axis=1)
    own = jnp.broadcast_to(own, (2 * GROUP, LANES))
    row = lax.broadcasted_iota(jnp.int32, own.shape, 0)
    lane = lax.broadcasted_iota(jnp.int32, own.shape, 1)
    here = (row == rcv_index // turns) & (lane // (2 * half) == rcv_index % turns)
    sum_ref[sets * NF :, :] = jnp.where(here, own, 0.0).astype(BF16)


def first_kernel(
    gain, index_ref, traces_hbm, shift_hbm, deconv_hbm, focal_hbm, onset_hbm,
    forward_hbm, taps_hbm, gather_hbm, matrix_ref, sum_ref, own_ref, vector_ref,
    upper_ref, shift_ref, deconv_ref, onset_ref, forward_ref, taps_ref, gather_ref,
    kept_ref, traces_ref, focal_ref, large_sem, small_sem, delay_ref,
):
    half = traces_ref.shape[0]
    fields = focal_ref.shape[0]
    small = [
        pltpu.make_async_copy(source, target, small_sem.at[place])
        for place, (source, target) in enumerate(
            [
                (forward_hbm, forward_ref),
                (deconv_hbm, deconv_ref),
                (taps_hbm, taps_ref),
                (shift_hbm, shift_ref),
                (gather_hbm, gather_ref),
                (onset_hbm, onset_ref),
            ]
        )
    ]
    step = half // 4
    fields_step = fields // 2
    ranges = [(focal_hbm, focal_ref, piece * fields_step, 0, fields_step) for piece in range(2)]
    ranges += [(traces_hbm, traces_ref, piece * step, 0, step) for piece in range(4)]
    ranges += [(traces_hbm, upper_ref, piece * 2 * step, half, 2 * step) for piece in range(2)]
    large = [
        pltpu.make_async_copy(
            source.at[pl.ds(offset + start, count)],
            target.at[pl.ds(start, count)],
            large_sem.at[place],
        )
        for place, (source, target, start, offset, count) in enumerate(ranges)
    ]
    for copy in small[:4] + large[:6] + small[4:] + large[6:]:
        copy.start()
    for copy in small[:3]:
        copy.wait()
    make_delays(0, half, forward_ref, deconv_ref, taps_ref, gain, delay_ref)
    forward = forward_ref[...]
    for place in range(fields):
        if place % fields_step == 0:
            large[place // fields_step].wait()
        spectra = mm(forward, focal_ref[place], NT_DIMS)
        store_vector(vector_ref, place, spectra[:NF], spectra[NF:])
    own_ref[...] = focal_ref[index_ref[0]]
    small[3].wait()
    for couple in range(half // 2):
        if (2 * couple) % step == 0:
            large[2 + 2 * couple // step].wait()
        make_matrix(0, couple, forward, traces_ref, shift_ref, delay_ref, matrix_ref)
    small[4].wait()
    small[5].wait()
    make_sums(
        0, index_ref[1], matrix_ref, vector_ref, kept_ref, gather_ref[...], onset_ref, sum_ref
    )
    large[6].wait()
    large[7].wait()


def rest_kernel(
    gain, index_ref, traces_ref, shift_ref, deconv_ref, onset_ref, forward_ref, taps_ref,
    gather_ref, vector_ref, matrix_ref, sum_ref, kept_ref, delay_ref,
):
    half = traces_ref.shape[0]
    make_delays(half, half, forward_ref, deconv_ref, taps_ref, gain, delay_ref)
    forward = forward_ref[...]
    for couple in range(half // 2):
        make_matrix(half, couple, forward, traces_ref, shift_ref, delay_ref, matrix_ref)
    make_sums(
        half, index_ref[1], matrix_ref, vector_ref, kept_ref, gather_ref[...], onset_ref, sum_ref
    )


def split_halves(first, second):
    lane = lax.broadcasted_iota(jnp.int32, first.shape, 1)
    low = lane < LANES // 2
    re = jnp.where(low, first, pltpu.roll(second, LANES // 2, 1))
    im = jnp.where(low, pltpu.roll(first, LANES // 2, 1), second)
    return jnp.concatenate([re, im], axis=0)


def mute(signal, onset):
    sample = lax.broadcasted_iota(jnp.int32, signal.shape, 0)
    folded = jnp.minimum(sample, NT - sample).astype(F32)
    return jnp.where(folded < onset, signal, 0.0)


def mute_half(index_ref, mine_ref, other_ref, forward, inverse, spread_ref, vector_ref):
    shot_index = index_ref[0]
    rcv_index = index_ref[1]
    core = shot_index % 2
    chip = shot_index // 2
    width = vector_ref.shape[-1]
    half = width // GROUP
    blocks = LANES // half
    sets = (mine_ref.shape[0] - 2 * GROUP) // NF
    turns = blocks // 2
    onsets = mine_ref[sets * NF :, :].astype(F32) + other_ref[sets * NF :, :].astype(F32)
    owned = jnp.zeros((NT, LANES), F32)
    diagonal = same_bin(2 * NF, 2 * width)
    for couple in range(sets // 2):
        rows = slice(2 * couple * NF, 2 * (couple + 1) * NF)
        total = mine_ref[rows, :].astype(F32) + other_ref[rows, :].astype(F32)
        spectra = split_halves(total[:NF], total[NF:]).astype(BF16)
        signal = mute(mm(inverse, spectra), onsets[couple : couple + 1, :])
        owned = jnp.where(rcv_index // turns == couple, signal, owned)
        echo = mm(forward, signal.astype(BF16)).astype(BF16)
        for pair in range(blocks // 2):
            slot = (couple * (blocks // 2) + pair) ^ chip
            wide = jnp.where(diagonal, mm(echo, spread_ref[core, pair]), 0.0)
            for part in range(2):
                rows = slice(part * NF, (part + 1) * NF)
                vector_ref[:, part, slot] = interleave(
                    wide[rows, :width], wide[rows, width:]
                ).astype(BF16)
    turn = (turns - rcv_index % turns) % turns
    owned = pltpu.roll(owned, turn * (2 * half), 1)
    return jnp.transpose(owned)[: 2 * half].reshape(2, half, NT)


def mute_kernel(
    index_ref, mine_ref, other_ref, forward_ref, inverse_ref, spread_ref, vector_ref, field_ref
):
    field_ref[...] = mute_half(
        index_ref, mine_ref, other_ref, forward_ref[...], inverse_ref[...], spread_ref, vector_ref
    )


def adjoint_kernel(
    index_ref, mine_ref, other_ref, forward_ref, inverse_ref, spread_ref,
    lower_ref, field_half_ref, first_ref, rest_ref, *refs
):
    keep_ref, far_ref, send_ref, field_hbm, upper_ref, field_ref, field_sem = refs
    pairs = keep_ref.shape[0]
    receivers = first_ref.shape[-1] // 2
    width = lower_ref.shape[-1]
    half = width // GROUP
    field_ref[:, :half] = field_half_ref[...]
    field_ref[:, half:] = mute_half(
        index_ref, mine_ref, other_ref, forward_ref[...], inverse_ref[...], spread_ref, upper_ref
    )
    copy = pltpu.make_async_copy(field_ref, field_hbm, field_sem)
    copy.start()

    def one(group):
        rows = 2 * pairs * 2 * GROUP
        vector = jnp.concatenate(
            [ref[group].reshape(rows, width) for ref in (lower_ref, upper_ref)], axis=1
        )
        matrix = jnp.concatenate(
            [ref[group].reshape(width, 2 * receivers) for ref in (first_ref, rest_ref)], axis=0
        )
        full = mm(vector, matrix).reshape(2, pairs, 2, GROUP, 2 * receivers)
        re = full[0, ..., :receivers] + full[1, ..., receivers:]
        im = full[1, ..., :receivers] - full[0, ..., receivers:]
        return re, im

    for couple in range(NG // 2):
        even = one(2 * couple)
        odd = one(2 * couple + 1)
        for part in range(2):
            both = jnp.concatenate([even[part], odd[part]], axis=2).astype(BF16)
            row = part * NF + couple * 2 * GROUP
            keep_ref[:, row : row + 2 * GROUP, :] = both[:, 0]
            far_ref[row : row + 2 * GROUP, :] = both[pairs - 1, 1]
            send_ref[:, row : row + 2 * GROUP, :] = both[: pairs - 1, 1]
    copy.wait()


def downgoing_kernel(*refs):
    parts = refs[:-6]
    focal_ref, onset_ref, forward_ref, inverse_ref, field_ref, plus_ref = refs[-6:]
    total = parts[0][...].astype(F32)
    for part in parts[1:]:
        total = total + part[...].astype(F32)
    onset = onset_ref[...].astype(F32)
    signal = mute(mm(inverse_ref[...], total.astype(BF16)), onset)
    field = focal_ref[...].astype(F32) + jnp.transpose(signal)
    field_ref[...] = field
    spectra = mm(forward_ref[...], field.astype(BF16), NT_DIMS)
    plus_ref[...] = interleave(spectra[:NF], spectra[NF:]).astype(BF16)


def second_kernel(pairs, index_ref, *refs):
    near_refs, far_refs = refs[:pairs], refs[pairs : 2 * pairs]
    first_ref, rest_ref, gather_ref, field_ref, field_hbm = refs[2 * pairs : 2 * pairs + 5]
    sum_refs = refs[2 * pairs + 5 : -3]
    vector_ref, kept_ref, field_sem = refs[-3:]
    copy = pltpu.make_async_copy(field_ref, field_hbm.at[0], field_sem)
    copy.start()
    shot_index = index_ref[0]
    rcv_index = index_ref[1]
    core = shot_index % 2
    chip = shot_index // 2
    for distance in range(pairs):
        slot = (chip ^ distance) ^ rcv_index
        store_vector(vector_ref, 2 * slot + core, *unpack(near_refs[distance]))
        store_vector(vector_ref, 2 * slot + 1 - core, *unpack(far_refs[distance]))

    def store(row, value):
        for slot in range(pairs):
            sum_refs[slot][row : row + 2 * GROUP, :] = value[slot]

    apply_matrix([first_ref, rest_ref], vector_ref, kept_ref, gather_ref[...], store)
    copy.wait()


def final_kernel(*refs):
    parts = refs[:-3]
    onset_ref, inverse_ref, field_ref = refs[-3:]
    total = parts[0][...].astype(F32)
    for part in parts[1:]:
        total = total + part[...].astype(F32)
    spectra = split_halves(total, total).astype(BF16)
    onset = onset_ref[...].astype(F32)
    onset = jnp.concatenate([onset[0:1], onset[1:2]] * 2, axis=1)
    signal = mute(mm(inverse_ref[...], spectra), onset)
    field_ref[...] = jnp.transpose(signal)[: LANES // 2].reshape(field_ref.shape)


def vmem(count):
    return [pl.BlockSpec(memory_space=pltpu.VMEM) for _ in range(count)]


def smem():
    return [pl.BlockSpec(memory_space=pltpu.SMEM)]


def hbm(count):
    return [pl.BlockSpec(memory_space=pltpu.HBM) for _ in range(count)]


def call(kernel, name, out_shape, in_specs, scratch=(), work=1.0e9, out_specs=None):
    if out_specs is None:
        many = isinstance(out_shape, (tuple, list))
        out_specs = vmem(len(out_shape)) if many else vmem(1)[0]
    return pl.pallas_call(
        kernel,
        name=name,
        out_shape=out_shape,
        in_specs=in_specs,
        out_specs=out_specs,
        scratch_shapes=list(scratch),
        compiler_params=pltpu.CompilerParams(vmem_limit_bytes=40 << 20),
        cost_estimate=pl.CostEstimate(flops=int(work), bytes_accessed=1 << 20, transcendentals=0),
    )


def exchange(value, axis, distance):
    count = lax.axis_size(axis)
    return lax.ppermute(value, axis, [(place, place ^ distance) for place in range(count)])


def add_rounded(left, right):
    return (left.astype(F32) + right.astype(F32)).astype(BF16)


def body(traces, shift_index, deconv, focal_start, onset_source, onset_receiver):
    shot_count = lax.axis_size("shot")
    rcv_count = lax.axis_size("rcv")
    sources, receivers, _ = traces.shape
    focal_total = focal_start.shape[0]
    pairs = focal_total // 2
    assert onset_source.shape[0] == 2 and pairs == rcv_count
    assert focal_total == shot_count and 4 * sources == LANES and receivers == LANES
    gain = 1.0 / math.sqrt(NT * receivers * rcv_count)
    tables = make_tables(sources)
    index = jnp.stack([lax.axis_index("shot"), lax.axis_index("rcv")]).astype(jnp.int32)
    shape = jax.ShapeDtypeStruct
    half = sources // 2
    sets = focal_total // (LANES // half // 2)
    vector = shape((NG, focal_total, 2 * GROUP, 2 * receivers), BF16)
    half_matrix = shape((NG, half // 2, 2 * GROUP, 2 * receivers), BF16)
    half_sums = shape((sets * NF + 2 * GROUP, LANES), BF16)
    half_kept = pltpu.VMEM((NG * focal_total * 2 * GROUP, half * GROUP), BF16)
    half_delays = pltpu.VMEM((half // 2, 2 * NF, LANES), BF16)
    assert sets % 2 == 0 and rcv_count <= 2 * GROUP * (LANES // half // 2)

    def buffer(value):
        return pltpu.VMEM(value.shape, value.dtype)

    inputs = (
        traces, shift_index, deconv, focal_start, onset_source,
        tables["forward"], tables["taps"], tables["gather_half"],
    )
    small = (shift_index, deconv, onset_source) + inputs[5:]
    first, first_sum, focal_own, start, upper, *loaded = call(
        functools.partial(first_kernel, gain),
        "first",
        [
            half_matrix,
            half_sums,
            shape((receivers, NT), BF16),
            vector,
            shape((half, receivers, NT), BF16),
        ]
        + [shape(value.shape, value.dtype) for value in small],
        smem() + hbm(len(inputs)),
        [
            half_kept,
            pltpu.VMEM((half, receivers, NT), BF16),
            buffer(focal_start),
            pltpu.SemaphoreType.DMA((8,)),
            pltpu.SemaphoreType.DMA((6,)),
            half_delays,
        ],
        work=4.0e9,
    )(index, *[pltpu.with_memory_space_constraint(value, pltpu.HBM) for value in inputs])
    forward = loaded[3]
    rest, rest_sum = call(
        functools.partial(rest_kernel, gain),
        "rest",
        (half_matrix, half_sums),
        smem() + vmem(8),
        [half_kept, half_delays],
        work=3.0e9,
    )(index, upper, *loaded, start)

    mine = [first_sum, rest_sum]
    other = [exchange(value, "rcv", 1) for value in mine]
    distance = 1
    while 2 * distance < rcv_count:
        distance *= 2
        mine = [add_rounded(left, right) for left, right in zip(mine, other)]
        other = [exchange(value, "rcv", distance) for value in mine]

    echo = shape((NG, 2, pairs, 2 * GROUP, half * GROUP), BF16)
    shared = (forward, tables["inverse"], tables["spread"])
    lower, field_half = call(
        mute_kernel,
        "mute",
        (echo, shape((2, half, NT), F32)),
        smem() + vmem(5),
        work=1.0e9,
    )(index, mine[0], other[0], *shared)

    keep, far, send, upgoing_first = call(
        adjoint_kernel,
        "adjoint",
        [
            shape((pairs, 2 * NF, receivers), BF16),
            shape((2 * NF, receivers), BF16),
            shape((pairs - 1, 2 * NF, receivers), BF16),
            shape((2, sources, NT), F32),
        ],
        smem() + vmem(9),
        [buffer(echo), pltpu.VMEM((2, sources, NT), F32), pltpu.SemaphoreType.DMA(())],
        work=2.0e9,
        out_specs=vmem(3) + hbm(1),
    )(index, mine[1], other[1], *shared, lower, field_half, first, rest)

    far = exchange(far, "shot", 1)
    near = exchange(send, "shot", 1)
    parts = [exchange(add_rounded(keep[pairs - 1], far), "shot", 2 * (pairs - 1))]
    for distance in reversed(range(pairs - 1)):
        block = add_rounded(keep[distance], near[distance])
        parts.append(exchange(block, "shot", 2 * distance) if distance else block)

    downgoing, plus = call(
        downgoing_kernel,
        "downgoing",
        (
            shape((receivers, NT), F32),
            shape((NG, 2 * GROUP, receivers), BF16),
        ),
        vmem(pairs + 4),
    )(*parts, focal_own, onset_receiver, forward, tables["inverse"])

    near = [plus]
    for distance in range(1, pairs):
        near.append(exchange(plus, "shot", 2 * distance))
    far = [exchange(value, "shot", 1) for value in near]

    downgoing, *parts = call(
        functools.partial(second_kernel, pairs),
        "second",
        [shape((1, receivers, NT), F32)] + [shape((NF, LANES), BF16)] * pairs,
        smem() + vmem(2 * pairs + 4),
        [
            buffer(vector),
            pltpu.VMEM((NG * focal_total * 2 * GROUP, sources * GROUP), BF16),
            pltpu.SemaphoreType.DMA(()),
        ],
        out_specs=hbm(1) + vmem(pairs),
    )(index, *near, *far, first, rest, tables["gather"], downgoing)

    parts = [
        exchange(parts[distance], "rcv", distance) for distance in reversed(range(1, rcv_count))
    ] + [parts[0]]
    upgoing_second = call(
        final_kernel, "final", shape((2, sources, NT), F32), vmem(len(parts) + 2)
    )(*parts, loaded[2], tables["inverse"])
    return (upgoing_first, downgoing, upgoing_second)


def solution(mesh):
    placed = (
        P("shot", "rcv", None),
        P("shot", "rcv"),
        P("shot", None),
        P(None, "rcv", None),
        P("rcv", "shot"),
        P("shot", "rcv"),
    )
    return jax.shard_map(
        body,
        mesh=mesh,
        in_specs=placed,
        out_specs=(P("rcv", "shot", None), P("shot", "rcv", None), P("rcv", "shot", None)),
        check_vma=False,
    )
```

```python
import functools
import math

import jax
import jax.numpy as jnp
import numpy as np
from jax import lax
from jax.experimental import pallas as pl
from jax.experimental.pallas import tpu as pltpu
from jax.sharding import PartitionSpec as P

NT = 256
NF = 128
TAPS = 64
KSHIFT = 64
LANES = 128
GROUP = 8
NG = NF // GROUP

F32 = jnp.float32
BF16 = jnp.bfloat16
NN = (((1,), (0,)), ((), ()))
NT_DIMS = (((1,), (1,)), ((), ()))


def make_tables(source_local):
    sample = np.arange(NT)
    bins = np.arange(NF)
    angles = 2.0 * np.pi / NT * (bins[:, None] * sample[None, :] % NT)
    forward = np.concatenate([np.cos(angles), -np.sin(angles)], axis=0)
    weights = np.where(bins == 0, 1.0, 2.0) / NT
    inverse = (forward * np.concatenate([weights, weights])[:, None]).T
    tap = np.arange(TAPS, dtype=np.float64)
    fraction = np.arange(KSHIFT) * (TAPS / (4.0 * KSHIFT))
    offset = tap[None, :] - 0.375 * TAPS - fraction[:, None]
    window = 0.5 - 0.5 * np.cos(2.0 * np.pi * (tap + 0.5) / TAPS)
    tap_spec = forward[:, :TAPS] @ (np.sinc(offset) * window[None, :]).T
    return dict(
        forward=jnp.asarray(forward, F32).astype(BF16),
        inverse=jnp.asarray(inverse, F32).astype(BF16),
        taps=jnp.asarray(np.tile(tap_spec, (1, LANES // KSHIFT)), F32),
        gather=gather_table(source_local),
        gather_half=gather_table(source_local // 2),
        spread=spread_table(source_local // 2),
    )


def gather_table(sources):
    source_of = np.arange(sources * GROUP) // GROUP
    pick = source_of[:, None] == np.arange(sources)[None, :]
    return jnp.asarray(np.tile(pick, (1, LANES // sources)), F32).astype(BF16)


def spread_table(sources):
    pick = (np.arange(sources * GROUP)[None, :] // GROUP == np.arange(sources)[:, None]).astype(
        np.float32
    )
    blocks = LANES // sources
    table = np.zeros((2, blocks // 2, blocks, sources, 2, sources * GROUP), np.float32)
    for core in range(2):
        for pair in range(blocks // 2):
            table[core, pair, 2 * pair + core, :, 0] = pick
            table[core, pair, 2 * pair + 1 - core, :, 1] = pick
    table = table.reshape(2, blocks // 2, LANES, 2 * sources * GROUP)
    return jnp.asarray(table, F32).astype(BF16)


def mm(left, right, dims=NN):
    return lax.dot_general(left, right, dims, preferred_element_type=F32)


def interleave(first, second):
    width = first.shape[-1]
    pair = jnp.stack(
        [first.reshape(NG, GROUP, width), second.reshape(NG, GROUP, width)], axis=1
    )
    return pair.reshape(NG, 2 * GROUP, width)


def same_bin(rows, lanes):
    row = lax.broadcasted_iota(jnp.int32, (rows, lanes), 0)
    lane = lax.broadcasted_iota(jnp.int32, (rows, lanes), 1)
    return (row % GROUP) == (lane % GROUP)


def store_vector(vector_ref, place, re, im):
    receivers = re.shape[-1]
    vector_ref[:, place, :, :receivers] = interleave(re, im).astype(BF16)
    vector_ref[:, place, :, receivers:] = interleave(-im, re).astype(BF16)


def unpack(spectra_ref):
    receivers = spectra_ref.shape[-1]
    values = spectra_ref[...].astype(F32).reshape(NG, 2, GROUP, receivers)
    return values[:, 0].reshape(NF, receivers), values[:, 1].reshape(NF, receivers)


def apply_matrix(matrix_refs, vector_ref, kept_ref, gather, store):
    fields = vector_ref.shape[1]
    rows = fields * 2 * GROUP
    half = matrix_refs[0].shape[1] * matrix_refs[0].shape[2]
    width = half * len(matrix_refs)
    blocks = LANES // (width // GROUP)
    members = blocks // 2
    sets = fields // members
    diagonal = same_bin(rows, width)
    block_of = lax.broadcasted_iota(jnp.int32, (sets, GROUP, LANES), 2) // (LANES // blocks)

    for group in range(NG):
        vector = vector_ref[group].reshape(rows, vector_ref.shape[-1])
        matrix = [ref[group].reshape(half, ref.shape[-1]) for ref in matrix_refs]
        matrix = matrix[0] if len(matrix) == 1 else jnp.concatenate(matrix, axis=0)
        full = mm(vector, matrix, NT_DIMS)
        kept_ref[group * rows : (group + 1) * rows, :] = jnp.where(diagonal, full, 0.0).astype(BF16)

    for couple in range(NG // 2):
        kept = kept_ref[couple * 2 * rows : (couple + 1) * 2 * rows, :]
        spread = mm(kept, gather).reshape(2, sets, members, 2, GROUP, LANES)
        both = []
        for one in range(2):
            value = spread[one, :, 0, 0]
            for block in range(1, blocks):
                term = spread[one, :, block % members, block // members]
                value = jnp.where(block_of == block, term, value)
            both.append(value)
        store(couple * 2 * GROUP, jnp.concatenate(both, axis=1).astype(BF16))


def make_delays(first, count, forward_ref, deconv_ref, taps_ref, gain, delay_ref):
    deconv = deconv_ref[...]
    sources = deconv.shape[0]
    deconv_high = deconv.astype(BF16)
    deconv_low = (deconv - deconv_high.astype(F32)).astype(BF16)
    head = forward_ref[:, :TAPS]
    wave = (mm(head, deconv_high, NT_DIMS) + mm(head, deconv_low, NT_DIMS)) * gain
    wave_high = wave.astype(BF16)
    wave_low = (wave - wave_high.astype(F32)).astype(BF16)
    wave_both = jnp.concatenate([wave_high, wave_low], axis=1)
    taps = taps_ref[...]
    taps_re, taps_im = taps[:NF], taps[NF:]
    owner = lax.broadcasted_iota(jnp.int32, (2 * sources, 2 * LANES), 0) % sources
    place = lax.broadcasted_iota(jnp.int32, (2 * sources, 2 * LANES), 1) // KSHIFT
    for quad in range(count // 4):
        spread = mm(wave_both, (owner == place + (first + 4 * quad)).astype(F32).astype(BF16))
        for couple in range(2):
            lanes = slice(couple * LANES, (couple + 1) * LANES)
            wave_re, wave_im = spread[:NF, lanes], spread[NF:, lanes]
            delay_re = taps_re * wave_re - taps_im * wave_im
            delay_im = taps_re * wave_im + taps_im * wave_re
            delay_ref[2 * quad + couple] = jnp.concatenate([delay_re, delay_im], axis=0).astype(BF16)


def make_matrix(first, couple, forward, traces_ref, shift_ref, delay_ref, matrix_ref):
    receivers = shift_ref.shape[1]
    source = first + 2 * couple
    zeros = jnp.zeros((KSHIFT, receivers), F32)
    kinds = lax.broadcasted_iota(jnp.int32, (KSHIFT, receivers), 0)
    signals = traces_ref[2 * couple : 2 * couple + 2].reshape(2 * receivers, NT)
    raw = mm(forward, signals, NT_DIMS)
    hot = [
        (kinds == shift_ref[source + half : source + half + 1, :]).astype(F32)
        for half in range(2)
    ]
    hot = jnp.concatenate(
        [jnp.concatenate([hot[0], zeros], axis=1), jnp.concatenate([zeros, hot[1]], axis=1)],
        axis=0,
    ).astype(BF16)
    delay = mm(delay_ref[couple], hot)
    re = raw[:NF] * delay[:NF] - raw[NF:] * delay[NF:]
    im = raw[:NF] * delay[NF:] + raw[NF:] * delay[:NF]
    matrix_ref[:, couple, :, :receivers] = interleave(
        re[:, :receivers], re[:, receivers:]
    ).astype(BF16)
    matrix_ref[:, couple, :, receivers:] = interleave(
        im[:, :receivers], im[:, receivers:]
    ).astype(BF16)


def make_sums(first, rcv_index, matrix_ref, vector_ref, kept_ref, gather, onset_ref, sum_ref):
    half = 2 * matrix_ref.shape[1]
    sets = vector_ref.shape[1] // (LANES // half // 2)

    def store(row, value):
        for one in range(sets):
            sum_ref[one * NF + row : one * NF + row + 2 * GROUP, :] = value[one]

    apply_matrix([matrix_ref], vector_ref, kept_ref, gather, store)
    own = onset_ref[...].astype(F32)[:, first : first + half]
    turns = LANES // (2 * half)
    own = jnp.concatenate([own[0:1], own[1:2]] * turns, axis=1)
    own = jnp.broadcast_to(own, (2 * GROUP, LANES))
    row = lax.broadcasted_iota(jnp.int32, own.shape, 0)
    lane = lax.broadcasted_iota(jnp.int32, own.shape, 1)
    here = (row == rcv_index // turns) & (lane // (2 * half) == rcv_index % turns)
    sum_ref[sets * NF :, :] = jnp.where(here, own, 0.0).astype(BF16)


def first_kernel(
    gain, index_ref, traces_hbm, shift_hbm, deconv_hbm, focal_hbm, onset_hbm,
    forward_hbm, taps_hbm, gather_hbm, matrix_ref, sum_ref, own_ref, vector_ref,
    shift_ref, deconv_ref, onset_ref, forward_ref, taps_ref, gather_ref,
    kept_ref, traces_ref, focal_ref, large_sem, small_sem, delay_ref,
):
    half = traces_ref.shape[0]
    fields = focal_ref.shape[0]
    small = [
        pltpu.make_async_copy(source, target, small_sem.at[place])
        for place, (source, target) in enumerate(
            [
                (forward_hbm, forward_ref),
                (deconv_hbm, deconv_ref),
                (taps_hbm, taps_ref),
                (shift_hbm, shift_ref),
                (gather_hbm, gather_ref),
                (onset_hbm, onset_ref),
            ]
        )
    ]
    large = [
        pltpu.make_async_copy(focal_hbm, focal_ref, large_sem.at[0]),
        pltpu.make_async_copy(traces_hbm.at[pl.ds(0, half)], traces_ref, large_sem.at[1]),
    ]
    for copy in small[:3] + large + small[3:]:
        copy.start()
    for copy in small[:3] + large[:1]:
        copy.wait()
    make_delays(0, half, forward_ref, deconv_ref, taps_ref, gain, delay_ref)
    forward = forward_ref[...]
    for place in range(fields):
        spectra = mm(forward, focal_ref[place], NT_DIMS)
        store_vector(vector_ref, place, spectra[:NF], spectra[NF:])
    own_ref[...] = focal_ref[index_ref[0]]
    for copy in small[3:] + large[1:]:
        copy.wait()
    for couple in range(half // 2):
        make_matrix(0, couple, forward, traces_ref, shift_ref, delay_ref, matrix_ref)
    make_sums(
        0, index_ref[1], matrix_ref, vector_ref, kept_ref, gather_ref[...], onset_ref, sum_ref
    )


def rest_kernel(
    gain, index_ref, traces_ref, shift_ref, deconv_ref, onset_ref, forward_ref, taps_ref,
    gather_ref, vector_ref, matrix_ref, sum_ref, kept_ref, delay_ref,
):
    half = traces_ref.shape[0] // 2
    make_delays(half, half, forward_ref, deconv_ref, taps_ref, gain, delay_ref)
    forward = forward_ref[...]
    upper = traces_ref.at[pl.ds(half, half)]
    for couple in range(half // 2):
        make_matrix(half, couple, forward, upper, shift_ref, delay_ref, matrix_ref)
    make_sums(
        half, index_ref[1], matrix_ref, vector_ref, kept_ref, gather_ref[...], onset_ref, sum_ref
    )


def split_halves(first, second):
    lane = lax.broadcasted_iota(jnp.int32, first.shape, 1)
    low = lane < LANES // 2
    re = jnp.where(low, first, pltpu.roll(second, LANES // 2, 1))
    im = jnp.where(low, pltpu.roll(first, LANES // 2, 1), second)
    return jnp.concatenate([re, im], axis=0)


def mute(signal, onset):
    sample = lax.broadcasted_iota(jnp.int32, signal.shape, 0)
    folded = jnp.minimum(sample, NT - sample).astype(F32)
    return jnp.where(folded < onset, signal, 0.0)


def mute_half(index_ref, mine_ref, other_ref, forward, inverse, spread_ref, vector_ref):
    shot_index = index_ref[0]
    rcv_index = index_ref[1]
    core = shot_index % 2
    chip = shot_index // 2
    width = vector_ref.shape[-1]
    half = width // GROUP
    blocks = LANES // half
    sets = (mine_ref.shape[0] - 2 * GROUP) // NF
    turns = blocks // 2
    onsets = mine_ref[sets * NF :, :].astype(F32) + other_ref[sets * NF :, :].astype(F32)
    owned = jnp.zeros((NT, LANES), F32)
    diagonal = same_bin(2 * NF, 2 * width)
    for couple in range(sets // 2):
        rows = slice(2 * couple * NF, 2 * (couple + 1) * NF)
        total = mine_ref[rows, :].astype(F32) + other_ref[rows, :].astype(F32)
        spectra = split_halves(total[:NF], total[NF:]).astype(BF16)
        signal = mute(mm(inverse, spectra), onsets[couple : couple + 1, :])
        owned = jnp.where(rcv_index // turns == couple, signal, owned)
        echo = mm(forward, signal.astype(BF16)).astype(BF16)
        for pair in range(blocks // 2):
            slot = (couple * (blocks // 2) + pair) ^ chip
            wide = jnp.where(diagonal, mm(echo, spread_ref[core, pair]), 0.0)
            for part in range(2):
                rows = slice(part * NF, (part + 1) * NF)
                vector_ref[:, part, slot] = interleave(
                    wide[rows, :width], wide[rows, width:]
                ).astype(BF16)
    turn = (turns - rcv_index % turns) % turns
    owned = pltpu.roll(owned, turn * (2 * half), 1)
    return jnp.transpose(owned)[: 2 * half].reshape(2, half, NT)


def mute_kernel(
    index_ref, mine_ref, other_ref, forward_ref, inverse_ref, spread_ref, vector_ref, field_ref
):
    field_ref[...] = mute_half(
        index_ref, mine_ref, other_ref, forward_ref[...], inverse_ref[...], spread_ref, vector_ref
    )


def adjoint_kernel(
    index_ref, mine_ref, other_ref, forward_ref, inverse_ref, spread_ref,
    lower_ref, field_half_ref, first_ref, rest_ref, *refs
):
    keep_ref, far_ref, send_ref, field_ref, upper_ref = refs
    pairs = keep_ref.shape[0]
    receivers = first_ref.shape[-1] // 2
    width = lower_ref.shape[-1]
    half = width // GROUP
    field_ref[:, :half] = field_half_ref[...]
    field_ref[:, half:] = mute_half(
        index_ref, mine_ref, other_ref, forward_ref[...], inverse_ref[...], spread_ref, upper_ref
    )

    def one(group):
        rows = 2 * pairs * 2 * GROUP
        vector = jnp.concatenate(
            [ref[group].reshape(rows, width) for ref in (lower_ref, upper_ref)], axis=1
        )
        matrix = jnp.concatenate(
            [ref[group].reshape(width, 2 * receivers) for ref in (first_ref, rest_ref)], axis=0
        )
        full = mm(vector, matrix).reshape(2, pairs, 2, GROUP, 2 * receivers)
        re = full[0, ..., :receivers] + full[1, ..., receivers:]
        im = full[1, ..., :receivers] - full[0, ..., receivers:]
        return re, im

    for couple in range(NG // 2):
        even = one(2 * couple)
        odd = one(2 * couple + 1)
        for part in range(2):
            both = jnp.concatenate([even[part], odd[part]], axis=2).astype(BF16)
            row = part * NF + couple * 2 * GROUP
            keep_ref[:, row : row + 2 * GROUP, :] = both[:, 0]
            far_ref[row : row + 2 * GROUP, :] = both[pairs - 1, 1]
            send_ref[:, row : row + 2 * GROUP, :] = both[: pairs - 1, 1]


def downgoing_kernel(*refs):
    parts = refs[:-6]
    focal_ref, onset_ref, forward_ref, inverse_ref, field_ref, plus_ref = refs[-6:]
    total = parts[0][...].astype(F32)
    for part in parts[1:]:
        total = total + part[...].astype(F32)
    onset = onset_ref[...].astype(F32)
    signal = mute(mm(inverse_ref[...], total.astype(BF16)), onset)
    field = focal_ref[...].astype(F32) + jnp.transpose(signal)
    field_ref[0] = field
    spectra = mm(forward_ref[...], field.astype(BF16), NT_DIMS)
    plus_ref[...] = interleave(spectra[:NF], spectra[NF:]).astype(BF16)


def second_kernel(pairs, index_ref, *refs):
    near_refs, far_refs = refs[:pairs], refs[pairs : 2 * pairs]
    first_ref, rest_ref, gather_ref = refs[2 * pairs : 2 * pairs + 3]
    sum_refs = refs[2 * pairs + 3 : -2]
    vector_ref, kept_ref = refs[-2:]
    shot_index = index_ref[0]
    rcv_index = index_ref[1]
    core = shot_index % 2
    chip = shot_index // 2
    for distance in range(pairs):
        slot = (chip ^ distance) ^ rcv_index
        store_vector(vector_ref, 2 * slot + core, *unpack(near_refs[distance]))
        store_vector(vector_ref, 2 * slot + 1 - core, *unpack(far_refs[distance]))

    def store(row, value):
        for slot in range(pairs):
            sum_refs[slot][row : row + 2 * GROUP, :] = value[slot]

    apply_matrix([first_ref, rest_ref], vector_ref, kept_ref, gather_ref[...], store)


def final_kernel(*refs):
    parts = refs[:-3]
    onset_ref, inverse_ref, field_ref = refs[-3:]
    total = parts[0][...].astype(F32)
    for part in parts[1:]:
        total = total + part[...].astype(F32)
    spectra = split_halves(total, total).astype(BF16)
    onset = onset_ref[...].astype(F32)
    onset = jnp.concatenate([onset[0:1], onset[1:2]] * 2, axis=1)
    signal = mute(mm(inverse_ref[...], spectra), onset)
    field_ref[...] = jnp.transpose(signal)[: LANES // 2].reshape(field_ref.shape)


def emit_kernel(field_ref, out_ref):
    out_ref[...] = field_ref[...]


def vmem(count):
    return [pl.BlockSpec(memory_space=pltpu.VMEM) for _ in range(count)]


def smem():
    return [pl.BlockSpec(memory_space=pltpu.SMEM)]


def hbm(count):
    return [pl.BlockSpec(memory_space=pltpu.HBM) for _ in range(count)]


def call(kernel, name, out_shape, in_specs, scratch=(), work=1.0e9, out_specs=None):
    if out_specs is None:
        many = isinstance(out_shape, (tuple, list))
        out_specs = vmem(len(out_shape)) if many else vmem(1)[0]
    return pl.pallas_call(
        kernel,
        name=name,
        out_shape=out_shape,
        in_specs=in_specs,
        out_specs=out_specs,
        scratch_shapes=list(scratch),
        compiler_params=pltpu.CompilerParams(vmem_limit_bytes=40 << 20),
        cost_estimate=pl.CostEstimate(flops=int(work), bytes_accessed=1 << 20, transcendentals=0),
    )


def emit(field):
    return call(
        emit_kernel, "emit", jax.ShapeDtypeStruct(field.shape, field.dtype), vmem(1), work=0.3e9
    )(field)


def exchange(value, axis, distance):
    count = lax.axis_size(axis)
    return lax.ppermute(value, axis, [(place, place ^ distance) for place in range(count)])


def add_rounded(left, right):
    return (left.astype(F32) + right.astype(F32)).astype(BF16)


def body(traces, shift_index, deconv, focal_start, onset_source, onset_receiver):
    shot_count = lax.axis_size("shot")
    rcv_count = lax.axis_size("rcv")
    sources, receivers, _ = traces.shape
    focal_total = focal_start.shape[0]
    pairs = focal_total // 2
    assert onset_source.shape[0] == 2 and pairs == rcv_count
    assert focal_total == shot_count and 4 * sources == LANES and receivers == LANES
    gain = 1.0 / math.sqrt(NT * receivers * rcv_count)
    tables = make_tables(sources)
    index = jnp.stack([lax.axis_index("shot"), lax.axis_index("rcv")]).astype(jnp.int32)
    shape = jax.ShapeDtypeStruct
    half = sources // 2
    sets = focal_total // (LANES // half // 2)
    vector = shape((NG, focal_total, 2 * GROUP, 2 * receivers), BF16)
    half_matrix = shape((NG, half // 2, 2 * GROUP, 2 * receivers), BF16)
    half_sums = shape((sets * NF + 2 * GROUP, LANES), BF16)
    half_kept = pltpu.VMEM((NG * focal_total * 2 * GROUP, half * GROUP), BF16)
    half_delays = pltpu.VMEM((half // 2, 2 * NF, LANES), BF16)
    assert sets % 2 == 0 and rcv_count <= 2 * GROUP * (LANES // half // 2)

    def buffer(value):
        return pltpu.VMEM(value.shape, value.dtype)

    inputs = (
        traces, shift_index, deconv, focal_start, onset_source,
        tables["forward"], tables["taps"], tables["gather_half"],
    )
    small = (shift_index, deconv, onset_source) + inputs[5:]
    first, first_sum, focal_own, start, *loaded = call(
        functools.partial(first_kernel, gain),
        "first",
        [
            half_matrix,
            half_sums,
            shape((receivers, NT), BF16),
            vector,
        ]
        + [shape(value.shape, value.dtype) for value in small],
        smem() + hbm(len(inputs)),
        [
            half_kept,
            pltpu.VMEM((half, receivers, NT), BF16),
            buffer(focal_start),
            pltpu.SemaphoreType.DMA((2,)),
            pltpu.SemaphoreType.DMA((6,)),
            half_delays,
        ],
        work=4.0e9,
    )(index, *[pltpu.with_memory_space_constraint(value, pltpu.HBM) for value in inputs])
    forward = loaded[3]
    rest, rest_sum = call(
        functools.partial(rest_kernel, gain),
        "rest",
        (half_matrix, half_sums),
        smem() + vmem(8),
        [half_kept, half_delays],
        work=3.0e9,
    )(index, traces, *loaded, start)

    mine = [first_sum, rest_sum]
    other = [exchange(value, "rcv", 1) for value in mine]
    distance = 1
    while 2 * distance < rcv_count:
        distance *= 2
        mine = [add_rounded(left, right) for left, right in zip(mine, other)]
        other = [exchange(value, "rcv", distance) for value in mine]

    echo = shape((NG, 2, pairs, 2 * GROUP, half * GROUP), BF16)
    shared = (forward, tables["inverse"], tables["spread"])
    lower, field_half = call(
        mute_kernel,
        "mute",
        (echo, shape((2, half, NT), F32)),
        smem() + vmem(5),
        work=1.0e9,
    )(index, mine[0], other[0], *shared)

    keep, far, send, upgoing_first = call(
        adjoint_kernel,
        "adjoint",
        [
            shape((pairs, 2 * NF, receivers), BF16),
            shape((2 * NF, receivers), BF16),
            shape((pairs - 1, 2 * NF, receivers), BF16),
            shape((2, sources, NT), F32),
        ],
        smem() + vmem(9),
        [buffer(echo)],
        work=2.0e9,
    )(index, mine[1], other[1], *shared, lower, field_half, first, rest)

    far = exchange(far, "shot", 1)
    near = exchange(send, "shot", 1)
    parts = [exchange(add_rounded(keep[pairs - 1], far), "shot", 2 * (pairs - 1))]
    for distance in reversed(range(pairs - 1)):
        block = add_rounded(keep[distance], near[distance])
        parts.append(exchange(block, "shot", 2 * distance) if distance else block)

    downgoing, plus = call(
        downgoing_kernel,
        "downgoing",
        (
            shape((1, receivers, NT), F32),
            shape((NG, 2 * GROUP, receivers), BF16),
        ),
        vmem(pairs + 4),
    )(*parts, focal_own, onset_receiver, forward, tables["inverse"])

    near = [plus]
    for distance in range(1, pairs):
        near.append(exchange(plus, "shot", 2 * distance))
    far = [exchange(value, "shot", 1) for value in near]

    parts = call(
        functools.partial(second_kernel, pairs),
        "second",
        [shape((NF, LANES), BF16)] * pairs,
        smem() + vmem(2 * pairs + 3),
        [
            buffer(vector),
            pltpu.VMEM((NG * focal_total * 2 * GROUP, sources * GROUP), BF16),
        ],
    )(index, *near, *far, first, rest, tables["gather"])

    parts = [
        exchange(parts[distance], "rcv", distance) for distance in reversed(range(1, rcv_count))
    ] + [parts[0]]
    upgoing_second = call(
        final_kernel, "final", shape((2, sources, NT), F32), vmem(len(parts) + 2)
    )(*parts, loaded[2], tables["inverse"])
    return (emit(upgoing_first), emit(downgoing), upgoing_second)


def solution(mesh):
    placed = (
        P("shot", "rcv", None),
        P("shot", "rcv"),
        P("shot", None),
        P(None, "rcv", None),
        P("rcv", "shot"),
        P("shot", "rcv"),
    )
    return jax.shard_map(
        body,
        mesh=mesh,
        in_specs=placed,
        out_specs=(P("rcv", "shot", None), P("shot", "rcv", None), P("rcv", "shot", None)),
        check_vma=False,
    )
```

```python
import functools
import math

import jax
import jax.numpy as jnp
import numpy as np
from jax import lax
from jax.experimental import pallas as pl
from jax.experimental.pallas import tpu as pltpu
from jax.sharding import PartitionSpec as P

NT = 256
NF = 128
TAPS = 64
KSHIFT = 64
LANES = 128
GROUP = 8
NG = NF // GROUP

F32 = jnp.float32
BF16 = jnp.bfloat16
NN = (((1,), (0,)), ((), ()))
NT_DIMS = (((1,), (1,)), ((), ()))


def make_tables(source_local):
    sample = np.arange(NT)
    bins = np.arange(NF)
    angles = 2.0 * np.pi / NT * (bins[:, None] * sample[None, :] % NT)
    forward = np.concatenate([np.cos(angles), -np.sin(angles)], axis=0)
    weights = np.where(bins == 0, 1.0, 2.0) / NT
    inverse = (forward * np.concatenate([weights, weights])[:, None]).T
    tap = np.arange(TAPS, dtype=np.float64)
    fraction = np.arange(KSHIFT) * (TAPS / (4.0 * KSHIFT))
    offset = tap[None, :] - 0.375 * TAPS - fraction[:, None]
    window = 0.5 - 0.5 * np.cos(2.0 * np.pi * (tap + 0.5) / TAPS)
    tap_spec = forward[:, :TAPS] @ (np.sinc(offset) * window[None, :]).T
    return dict(
        forward=jnp.asarray(forward, F32).astype(BF16),
        inverse=jnp.asarray(inverse, F32).astype(BF16),
        taps=jnp.asarray(np.tile(tap_spec, (1, LANES // KSHIFT)), F32),
        gather=gather_table(source_local),
        gather_half=gather_table(source_local // 2),
        spread=spread_table(source_local // 2),
    )


def gather_table(sources):
    source_of = np.arange(sources * GROUP) // GROUP
    pick = source_of[:, None] == np.arange(sources)[None, :]
    return jnp.asarray(np.tile(pick, (1, LANES // sources)), F32).astype(BF16)


def spread_table(sources):
    pick = (np.arange(sources * GROUP)[None, :] // GROUP == np.arange(sources)[:, None]).astype(
        np.float32
    )
    blocks = LANES // sources
    table = np.zeros((2, blocks // 2, blocks, sources, 2, sources * GROUP), np.float32)
    for core in range(2):
        for pair in range(blocks // 2):
            table[core, pair, 2 * pair + core, :, 0] = pick
            table[core, pair, 2 * pair + 1 - core, :, 1] = pick
    table = table.reshape(2, blocks // 2, LANES, 2 * sources * GROUP)
    return jnp.asarray(table, F32).astype(BF16)


def mm(left, right, dims=NN):
    return lax.dot_general(left, right, dims, preferred_element_type=F32)


def interleave(first, second):
    width = first.shape[-1]
    pair = jnp.stack(
        [first.reshape(NG, GROUP, width), second.reshape(NG, GROUP, width)], axis=1
    )
    return pair.reshape(NG, 2 * GROUP, width)


def same_bin(rows, lanes):
    row = lax.broadcasted_iota(jnp.int32, (rows, lanes), 0)
    lane = lax.broadcasted_iota(jnp.int32, (rows, lanes), 1)
    return (row % GROUP) == (lane % GROUP)


def store_vector(vector_ref, place, re, im):
    receivers = re.shape[-1]
    vector_ref[:, place, :, :receivers] = interleave(re, im).astype(BF16)
    vector_ref[:, place, :, receivers:] = interleave(-im, re).astype(BF16)


def unpack(spectra_ref):
    receivers = spectra_ref.shape[-1]
    values = spectra_ref[...].astype(F32).reshape(NG, 2, GROUP, receivers)
    return values[:, 0].reshape(NF, receivers), values[:, 1].reshape(NF, receivers)


def apply_matrix(matrix_refs, vector_ref, kept_ref, gather, store):
    fields = vector_ref.shape[1]
    rows = fields * 2 * GROUP
    half = matrix_refs[0].shape[1] * matrix_refs[0].shape[2]
    width = half * len(matrix_refs)
    blocks = LANES // (width // GROUP)
    members = blocks // 2
    sets = fields // members
    diagonal = same_bin(rows, width)
    block_of = lax.broadcasted_iota(jnp.int32, (sets, GROUP, LANES), 2) // (LANES // blocks)

    for group in range(NG):
        vector = vector_ref[group].reshape(rows, vector_ref.shape[-1])
        matrix = [ref[group].reshape(half, ref.shape[-1]) for ref in matrix_refs]
        matrix = matrix[0] if len(matrix) == 1 else jnp.concatenate(matrix, axis=0)
        full = mm(vector, matrix, NT_DIMS)
        kept_ref[group * rows : (group + 1) * rows, :] = jnp.where(diagonal, full, 0.0).astype(BF16)

    for couple in range(NG // 2):
        kept = kept_ref[couple * 2 * rows : (couple + 1) * 2 * rows, :]
        spread = mm(kept, gather).reshape(2, sets, members, 2, GROUP, LANES)
        both = []
        for one in range(2):
            value = spread[one, :, 0, 0]
            for block in range(1, blocks):
                term = spread[one, :, block % members, block // members]
                value = jnp.where(block_of == block, term, value)
            both.append(value)
        store(couple * 2 * GROUP, jnp.concatenate(both, axis=1).astype(BF16))


def make_delays(first, count, forward_ref, deconv_ref, taps_ref, gain, delay_ref):
    deconv = deconv_ref[...]
    sources = deconv.shape[0]
    deconv_high = deconv.astype(BF16)
    deconv_low = (deconv - deconv_high.astype(F32)).astype(BF16)
    head = forward_ref[:, :TAPS]
    wave = (mm(head, deconv_high, NT_DIMS) + mm(head, deconv_low, NT_DIMS)) * gain
    wave_high = wave.astype(BF16)
    wave_low = (wave - wave_high.astype(F32)).astype(BF16)
    wave_both = jnp.concatenate([wave_high, wave_low], axis=1)
    taps = taps_ref[...]
    taps_re, taps_im = taps[:NF], taps[NF:]
    owner = lax.broadcasted_iota(jnp.int32, (2 * sources, 2 * LANES), 0) % sources
    place = lax.broadcasted_iota(jnp.int32, (2 * sources, 2 * LANES), 1) // KSHIFT
    for quad in range(count // 4):
        spread = mm(wave_both, (owner == place + (first + 4 * quad)).astype(F32).astype(BF16))
        for couple in range(2):
            lanes = slice(couple * LANES, (couple + 1) * LANES)
            wave_re, wave_im = spread[:NF, lanes], spread[NF:, lanes]
            delay_re = taps_re * wave_re - taps_im * wave_im
            delay_im = taps_re * wave_im + taps_im * wave_re
            delay_ref[2 * quad + couple] = jnp.concatenate([delay_re, delay_im], axis=0).astype(BF16)


def make_matrix(first, couple, forward, traces_ref, shift_ref, delay_ref, matrix_ref):
    receivers = shift_ref.shape[1]
    source = first + 2 * couple
    zeros = jnp.zeros((KSHIFT, receivers), F32)
    kinds = lax.broadcasted_iota(jnp.int32, (KSHIFT, receivers), 0)
    signals = traces_ref[2 * couple : 2 * couple + 2].reshape(2 * receivers, NT)
    raw = mm(forward, signals, NT_DIMS)
    hot = [
        (kinds == shift_ref[source + half : source + half + 1, :]).astype(F32)
        for half in range(2)
    ]
    hot = jnp.concatenate(
        [jnp.concatenate([hot[0], zeros], axis=1), jnp.concatenate([zeros, hot[1]], axis=1)],
        axis=0,
    ).astype(BF16)
    delay = mm(delay_ref[couple], hot)
    re = raw[:NF] * delay[:NF] - raw[NF:] * delay[NF:]
    im = raw[:NF] * delay[NF:] + raw[NF:] * delay[:NF]
    matrix_ref[:, couple, :, :receivers] = interleave(
        re[:, :receivers], re[:, receivers:]
    ).astype(BF16)
    matrix_ref[:, couple, :, receivers:] = interleave(
        im[:, :receivers], im[:, receivers:]
    ).astype(BF16)


def make_sums(first, rcv_index, matrix_ref, vector_ref, kept_ref, gather, onset_ref, sum_ref):
    half = 2 * matrix_ref.shape[1]
    sets = vector_ref.shape[1] // (LANES // half // 2)

    def store(row, value):
        for one in range(sets):
            sum_ref[one * NF + row : one * NF + row + 2 * GROUP, :] = value[one]

    apply_matrix([matrix_ref], vector_ref, kept_ref, gather, store)
    own = onset_ref[...].astype(F32)[:, first : first + half]
    turns = LANES // (2 * half)
    own = jnp.concatenate([own[0:1], own[1:2]] * turns, axis=1)
    own = jnp.broadcast_to(own, (2 * GROUP, LANES))
    row = lax.broadcasted_iota(jnp.int32, own.shape, 0)
    lane = lax.broadcasted_iota(jnp.int32, own.shape, 1)
    here = (row == rcv_index // turns) & (lane // (2 * half) == rcv_index % turns)
    sum_ref[sets * NF :, :] = jnp.where(here, own, 0.0).astype(BF16)


def first_kernel(
    gain, traces_hbm, shift_hbm, deconv_hbm, focal_hbm, onset_hbm,
    forward_hbm, taps_hbm, gather_hbm, matrix_ref, sum_ref, own_ref, vector_ref,
    shift_ref, deconv_ref, onset_ref, forward_ref, taps_ref, gather_ref,
    kept_ref, traces_ref, focal_ref, large_sem, small_sem, delay_ref,
):
    half = traces_ref.shape[0]
    fields = focal_ref.shape[0]
    small = [
        pltpu.make_async_copy(source, target, small_sem.at[place])
        for place, (source, target) in enumerate(
            [
                (forward_hbm, forward_ref),
                (deconv_hbm, deconv_ref),
                (taps_hbm, taps_ref),
                (shift_hbm, shift_ref),
                (gather_hbm, gather_ref),
                (onset_hbm, onset_ref),
            ]
        )
    ]
    large = [
        pltpu.make_async_copy(focal_hbm, focal_ref, large_sem.at[0]),
        pltpu.make_async_copy(traces_hbm.at[pl.ds(0, half)], traces_ref, large_sem.at[1]),
    ]
    for copy in small[:3] + large + small[3:]:
        copy.start()
    for copy in small[:3] + large[:1]:
        copy.wait()
    make_delays(0, half, forward_ref, deconv_ref, taps_ref, gain, delay_ref)
    forward = forward_ref[...]
    for place in range(fields):
        spectra = mm(forward, focal_ref[place], NT_DIMS)
        store_vector(vector_ref, place, spectra[:NF], spectra[NF:])
    own_ref[...] = focal_ref[lax.axis_index("shot")]
    for copy in small[3:] + large[1:]:
        copy.wait()
    for couple in range(half // 2):
        make_matrix(0, couple, forward, traces_ref, shift_ref, delay_ref, matrix_ref)
    make_sums(
        0, lax.axis_index("rcv"), matrix_ref, vector_ref, kept_ref, gather_ref[...], onset_ref, sum_ref
    )


def rest_kernel(
    gain, traces_ref, shift_ref, deconv_ref, onset_ref, forward_ref, taps_ref,
    gather_ref, vector_ref, matrix_ref, sum_ref, kept_ref, delay_ref,
):
    half = traces_ref.shape[0] // 2
    make_delays(half, half, forward_ref, deconv_ref, taps_ref, gain, delay_ref)
    forward = forward_ref[...]
    upper = traces_ref.at[pl.ds(half, half)]
    for couple in range(half // 2):
        make_matrix(half, couple, forward, upper, shift_ref, delay_ref, matrix_ref)
    make_sums(
        half, lax.axis_index("rcv"), matrix_ref, vector_ref, kept_ref, gather_ref[...], onset_ref, sum_ref
    )


def split_halves(first, second):
    lane = lax.broadcasted_iota(jnp.int32, first.shape, 1)
    low = lane < LANES // 2
    re = jnp.where(low, first, pltpu.roll(second, LANES // 2, 1))
    im = jnp.where(low, pltpu.roll(first, LANES // 2, 1), second)
    return jnp.concatenate([re, im], axis=0)


def mute(signal, onset):
    sample = lax.broadcasted_iota(jnp.int32, signal.shape, 0)
    folded = jnp.minimum(sample, NT - sample).astype(F32)
    return jnp.where(folded < onset, signal, 0.0)


def mute_half(mine_ref, other_ref, forward, inverse, spread_ref, vector_ref):
    shot_index = lax.axis_index("shot")
    rcv_index = lax.axis_index("rcv")
    core = shot_index % 2
    chip = shot_index // 2
    width = vector_ref.shape[-1]
    half = width // GROUP
    blocks = LANES // half
    sets = (mine_ref.shape[0] - 2 * GROUP) // NF
    turns = blocks // 2
    onsets = mine_ref[sets * NF :, :].astype(F32) + other_ref[sets * NF :, :].astype(F32)
    owned = jnp.zeros((NT, LANES), F32)
    diagonal = same_bin(2 * NF, 2 * width)
    for couple in range(sets // 2):
        rows = slice(2 * couple * NF, 2 * (couple + 1) * NF)
        total = mine_ref[rows, :].astype(F32) + other_ref[rows, :].astype(F32)
        spectra = split_halves(total[:NF], total[NF:]).astype(BF16)
        signal = mute(mm(inverse, spectra), onsets[couple : couple + 1, :])
        owned = jnp.where(rcv_index // turns == couple, signal, owned)
        echo = mm(forward, signal.astype(BF16)).astype(BF16)
        for pair in range(blocks // 2):
            slot = (couple * (blocks // 2) + pair) ^ chip
            wide = jnp.where(diagonal, mm(echo, spread_ref[core, pair]), 0.0)
            for part in range(2):
                rows = slice(part * NF, (part + 1) * NF)
                vector_ref[:, part, slot] = interleave(
                    wide[rows, :width], wide[rows, width:]
                ).astype(BF16)
    turn = (turns - rcv_index % turns) % turns
    owned = pltpu.roll(owned, turn * (2 * half), 1)
    return jnp.transpose(owned)[: 2 * half].reshape(2, half, NT)


def mute_kernel(
    mine_ref, other_ref, forward_ref, inverse_ref, spread_ref, vector_ref, field_ref
):
    field_ref[...] = mute_half(
        mine_ref, other_ref, forward_ref[...], inverse_ref[...], spread_ref, vector_ref
    )


def adjoint_kernel(
    mine_ref, other_ref, forward_ref, inverse_ref, spread_ref,
    lower_ref, field_half_ref, first_ref, rest_ref, *refs
):
    keep_ref, far_ref, send_ref, field_ref, upper_ref = refs
    pairs = keep_ref.shape[0]
    receivers = first_ref.shape[-1] // 2
    width = lower_ref.shape[-1]
    half = width // GROUP
    field_ref[:, :half] = field_half_ref[...]
    field_ref[:, half:] = mute_half(
        mine_ref, other_ref, forward_ref[...], inverse_ref[...], spread_ref, upper_ref
    )

    def one(group):
        rows = 2 * pairs * 2 * GROUP
        vector = jnp.concatenate(
            [ref[group].reshape(rows, width) for ref in (lower_ref, upper_ref)], axis=1
        )
        matrix = jnp.concatenate(
            [ref[group].reshape(width, 2 * receivers) for ref in (first_ref, rest_ref)], axis=0
        )
        full = mm(vector, matrix).reshape(2, pairs, 2, GROUP, 2 * receivers)
        re = full[0, ..., :receivers] + full[1, ..., receivers:]
        im = full[1, ..., :receivers] - full[0, ..., receivers:]
        return re, im

    for couple in range(NG // 2):
        even = one(2 * couple)
        odd = one(2 * couple + 1)
        for part in range(2):
            both = jnp.concatenate([even[part], odd[part]], axis=2).astype(BF16)
            row = part * NF + couple * 2 * GROUP
            keep_ref[:, row : row + 2 * GROUP, :] = both[:, 0]
            far_ref[row : row + 2 * GROUP, :] = both[pairs - 1, 1]
            send_ref[:, row : row + 2 * GROUP, :] = both[: pairs - 1, 1]


def downgoing_kernel(*refs):
    parts = refs[:-6]
    focal_ref, onset_ref, forward_ref, inverse_ref, field_ref, plus_ref = refs[-6:]
    total = parts[0][...].astype(F32)
    for part in parts[1:]:
        total = total + part[...].astype(F32)
    onset = onset_ref[...].astype(F32)
    signal = mute(mm(inverse_ref[...], total.astype(BF16)), onset)
    field = focal_ref[...].astype(F32) + jnp.transpose(signal)
    field_ref[0] = field
    spectra = mm(forward_ref[...], field.astype(BF16), NT_DIMS)
    plus_ref[...] = interleave(spectra[:NF], spectra[NF:]).astype(BF16)


def second_kernel(pairs, *refs):
    near_refs, far_refs = refs[:pairs], refs[pairs : 2 * pairs]
    first_ref, rest_ref, gather_ref = refs[2 * pairs : 2 * pairs + 3]
    sum_refs = refs[2 * pairs + 3 : -2]
    vector_ref, kept_ref = refs[-2:]
    shot_index = lax.axis_index("shot")
    rcv_index = lax.axis_index("rcv")
    core = shot_index % 2
    chip = shot_index // 2
    for distance in range(pairs):
        slot = (chip ^ distance) ^ rcv_index
        store_vector(vector_ref, 2 * slot + core, *unpack(near_refs[distance]))
        store_vector(vector_ref, 2 * slot + 1 - core, *unpack(far_refs[distance]))

    def store(row, value):
        for slot in range(pairs):
            sum_refs[slot][row : row + 2 * GROUP, :] = value[slot]

    apply_matrix([first_ref, rest_ref], vector_ref, kept_ref, gather_ref[...], store)


def final_kernel(*refs):
    parts = refs[:-3]
    onset_ref, inverse_ref, field_ref = refs[-3:]
    total = parts[0][...].astype(F32)
    for part in parts[1:]:
        total = total + part[...].astype(F32)
    spectra = split_halves(total, total).astype(BF16)
    onset = onset_ref[...].astype(F32)
    onset = jnp.concatenate([onset[0:1], onset[1:2]] * 2, axis=1)
    signal = mute(mm(inverse_ref[...], spectra), onset)
    field_ref[...] = jnp.transpose(signal)[: LANES // 2].reshape(field_ref.shape)


def emit_kernel(field_ref, out_ref):
    out_ref[...] = field_ref[...]


def vmem(count):
    return [pl.BlockSpec(memory_space=pltpu.VMEM) for _ in range(count)]


def hbm(count):
    return [pl.BlockSpec(memory_space=pltpu.HBM) for _ in range(count)]


def call(kernel, name, out_shape, in_specs, scratch=(), work=1.0e9, out_specs=None):
    if out_specs is None:
        many = isinstance(out_shape, (tuple, list))
        out_specs = vmem(len(out_shape)) if many else vmem(1)[0]
    return pl.pallas_call(
        kernel,
        name=name,
        out_shape=out_shape,
        in_specs=in_specs,
        out_specs=out_specs,
        scratch_shapes=list(scratch),
        compiler_params=pltpu.CompilerParams(vmem_limit_bytes=40 << 20),
        cost_estimate=pl.CostEstimate(flops=int(work), bytes_accessed=1 << 20, transcendentals=0),
    )


def emit(field):
    return call(
        emit_kernel, "emit", jax.ShapeDtypeStruct(field.shape, field.dtype), vmem(1), work=0.3e9
    )(field)


def exchange(value, axis, distance):
    count = lax.axis_size(axis)
    return lax.ppermute(value, axis, [(place, place ^ distance) for place in range(count)])


def add_rounded(left, right):
    return (left.astype(F32) + right.astype(F32)).astype(BF16)


def body(traces, shift_index, deconv, focal_start, onset_source, onset_receiver):
    shot_count = lax.axis_size("shot")
    rcv_count = lax.axis_size("rcv")
    sources, receivers, _ = traces.shape
    focal_total = focal_start.shape[0]
    pairs = focal_total // 2
    assert onset_source.shape[0] == 2 and pairs == rcv_count
    assert focal_total == shot_count and 4 * sources == LANES and receivers == LANES
    gain = 1.0 / math.sqrt(NT * receivers * rcv_count)
    tables = make_tables(sources)
    shape = jax.ShapeDtypeStruct
    half = sources // 2
    sets = focal_total // (LANES // half // 2)
    vector = shape((NG, focal_total, 2 * GROUP, 2 * receivers), BF16)
    half_matrix = shape((NG, half // 2, 2 * GROUP, 2 * receivers), BF16)
    half_sums = shape((sets * NF + 2 * GROUP, LANES), BF16)
    half_kept = pltpu.VMEM((NG * focal_total * 2 * GROUP, half * GROUP), BF16)
    half_delays = pltpu.VMEM((half // 2, 2 * NF, LANES), BF16)
    assert sets % 2 == 0 and rcv_count <= 2 * GROUP * (LANES // half // 2)

    def buffer(value):
        return pltpu.VMEM(value.shape, value.dtype)

    inputs = (
        traces, shift_index, deconv, focal_start, onset_source,
        tables["forward"], tables["taps"], tables["gather_half"],
    )
    small = (shift_index, deconv, onset_source) + inputs[5:]
    first, first_sum, focal_own, start, *loaded = call(
        functools.partial(first_kernel, gain),
        "first",
        [
            half_matrix,
            half_sums,
            shape((receivers, NT), BF16),
            vector,
        ]
        + [shape(value.shape, value.dtype) for value in small],
        hbm(len(inputs)),
        [
            half_kept,
            pltpu.VMEM((half, receivers, NT), BF16),
            buffer(focal_start),
            pltpu.SemaphoreType.DMA((2,)),
            pltpu.SemaphoreType.DMA((6,)),
            half_delays,
        ],
        work=4.0e9,
    )(*[pltpu.with_memory_space_constraint(value, pltpu.HBM) for value in inputs])
    forward = loaded[3]
    rest, rest_sum = call(
        functools.partial(rest_kernel, gain),
        "rest",
        (half_matrix, half_sums),
        vmem(8),
        [half_kept, half_delays],
        work=3.0e9,
    )(traces, *loaded, start)

    mine = [first_sum, rest_sum]
    other = [exchange(value, "rcv", 1) for value in mine]
    distance = 1
    while 2 * distance < rcv_count:
        distance *= 2
        mine = [add_rounded(left, right) for left, right in zip(mine, other)]
        other = [exchange(value, "rcv", distance) for value in mine]

    echo = shape((NG, 2, pairs, 2 * GROUP, half * GROUP), BF16)
    shared = (forward, tables["inverse"], tables["spread"])
    lower, field_half = call(
        mute_kernel,
        "mute",
        (echo, shape((2, half, NT), F32)),
        vmem(5),
        work=1.0e9,
    )(mine[0], other[0], *shared)

    keep, far, send, upgoing_first = call(
        adjoint_kernel,
        "adjoint",
        [
            shape((pairs, 2 * NF, receivers), BF16),
            shape((2 * NF, receivers), BF16),
            shape((pairs - 1, 2 * NF, receivers), BF16),
            shape((2, sources, NT), F32),
        ],
        vmem(9),
        [buffer(echo)],
        work=2.0e9,
    )(mine[1], other[1], *shared, lower, field_half, first, rest)

    far = exchange(far, "shot", 1)
    near = exchange(send, "shot", 1)
    parts = [exchange(add_rounded(keep[pairs - 1], far), "shot", 2 * (pairs - 1))]
    for distance in reversed(range(pairs - 1)):
        block = add_rounded(keep[distance], near[distance])
        parts.append(exchange(block, "shot", 2 * distance) if distance else block)

    downgoing, plus = call(
        downgoing_kernel,
        "downgoing",
        (
            shape((1, receivers, NT), F32),
            shape((NG, 2 * GROUP, receivers), BF16),
        ),
        vmem(pairs + 4),
    )(*parts, focal_own, onset_receiver, forward, tables["inverse"])

    near = [plus]
    for distance in range(1, pairs):
        near.append(exchange(plus, "shot", 2 * distance))
    far = [exchange(value, "shot", 1) for value in near]

    parts = call(
        functools.partial(second_kernel, pairs),
        "second",
        [shape((NF, LANES), BF16)] * pairs,
        vmem(2 * pairs + 3),
        [
            buffer(vector),
            pltpu.VMEM((NG * focal_total * 2 * GROUP, sources * GROUP), BF16),
        ],
    )(*near, *far, first, rest, tables["gather"])

    parts = [
        exchange(parts[distance], "rcv", distance) for distance in reversed(range(1, rcv_count))
    ] + [parts[0]]
    upgoing_second = call(
        final_kernel, "final", shape((2, sources, NT), F32), vmem(len(parts) + 2)
    )(*parts, loaded[2], tables["inverse"])
    return (emit(upgoing_first), emit(downgoing), upgoing_second)


def solution(mesh):
    placed = (
        P("shot", "rcv", None),
        P("shot", "rcv"),
        P("shot", None),
        P(None, "rcv", None),
        P("rcv", "shot"),
        P("shot", "rcv"),
    )
    return jax.shard_map(
        body,
        mesh=mesh,
        in_specs=placed,
        out_specs=(P("rcv", "shot", None), P("shot", "rcv", None), P("rcv", "shot", None)),
        check_vma=False,
    )
```

```python
import functools
import math

import jax
import jax.numpy as jnp
import numpy as np
from jax import lax
from jax.experimental import pallas as pl
from jax.experimental.pallas import tpu as pltpu
from jax.sharding import PartitionSpec as P

NT = 256
NF = 128
TAPS = 64
KSHIFT = 64
LANES = 128
GROUP = 8
NG = NF // GROUP

F32 = jnp.float32
BF16 = jnp.bfloat16
NN = (((1,), (0,)), ((), ()))
NT_DIMS = (((1,), (1,)), ((), ()))


def make_tables(source_local):
    sample = np.arange(NT)
    bins = np.arange(NF)
    angles = 2.0 * np.pi / NT * (bins[:, None] * sample[None, :] % NT)
    forward = np.concatenate([np.cos(angles), -np.sin(angles)], axis=0)
    weights = np.where(bins == 0, 1.0, 2.0) / NT
    inverse = (forward * np.concatenate([weights, weights])[:, None]).T
    tap = np.arange(TAPS, dtype=np.float64)
    fraction = np.arange(KSHIFT) * (TAPS / (4.0 * KSHIFT))
    offset = tap[None, :] - 0.375 * TAPS - fraction[:, None]
    window = 0.5 - 0.5 * np.cos(2.0 * np.pi * (tap + 0.5) / TAPS)
    tap_spec = forward[:, :TAPS] @ (np.sinc(offset) * window[None, :]).T
    return dict(
        forward=jnp.asarray(forward, F32).astype(BF16),
        inverse=jnp.asarray(inverse, F32).astype(BF16),
        taps=jnp.asarray(np.tile(tap_spec, (1, LANES // KSHIFT)), F32),
        gather=gather_table(source_local),
        gather_half=gather_table(source_local // 2),
        spread=spread_table(source_local // 2),
    )


def gather_table(sources):
    source_of = np.arange(sources * GROUP) // GROUP
    pick = source_of[:, None] == np.arange(sources)[None, :]
    return jnp.asarray(np.tile(pick, (1, LANES // sources)), F32).astype(BF16)


def spread_table(sources):
    pick = (np.arange(sources * GROUP)[None, :] // GROUP == np.arange(sources)[:, None]).astype(
        np.float32
    )
    blocks = LANES // sources
    table = np.zeros((2, blocks // 2, blocks, sources, 2, sources * GROUP), np.float32)
    for core in range(2):
        for pair in range(blocks // 2):
            table[core, pair, 2 * pair + core, :, 0] = pick
            table[core, pair, 2 * pair + 1 - core, :, 1] = pick
    table = table.reshape(2, blocks // 2, LANES, 2 * sources * GROUP)
    return jnp.asarray(table, F32).astype(BF16)


def mm(left, right, dims=NN):
    return lax.dot_general(left, right, dims, preferred_element_type=F32)


def interleave(first, second):
    width = first.shape[-1]
    pair = jnp.stack(
        [first.reshape(NG, GROUP, width), second.reshape(NG, GROUP, width)], axis=1
    )
    return pair.reshape(NG, 2 * GROUP, width)


def same_bin(rows, lanes):
    row = lax.broadcasted_iota(jnp.int32, (rows, lanes), 0)
    lane = lax.broadcasted_iota(jnp.int32, (rows, lanes), 1)
    return (row % GROUP) == (lane % GROUP)


def store_vector(vector_ref, place, re, im):
    receivers = re.shape[-1]
    vector_ref[:, place, :, :receivers] = interleave(re, im).astype(BF16)
    vector_ref[:, place, :, receivers:] = interleave(-im, re).astype(BF16)


def unpack(spectra_ref):
    receivers = spectra_ref.shape[-1]
    values = spectra_ref[...].astype(F32).reshape(NG, 2, GROUP, receivers)
    return values[:, 0].reshape(NF, receivers), values[:, 1].reshape(NF, receivers)


def apply_matrix(matrix_refs, vector_ref, kept_ref, gather, store):
    fields = vector_ref.shape[1]
    rows = fields * 2 * GROUP
    half = matrix_refs[0].shape[1] * matrix_refs[0].shape[2]
    width = half * len(matrix_refs)
    blocks = LANES // (width // GROUP)
    members = blocks // 2
    sets = fields // members
    diagonal = same_bin(rows, width)
    block_of = lax.broadcasted_iota(jnp.int32, (sets, GROUP, LANES), 2) // (LANES // blocks)

    for group in range(NG):
        vector = vector_ref[group].reshape(rows, vector_ref.shape[-1])
        matrix = [ref[group].reshape(half, ref.shape[-1]) for ref in matrix_refs]
        matrix = matrix[0] if len(matrix) == 1 else jnp.concatenate(matrix, axis=0)
        full = mm(vector, matrix, NT_DIMS)
        kept_ref[group * rows : (group + 1) * rows, :] = jnp.where(diagonal, full, 0.0).astype(BF16)

    for couple in range(NG // 2):
        kept = kept_ref[couple * 2 * rows : (couple + 1) * 2 * rows, :]
        spread = mm(kept, gather).reshape(2, sets, members, 2, GROUP, LANES)
        both = []
        for one in range(2):
            value = spread[one, :, 0, 0]
            for block in range(1, blocks):
                term = spread[one, :, block % members, block // members]
                value = jnp.where(block_of == block, term, value)
            both.append(value)
        store(couple * 2 * GROUP, jnp.concatenate(both, axis=1).astype(BF16))


def make_delays(first, count, forward_ref, deconv_ref, taps_ref, gain, delay_ref):
    deconv = deconv_ref[...]
    sources = deconv.shape[0]
    deconv_high = deconv.astype(BF16)
    deconv_low = (deconv - deconv_high.astype(F32)).astype(BF16)
    head = forward_ref[:, :TAPS]
    wave = (mm(head, deconv_high, NT_DIMS) + mm(head, deconv_low, NT_DIMS)) * gain
    wave_high = wave.astype(BF16)
    wave_low = (wave - wave_high.astype(F32)).astype(BF16)
    wave_both = jnp.concatenate([wave_high, wave_low], axis=1)
    taps = taps_ref[...]
    taps_re, taps_im = taps[:NF], taps[NF:]
    owner = lax.broadcasted_iota(jnp.int32, (2 * sources, 2 * LANES), 0) % sources
    place = lax.broadcasted_iota(jnp.int32, (2 * sources, 2 * LANES), 1) // KSHIFT
    for quad in range(count // 4):
        spread = mm(wave_both, (owner == place + (first + 4 * quad)).astype(F32).astype(BF16))
        for couple in range(2):
            lanes = slice(couple * LANES, (couple + 1) * LANES)
            wave_re, wave_im = spread[:NF, lanes], spread[NF:, lanes]
            delay_re = taps_re * wave_re - taps_im * wave_im
            delay_im = taps_re * wave_im + taps_im * wave_re
            delay_ref[2 * quad + couple] = jnp.concatenate([delay_re, delay_im], axis=0).astype(BF16)


def make_matrix(first, couple, forward, traces_ref, shift_ref, delay_ref, matrix_ref):
    receivers = shift_ref.shape[1]
    source = first + 2 * couple
    zeros = jnp.zeros((KSHIFT, receivers), F32)
    kinds = lax.broadcasted_iota(jnp.int32, (KSHIFT, receivers), 0)
    signals = traces_ref[2 * couple : 2 * couple + 2].reshape(2 * receivers, NT)
    raw = mm(forward, signals, NT_DIMS)
    hot = [
        (kinds == shift_ref[source + half : source + half + 1, :]).astype(F32)
        for half in range(2)
    ]
    hot = jnp.concatenate(
        [jnp.concatenate([hot[0], zeros], axis=1), jnp.concatenate([zeros, hot[1]], axis=1)],
        axis=0,
    ).astype(BF16)
    delay = mm(delay_ref[couple], hot)
    re = raw[:NF] * delay[:NF] - raw[NF:] * delay[NF:]
    im = raw[:NF] * delay[NF:] + raw[NF:] * delay[:NF]
    matrix_ref[:, couple, :, :receivers] = interleave(
        re[:, :receivers], re[:, receivers:]
    ).astype(BF16)
    matrix_ref[:, couple, :, receivers:] = interleave(
        im[:, :receivers], im[:, receivers:]
    ).astype(BF16)


def make_sums(first, rcv_index, matrix_ref, vector_ref, kept_ref, gather, onset_ref, sum_ref):
    half = 2 * matrix_ref.shape[1]
    sets = vector_ref.shape[1] // (LANES // half // 2)

    def store(row, value):
        for one in range(sets):
            sum_ref[one * NF + row : one * NF + row + 2 * GROUP, :] = value[one]

    apply_matrix([matrix_ref], vector_ref, kept_ref, gather, store)
    own = onset_ref[...].astype(F32)[:, first : first + half]
    turns = LANES // (2 * half)
    own = jnp.concatenate([own[0:1], own[1:2]] * turns, axis=1)
    own = jnp.broadcast_to(own, (2 * GROUP, LANES))
    row = lax.broadcasted_iota(jnp.int32, own.shape, 0)
    lane = lax.broadcasted_iota(jnp.int32, own.shape, 1)
    spare = (row == 0) & (lane >= LANES // 2)
    for one in range(sets):
        block = turns // 2 + (rcv_index - one * (turns // 2))
        here = (rcv_index // (turns // 2) == one) & (lane // (2 * half) == block)
        rows = slice(one * NF, one * NF + 2 * GROUP)
        value = sum_ref[rows, :].astype(F32)
        sum_ref[rows, :] = jnp.where(spare, jnp.where(here, own, 0.0), value).astype(BF16)


def first_kernel(
    gain, traces_hbm, shift_hbm, deconv_hbm, focal_hbm, onset_hbm,
    forward_hbm, taps_hbm, gather_hbm, matrix_ref, sum_ref, own_ref, vector_ref,
    shift_ref, deconv_ref, onset_ref, forward_ref, taps_ref, gather_ref,
    kept_ref, traces_ref, focal_ref, large_sem, small_sem, delay_ref,
):
    half = traces_ref.shape[0]
    fields = focal_ref.shape[0]
    small = [
        pltpu.make_async_copy(source, target, small_sem.at[place])
        for place, (source, target) in enumerate(
            [
                (forward_hbm, forward_ref),
                (deconv_hbm, deconv_ref),
                (taps_hbm, taps_ref),
                (shift_hbm, shift_ref),
                (gather_hbm, gather_ref),
                (onset_hbm, onset_ref),
            ]
        )
    ]
    large = [
        pltpu.make_async_copy(focal_hbm, focal_ref, large_sem.at[0]),
        pltpu.make_async_copy(traces_hbm.at[pl.ds(0, half)], traces_ref, large_sem.at[1]),
    ]
    for copy in small[:3] + large + small[3:]:
        copy.start()
    for copy in small[:3]:
        copy.wait()
    make_delays(0, half, forward_ref, deconv_ref, taps_ref, gain, delay_ref)
    forward = forward_ref[...]
    large[0].wait()
    for place in range(fields):
        spectra = mm(forward, focal_ref[place], NT_DIMS)
        store_vector(vector_ref, place, spectra[:NF], spectra[NF:])
    own_ref[...] = focal_ref[lax.axis_index("shot")]
    for copy in small[3:] + large[1:]:
        copy.wait()
    for couple in range(half // 2):
        make_matrix(0, couple, forward, traces_ref, shift_ref, delay_ref, matrix_ref)
    make_sums(
        0, lax.axis_index("rcv"), matrix_ref, vector_ref, kept_ref, gather_ref[...], onset_ref, sum_ref
    )


def rest_kernel(
    gain, traces_ref, shift_ref, deconv_ref, onset_ref, forward_ref, taps_ref,
    gather_ref, vector_ref, matrix_ref, sum_ref, kept_ref, delay_ref,
):
    half = traces_ref.shape[0] // 2
    make_delays(half, half, forward_ref, deconv_ref, taps_ref, gain, delay_ref)
    forward = forward_ref[...]
    upper = traces_ref.at[pl.ds(half, half)]
    for couple in range(half // 2):
        make_matrix(half, couple, forward, upper, shift_ref, delay_ref, matrix_ref)
    make_sums(
        half, lax.axis_index("rcv"), matrix_ref, vector_ref, kept_ref, gather_ref[...], onset_ref, sum_ref
    )


def split_halves(first, second):
    lane = lax.broadcasted_iota(jnp.int32, first.shape, 1)
    low = lane < LANES // 2
    re = jnp.where(low, first, pltpu.roll(second, LANES // 2, 1))
    im = jnp.where(low, pltpu.roll(first, LANES // 2, 1), second)
    return jnp.concatenate([re, im], axis=0)


def mute(signal, onset):
    sample = lax.broadcasted_iota(jnp.int32, signal.shape, 0)
    folded = jnp.minimum(sample, NT - sample).astype(F32)
    return jnp.where(folded < onset, signal, 0.0)


def mute_half(mine_ref, other_ref, forward, inverse, spread_ref, vector_ref):
    shot_index = lax.axis_index("shot")
    rcv_index = lax.axis_index("rcv")
    core = shot_index % 2
    chip = shot_index // 2
    width = vector_ref.shape[-1]
    half = width // GROUP
    blocks = LANES // half
    sets = mine_ref.shape[0] // NF
    turns = blocks // 2
    owned = jnp.zeros((NT, LANES), F32)
    diagonal = same_bin(2 * NF, 2 * width)
    for couple in range(sets // 2):
        rows = slice(2 * couple * NF, 2 * (couple + 1) * NF)
        total = mine_ref[rows, :].astype(F32) + other_ref[rows, :].astype(F32)
        spectra = split_halves(total[:NF], total[NF:])
        signal = mute(mm(inverse, spectra.astype(BF16)), spectra[NF : NF + 1, :])
        owned = jnp.where(rcv_index // turns == couple, signal, owned)
        echo = mm(forward, signal.astype(BF16)).astype(BF16)
        for pair in range(blocks // 2):
            slot = (couple * (blocks // 2) + pair) ^ chip
            wide = jnp.where(diagonal, mm(echo, spread_ref[core, pair]), 0.0)
            for part in range(2):
                rows = slice(part * NF, (part + 1) * NF)
                vector_ref[:, part, slot] = interleave(
                    wide[rows, :width], wide[rows, width:]
                ).astype(BF16)
    turn = (turns - rcv_index % turns) % turns
    owned = pltpu.roll(owned, turn * (2 * half), 1)
    return jnp.transpose(owned)[: 2 * half].reshape(2, half, NT)


def mute_kernel(
    mine_ref, other_ref, forward_ref, inverse_ref, spread_ref, vector_ref, field_ref
):
    field_ref[...] = mute_half(
        mine_ref, other_ref, forward_ref[...], inverse_ref[...], spread_ref, vector_ref
    )


def adjoint_kernel(
    mine_ref, other_ref, forward_ref, inverse_ref, spread_ref,
    lower_ref, field_half_ref, first_ref, rest_ref, *refs
):
    keep_ref, far_ref, send_ref, field_ref, upper_ref = refs
    pairs = keep_ref.shape[0]
    receivers = first_ref.shape[-1] // 2
    width = lower_ref.shape[-1]
    half = width // GROUP
    field_ref[:, :half] = field_half_ref[...]
    field_ref[:, half:] = mute_half(
        mine_ref, other_ref, forward_ref[...], inverse_ref[...], spread_ref, upper_ref
    )

    def one(group):
        rows = 2 * pairs * 2 * GROUP
        vector = jnp.concatenate(
            [ref[group].reshape(rows, width) for ref in (lower_ref, upper_ref)], axis=1
        )
        matrix = jnp.concatenate(
            [ref[group].reshape(width, 2 * receivers) for ref in (first_ref, rest_ref)], axis=0
        )
        full = mm(vector, matrix).reshape(2, pairs, 2, GROUP, 2 * receivers)
        re = full[0, ..., :receivers] + full[1, ..., receivers:]
        im = full[1, ..., :receivers] - full[0, ..., receivers:]
        return re, im

    for couple in range(NG // 2):
        even = one(2 * couple)
        odd = one(2 * couple + 1)
        for part in range(2):
            both = jnp.concatenate([even[part], odd[part]], axis=2).astype(BF16)
            row = part * NF + couple * 2 * GROUP
            keep_ref[:, row : row + 2 * GROUP, :] = both[:, 0]
            far_ref[row : row + 2 * GROUP, :] = both[pairs - 1, 1]
            send_ref[:, row : row + 2 * GROUP, :] = both[: pairs - 1, 1]


def downgoing_kernel(*refs):
    parts = refs[:-6]
    focal_ref, onset_ref, forward_ref, inverse_ref, field_ref, plus_ref = refs[-6:]
    total = parts[0][...].astype(F32)
    for part in parts[1:]:
        total = total + part[...].astype(F32)
    onset = onset_ref[...].astype(F32)
    signal = mute(mm(inverse_ref[...], total.astype(BF16)), onset)
    field = focal_ref[...].astype(F32) + jnp.transpose(signal)
    field_ref[0] = field
    spectra = mm(forward_ref[...], field.astype(BF16), NT_DIMS)
    plus_ref[...] = interleave(spectra[:NF], spectra[NF:]).astype(BF16)


def second_kernel(pairs, *refs):
    near_refs, far_refs = refs[:pairs], refs[pairs : 2 * pairs]
    first_ref, rest_ref, gather_ref = refs[2 * pairs : 2 * pairs + 3]
    sum_refs = refs[2 * pairs + 3 : -2]
    vector_ref, kept_ref = refs[-2:]
    shot_index = lax.axis_index("shot")
    rcv_index = lax.axis_index("rcv")
    core = shot_index % 2
    chip = shot_index // 2
    for distance in range(pairs):
        slot = (chip ^ distance) ^ rcv_index
        store_vector(vector_ref, 2 * slot + core, *unpack(near_refs[distance]))
        store_vector(vector_ref, 2 * slot + 1 - core, *unpack(far_refs[distance]))

    def store(row, value):
        for slot in range(pairs):
            sum_refs[slot][row : row + 2 * GROUP, :] = value[slot]

    apply_matrix([first_ref, rest_ref], vector_ref, kept_ref, gather_ref[...], store)


def final_kernel(*refs):
    parts = refs[:-3]
    onset_ref, inverse_ref, field_ref = refs[-3:]
    total = parts[0][...].astype(F32)
    for part in parts[1:]:
        total = total + part[...].astype(F32)
    spectra = split_halves(total, total).astype(BF16)
    onset = onset_ref[...].astype(F32)
    onset = jnp.concatenate([onset[0:1], onset[1:2]] * 2, axis=1)
    signal = mute(mm(inverse_ref[...], spectra), onset)
    field_ref[...] = jnp.transpose(signal)[: LANES // 2].reshape(field_ref.shape)


def emit_kernel(field_ref, out_ref):
    out_ref[...] = field_ref[...]


def vmem(count):
    return [pl.BlockSpec(memory_space=pltpu.VMEM) for _ in range(count)]


def hbm(count):
    return [pl.BlockSpec(memory_space=pltpu.HBM) for _ in range(count)]


def call(kernel, name, out_shape, in_specs, scratch=(), work=1.0e9, out_specs=None):
    if out_specs is None:
        many = isinstance(out_shape, (tuple, list))
        out_specs = vmem(len(out_shape)) if many else vmem(1)[0]
    return pl.pallas_call(
        kernel,
        name=name,
        out_shape=out_shape,
        in_specs=in_specs,
        out_specs=out_specs,
        scratch_shapes=list(scratch),
        compiler_params=pltpu.CompilerParams(vmem_limit_bytes=40 << 20),
        cost_estimate=pl.CostEstimate(flops=int(work), bytes_accessed=1 << 20, transcendentals=0),
    )


def emit(field):
    return call(
        emit_kernel, "emit", jax.ShapeDtypeStruct(field.shape, field.dtype), vmem(1), work=0.3e9
    )(field)


def exchange(value, axis, distance):
    count = lax.axis_size(axis)
    return lax.ppermute(value, axis, [(place, place ^ distance) for place in range(count)])


def add_rounded(left, right):
    return (left.astype(F32) + right.astype(F32)).astype(BF16)


def body(traces, shift_index, deconv, focal_start, onset_source, onset_receiver):
    shot_count = lax.axis_size("shot")
    rcv_count = lax.axis_size("rcv")
    sources, receivers, _ = traces.shape
    focal_total = focal_start.shape[0]
    pairs = focal_total // 2
    assert onset_source.shape[0] == 2 and pairs == rcv_count
    assert focal_total == shot_count and 4 * sources == LANES and receivers == LANES
    gain = 1.0 / math.sqrt(NT * receivers * rcv_count)
    tables = make_tables(sources)
    shape = jax.ShapeDtypeStruct
    half = sources // 2
    sets = focal_total // (LANES // half // 2)
    vector = shape((NG, focal_total, 2 * GROUP, 2 * receivers), BF16)
    half_matrix = shape((NG, half // 2, 2 * GROUP, 2 * receivers), BF16)
    half_sums = shape((sets * NF, LANES), BF16)
    half_kept = pltpu.VMEM((NG * focal_total * 2 * GROUP, half * GROUP), BF16)
    half_delays = pltpu.VMEM((half // 2, 2 * NF, LANES), BF16)
    assert sets % 2 == 0 and half * 8 == LANES

    def buffer(value):
        return pltpu.VMEM(value.shape, value.dtype)

    inputs = (
        traces, shift_index, deconv, focal_start, onset_source,
        tables["forward"], tables["taps"], tables["gather_half"],
    )
    small = (shift_index, deconv, onset_source) + inputs[5:]
    first, first_sum, focal_own, start, *loaded = call(
        functools.partial(first_kernel, gain),
        "first",
        [
            half_matrix,
            half_sums,
            shape((receivers, NT), BF16),
            vector,
        ]
        + [shape(value.shape, value.dtype) for value in small],
        hbm(len(inputs)),
        [
            half_kept,
            pltpu.VMEM((half, receivers, NT), BF16),
            buffer(focal_start),
            pltpu.SemaphoreType.DMA((2,)),
            pltpu.SemaphoreType.DMA((6,)),
            half_delays,
        ],
        work=4.0e9,
    )(*[pltpu.with_memory_space_constraint(value, pltpu.HBM) for value in inputs])
    forward = loaded[3]
    rest, rest_sum = call(
        functools.partial(rest_kernel, gain),
        "rest",
        (half_matrix, half_sums),
        vmem(8),
        [half_kept, half_delays],
        work=3.0e9,
    )(traces, *loaded, start)

    mine = [first_sum, rest_sum]
    other = [exchange(value, "rcv", 1) for value in mine]
    distance = 1
    while 2 * distance < rcv_count:
        distance *= 2
        mine = [add_rounded(left, right) for left, right in zip(mine, other)]
        other = [exchange(value, "rcv", distance) for value in mine]

    echo = shape((NG, 2, pairs, 2 * GROUP, half * GROUP), BF16)
    shared = (forward, tables["inverse"], tables["spread"])
    lower, field_half = call(
        mute_kernel,
        "mute",
        (echo, shape((2, half, NT), F32)),
        vmem(5),
        work=1.0e9,
    )(mine[0], other[0], *shared)

    keep, far, send, upgoing_first = call(
        adjoint_kernel,
        "adjoint",
        [
            shape((pairs, 2 * NF, receivers), BF16),
            shape((2 * NF, receivers), BF16),
            shape((pairs - 1, 2 * NF, receivers), BF16),
            shape((2, sources, NT), F32),
        ],
        vmem(9),
        [buffer(echo)],
        work=2.0e9,
    )(mine[1], other[1], *shared, lower, field_half, first, rest)

    far = exchange(far, "shot", 1)
    near = exchange(send, "shot", 1)
    parts = [exchange(add_rounded(keep[pairs - 1], far), "shot", 2 * (pairs - 1))]
    for distance in reversed(range(pairs - 1)):
        block = add_rounded(keep[distance], near[distance])
        parts.append(exchange(block, "shot", 2 * distance) if distance else block)

    downgoing, plus = call(
        downgoing_kernel,
        "downgoing",
        (
            shape((1, receivers, NT), F32),
            shape((NG, 2 * GROUP, receivers), BF16),
        ),
        vmem(pairs + 4),
    )(*parts, focal_own, onset_receiver, forward, tables["inverse"])

    near = [plus]
    for distance in range(1, pairs):
        near.append(exchange(plus, "shot", 2 * distance))
    far = [exchange(value, "shot", 1) for value in near]

    parts = call(
        functools.partial(second_kernel, pairs),
        "second",
        [shape((NF, LANES), BF16)] * pairs,
        vmem(2 * pairs + 3),
        [
            buffer(vector),
            pltpu.VMEM((NG * focal_total * 2 * GROUP, sources * GROUP), BF16),
        ],
    )(*near, *far, first, rest, tables["gather"])

    parts = [
        exchange(parts[distance], "rcv", distance) for distance in reversed(range(1, rcv_count))
    ] + [parts[0]]
    upgoing_second = call(
        final_kernel, "final", shape((2, sources, NT), F32), vmem(len(parts) + 2)
    )(*parts, loaded[2], tables["inverse"])
    return (emit(upgoing_first), emit(downgoing), upgoing_second)


def solution(mesh):
    placed = (
        P("shot", "rcv", None),
        P("shot", "rcv"),
        P("shot", None),
        P(None, "rcv", None),
        P("rcv", "shot"),
        P("shot", "rcv"),
    )
    return jax.shard_map(
        body,
        mesh=mesh,
        in_specs=placed,
        out_specs=(P("rcv", "shot", None), P("shot", "rcv", None), P("rcv", "shot", None)),
        check_vma=False,
    )
```

```python
import functools
import math

import jax
import jax.numpy as jnp
import numpy as np
from jax import lax
from jax.experimental import pallas as pl
from jax.experimental.pallas import tpu as pltpu
from jax.sharding import PartitionSpec as P

NT = 256
NF = 128
TAPS = 64
KSHIFT = 64
LANES = 128
GROUP = 8
NG = NF // GROUP

F32 = jnp.float32
BF16 = jnp.bfloat16
NN = (((1,), (0,)), ((), ()))
NT_DIMS = (((1,), (1,)), ((), ()))


def make_tables(source_local):
    sample = np.arange(NT)
    bins = np.arange(NF)
    angles = 2.0 * np.pi / NT * (bins[:, None] * sample[None, :] % NT)
    forward = np.concatenate([np.cos(angles), -np.sin(angles)], axis=0)
    weights = np.where(bins == 0, 1.0, 2.0) / NT
    inverse = (forward * np.concatenate([weights, weights])[:, None]).T
    tap = np.arange(TAPS, dtype=np.float64)
    fraction = np.arange(KSHIFT) * (TAPS / (4.0 * KSHIFT))
    offset = tap[None, :] - 0.375 * TAPS - fraction[:, None]
    window = 0.5 - 0.5 * np.cos(2.0 * np.pi * (tap + 0.5) / TAPS)
    tap_spec = forward[:, :TAPS] @ (np.sinc(offset) * window[None, :]).T
    return dict(
        forward=jnp.asarray(forward, F32).astype(BF16),
        inverse=jnp.asarray(inverse, F32).astype(BF16),
        taps=jnp.asarray(np.tile(tap_spec, (1, LANES // KSHIFT)), F32),
        gather=gather_table(source_local),
        gather_half=gather_table(source_local // 2, 2),
        spread=spread_table(source_local // 2),
    )


def gather_table(sources, count=1):
    source_of = np.arange(sources * GROUP) // GROUP
    pick = source_of[:, None] == np.arange(sources)[None, :]
    table = np.kron(np.eye(count), np.tile(pick, (1, LANES // sources)))
    return jnp.asarray(table, F32).astype(BF16)


def spread_table(sources):
    pick = (np.arange(sources * GROUP)[None, :] // GROUP == np.arange(sources)[:, None]).astype(
        np.float32
    )
    blocks = LANES // sources
    table = np.zeros((2, blocks // 2, blocks, sources, 2, sources * GROUP), np.float32)
    for core in range(2):
        for pair in range(blocks // 2):
            table[core, pair, 2 * pair + core, :, 0] = pick
            table[core, pair, 2 * pair + 1 - core, :, 1] = pick
    table = table.reshape(2, blocks // 2, LANES, 2 * sources * GROUP)
    return jnp.asarray(table, F32).astype(BF16)


def mm(left, right, dims=NN):
    return lax.dot_general(left, right, dims, preferred_element_type=F32)


def interleave(first, second):
    width = first.shape[-1]
    pair = jnp.stack(
        [first.reshape(NG, GROUP, width), second.reshape(NG, GROUP, width)], axis=1
    )
    return pair.reshape(NG, 2 * GROUP, width)


def same_bin(rows, lanes):
    row = lax.broadcasted_iota(jnp.int32, (rows, lanes), 0)
    lane = lax.broadcasted_iota(jnp.int32, (rows, lanes), 1)
    return (row % GROUP) == (lane % GROUP)


def store_vector(vector_ref, place, re, im):
    receivers = re.shape[-1]
    vector_ref[:, place, :, :receivers] = interleave(re, im).astype(BF16)
    vector_ref[:, place, :, receivers:] = interleave(-im, re).astype(BF16)


def unpack(spectra_ref):
    receivers = spectra_ref.shape[-1]
    values = spectra_ref[...].astype(F32).reshape(NG, 2, GROUP, receivers)
    return values[:, 0].reshape(NF, receivers), values[:, 1].reshape(NF, receivers)


def apply_matrix(matrix_refs, vector_ref, kept_ref, gather, store):
    fields = vector_ref.shape[1]
    rows = fields * 2 * GROUP
    half = matrix_refs[0].shape[1] * matrix_refs[0].shape[2]
    width = half * len(matrix_refs)
    blocks = LANES // (width // GROUP)
    members = blocks // 2
    sets = fields // members
    diagonal = same_bin(rows, width)
    block_of = lax.broadcasted_iota(jnp.int32, (sets, GROUP, LANES), 2) // (LANES // blocks)

    span = kept_ref.shape[1] // width

    for group in range(NG):
        vector = vector_ref[group].reshape(rows, vector_ref.shape[-1])
        matrix = [ref[group].reshape(half, ref.shape[-1]) for ref in matrix_refs]
        matrix = matrix[0] if len(matrix) == 1 else jnp.concatenate(matrix, axis=0)
        full = mm(vector, matrix, NT_DIMS)
        place, lane = group // span * rows, group % span * width
        kept_ref[place : place + rows, lane : lane + width] = jnp.where(
            diagonal, full, 0.0
        ).astype(BF16)

    for couple in range(NG // 2):
        count = 2 // span * rows
        spread = mm(kept_ref[couple * count : (couple + 1) * count, :], gather)
        both = []
        for one in range(2):
            place, lane = one // span * rows, one % span * LANES
            part = spread[place : place + rows, lane : lane + LANES]
            part = part.reshape(sets, members, 2, GROUP, LANES)
            value = part[:, 0, 0]
            for block in range(1, blocks):
                value = jnp.where(block_of == block, part[:, block % members, block // members], value)
            both.append(value)
        store(couple * 2 * GROUP, jnp.concatenate(both, axis=1).astype(BF16))


def make_delays(first, count, forward_ref, deconv_ref, taps_ref, gain, delay_ref):
    deconv = deconv_ref[...]
    sources = deconv.shape[0]
    deconv_high = deconv.astype(BF16)
    deconv_low = (deconv - deconv_high.astype(F32)).astype(BF16)
    head = forward_ref[:, :TAPS]
    wave = (mm(head, deconv_high, NT_DIMS) + mm(head, deconv_low, NT_DIMS)) * gain
    wave_high = wave.astype(BF16)
    wave_low = (wave - wave_high.astype(F32)).astype(BF16)
    wave_both = jnp.concatenate([wave_high, wave_low], axis=1)
    taps = taps_ref[...]
    taps_re, taps_im = taps[:NF], taps[NF:]
    owner = lax.broadcasted_iota(jnp.int32, (2 * sources, 2 * LANES), 0) % sources
    place = lax.broadcasted_iota(jnp.int32, (2 * sources, 2 * LANES), 1) // KSHIFT
    for quad in range(count // 4):
        spread = mm(wave_both, (owner == place + (first + 4 * quad)).astype(F32).astype(BF16))
        for couple in range(2):
            lanes = slice(couple * LANES, (couple + 1) * LANES)
            wave_re, wave_im = spread[:NF, lanes], spread[NF:, lanes]
            delay_re = taps_re * wave_re - taps_im * wave_im
            delay_im = taps_re * wave_im + taps_im * wave_re
            delay_ref[2 * quad + couple] = jnp.concatenate([delay_re, delay_im], axis=0).astype(BF16)


def make_matrix(first, couple, forward, traces_ref, shift_ref, delay_ref, matrix_ref):
    receivers = shift_ref.shape[1]
    source = first + 2 * couple
    zeros = jnp.zeros((KSHIFT, receivers), F32)
    kinds = lax.broadcasted_iota(jnp.int32, (KSHIFT, receivers), 0)
    signals = traces_ref[2 * couple : 2 * couple + 2].reshape(2 * receivers, NT)
    raw = mm(forward, signals, NT_DIMS)
    hot = [
        (kinds == shift_ref[source + half : source + half + 1, :]).astype(F32)
        for half in range(2)
    ]
    hot = jnp.concatenate(
        [jnp.concatenate([hot[0], zeros], axis=1), jnp.concatenate([zeros, hot[1]], axis=1)],
        axis=0,
    ).astype(BF16)
    delay = mm(delay_ref[couple], hot)
    re = raw[:NF] * delay[:NF] - raw[NF:] * delay[NF:]
    im = raw[:NF] * delay[NF:] + raw[NF:] * delay[:NF]
    matrix_ref[:, couple, :, :receivers] = interleave(
        re[:, :receivers], re[:, receivers:]
    ).astype(BF16)
    matrix_ref[:, couple, :, receivers:] = interleave(
        im[:, :receivers], im[:, receivers:]
    ).astype(BF16)


def make_sums(first, rcv_index, matrix_ref, vector_ref, kept_ref, gather, onset_ref, sum_ref):
    half = 2 * matrix_ref.shape[1]
    sets = vector_ref.shape[1] // (LANES // half // 2)

    def store(row, value):
        for one in range(sets):
            sum_ref[one * NF + row : one * NF + row + 2 * GROUP, :] = value[one]

    apply_matrix([matrix_ref], vector_ref, kept_ref, gather, store)
    own = onset_ref[...].astype(F32)[:, first : first + half]
    turns = LANES // (2 * half)
    own = jnp.concatenate([own[0:1], own[1:2]] * turns, axis=1)
    own = jnp.broadcast_to(own, (2 * GROUP, LANES))
    row = lax.broadcasted_iota(jnp.int32, own.shape, 0)
    lane = lax.broadcasted_iota(jnp.int32, own.shape, 1)
    spare = (row == 0) & (lane >= LANES // 2)
    for one in range(sets):
        block = turns // 2 + (rcv_index - one * (turns // 2))
        here = (rcv_index // (turns // 2) == one) & (lane // (2 * half) == block)
        rows = slice(one * NF, one * NF + 2 * GROUP)
        value = sum_ref[rows, :].astype(F32)
        sum_ref[rows, :] = jnp.where(spare, jnp.where(here, own, 0.0), value).astype(BF16)


def first_kernel(
    gain, traces_hbm, shift_hbm, deconv_hbm, focal_hbm, onset_hbm,
    forward_hbm, taps_hbm, gather_hbm, matrix_ref, sum_ref, own_ref, vector_ref,
    shift_ref, deconv_ref, onset_ref, forward_ref, taps_ref, gather_ref,
    kept_ref, traces_ref, focal_ref, large_sem, small_sem, delay_ref,
):
    half = traces_ref.shape[0]
    fields = focal_ref.shape[0]
    small = [
        pltpu.make_async_copy(source, target, small_sem.at[place])
        for place, (source, target) in enumerate(
            [
                (forward_hbm, forward_ref),
                (deconv_hbm, deconv_ref),
                (taps_hbm, taps_ref),
                (shift_hbm, shift_ref),
                (gather_hbm, gather_ref),
                (onset_hbm, onset_ref),
            ]
        )
    ]
    large = [
        pltpu.make_async_copy(focal_hbm, focal_ref, large_sem.at[0]),
        pltpu.make_async_copy(traces_hbm.at[pl.ds(0, half)], traces_ref, large_sem.at[1]),
    ]
    for copy in small[:3] + large + small[3:]:
        copy.start()
    for copy in small[:3]:
        copy.wait()
    make_delays(0, half, forward_ref, deconv_ref, taps_ref, gain, delay_ref)
    forward = forward_ref[...]
    large[0].wait()
    for place in range(0, fields, 2):
        signals = focal_ref[place : place + 2].reshape(-1, NT)
        receivers = signals.shape[0] // 2
        spectra = mm(forward, signals, NT_DIMS)
        for one in range(2):
            field = spectra[:, one * receivers : (one + 1) * receivers]
            store_vector(vector_ref, place + one, field[:NF], field[NF:])
    own_ref[...] = focal_ref[lax.axis_index("shot")]
    for copy in small[3:] + large[1:]:
        copy.wait()
    for couple in range(half // 2):
        make_matrix(0, couple, forward, traces_ref, shift_ref, delay_ref, matrix_ref)
    make_sums(
        0, lax.axis_index("rcv"), matrix_ref, vector_ref, kept_ref, gather_ref[...], onset_ref, sum_ref
    )


def rest_kernel(
    gain, traces_ref, shift_ref, deconv_ref, onset_ref, forward_ref, taps_ref,
    gather_ref, vector_ref, matrix_ref, sum_ref, kept_ref, delay_ref,
):
    half = traces_ref.shape[0] // 2
    make_delays(half, half, forward_ref, deconv_ref, taps_ref, gain, delay_ref)
    forward = forward_ref[...]
    upper = traces_ref.at[pl.ds(half, half)]
    for couple in range(half // 2):
        make_matrix(half, couple, forward, upper, shift_ref, delay_ref, matrix_ref)
    make_sums(
        half, lax.axis_index("rcv"), matrix_ref, vector_ref, kept_ref, gather_ref[...], onset_ref, sum_ref
    )


def split_halves(first, second):
    lane = lax.broadcasted_iota(jnp.int32, first.shape, 1)
    low = lane < LANES // 2
    re = jnp.where(low, first, pltpu.roll(second, LANES // 2, 1))
    im = jnp.where(low, pltpu.roll(first, LANES // 2, 1), second)
    return jnp.concatenate([re, im], axis=0)


def mute(signal, onset):
    sample = lax.broadcasted_iota(jnp.int32, signal.shape, 0)
    folded = jnp.minimum(sample, NT - sample).astype(F32)
    return jnp.where(folded < onset, signal, 0.0)


def mute_half(mine_ref, other_ref, forward, inverse, spread_ref, vector_ref):
    shot_index = lax.axis_index("shot")
    rcv_index = lax.axis_index("rcv")
    core = shot_index % 2
    chip = shot_index // 2
    width = vector_ref.shape[-1]
    half = width // GROUP
    blocks = LANES // half
    sets = mine_ref.shape[0] // NF
    turns = blocks // 2
    owned = jnp.zeros((NT, LANES), F32)
    diagonal = same_bin(2 * NF, 2 * width)
    for couple in range(sets // 2):
        rows = slice(2 * couple * NF, 2 * (couple + 1) * NF)
        total = mine_ref[rows, :].astype(F32) + other_ref[rows, :].astype(F32)
        spectra = split_halves(total[:NF], total[NF:])
        signal = mute(mm(inverse, spectra.astype(BF16)), spectra[NF : NF + 1, :])
        owned = jnp.where(rcv_index // turns == couple, signal, owned)
        echo = mm(forward, signal.astype(BF16)).astype(BF16)
        for pair in range(blocks // 2):
            slot = (couple * (blocks // 2) + pair) ^ chip
            wide = jnp.where(diagonal, mm(echo, spread_ref[core, pair]), 0.0)
            for part in range(2):
                rows = slice(part * NF, (part + 1) * NF)
                vector_ref[:, part, slot] = interleave(
                    wide[rows, :width], wide[rows, width:]
                ).astype(BF16)
    turn = (turns - rcv_index % turns) % turns
    owned = pltpu.roll(owned, turn * (2 * half), 1)
    return jnp.transpose(owned)[: 2 * half].reshape(2, half, NT)


def mute_kernel(
    mine_ref, other_ref, forward_ref, inverse_ref, spread_ref, vector_ref, field_ref
):
    field_ref[...] = mute_half(
        mine_ref, other_ref, forward_ref[...], inverse_ref[...], spread_ref, vector_ref
    )


def adjoint_kernel(
    mine_ref, other_ref, forward_ref, inverse_ref, spread_ref,
    lower_ref, field_half_ref, first_ref, rest_ref, *refs
):
    keep_ref, far_ref, send_ref, field_ref, upper_ref = refs
    pairs = keep_ref.shape[0]
    receivers = first_ref.shape[-1] // 2
    width = lower_ref.shape[-1]
    half = width // GROUP
    field_ref[:, :half] = field_half_ref[...]
    field_ref[:, half:] = mute_half(
        mine_ref, other_ref, forward_ref[...], inverse_ref[...], spread_ref, upper_ref
    )

    def one(group):
        rows = 2 * pairs * 2 * GROUP
        vector = jnp.concatenate(
            [ref[group].reshape(rows, width) for ref in (lower_ref, upper_ref)], axis=1
        )
        matrix = jnp.concatenate(
            [ref[group].reshape(width, 2 * receivers) for ref in (first_ref, rest_ref)], axis=0
        )
        full = mm(vector, matrix).reshape(2, pairs, 2, GROUP, 2 * receivers)
        re = full[0, ..., :receivers] + full[1, ..., receivers:]
        im = full[1, ..., :receivers] - full[0, ..., receivers:]
        return re, im

    for couple in range(NG // 2):
        even = one(2 * couple)
        odd = one(2 * couple + 1)
        for part in range(2):
            both = jnp.concatenate([even[part], odd[part]], axis=2).astype(BF16)
            row = part * NF + couple * 2 * GROUP
            keep_ref[:, row : row + 2 * GROUP, :] = both[:, 0]
            far_ref[row : row + 2 * GROUP, :] = both[pairs - 1, 1]
            send_ref[:, row : row + 2 * GROUP, :] = both[: pairs - 1, 1]


def downgoing_kernel(*refs):
    parts = refs[:-6]
    focal_ref, onset_ref, forward_ref, inverse_ref, field_ref, plus_ref = refs[-6:]
    total = parts[0][...].astype(F32)
    for part in parts[1:]:
        total = total + part[...].astype(F32)
    onset = onset_ref[...].astype(F32)
    signal = mute(mm(inverse_ref[...], total.astype(BF16)), onset)
    field = focal_ref[...].astype(F32) + jnp.transpose(signal)
    field_ref[0] = field
    spectra = mm(forward_ref[...], field.astype(BF16), NT_DIMS)
    plus_ref[...] = interleave(spectra[:NF], spectra[NF:]).astype(BF16)


def second_kernel(pairs, *refs):
    near_refs, far_refs = refs[:pairs], refs[pairs : 2 * pairs]
    first_ref, rest_ref, gather_ref = refs[2 * pairs : 2 * pairs + 3]
    sum_refs = refs[2 * pairs + 3 : -2]
    vector_ref, kept_ref = refs[-2:]
    shot_index = lax.axis_index("shot")
    rcv_index = lax.axis_index("rcv")
    core = shot_index % 2
    chip = shot_index // 2
    for distance in range(pairs):
        slot = (chip ^ distance) ^ rcv_index
        store_vector(vector_ref, 2 * slot + core, *unpack(near_refs[distance]))
        store_vector(vector_ref, 2 * slot + 1 - core, *unpack(far_refs[distance]))

    def store(row, value):
        for slot in range(pairs):
            sum_refs[slot][row : row + 2 * GROUP, :] = value[slot]

    apply_matrix([first_ref, rest_ref], vector_ref, kept_ref, gather_ref[...], store)


def final_kernel(*refs):
    parts = refs[:-3]
    onset_ref, inverse_ref, field_ref = refs[-3:]
    total = parts[0][...].astype(F32)
    for part in parts[1:]:
        total = total + part[...].astype(F32)
    spectra = split_halves(total, total).astype(BF16)
    onset = onset_ref[...].astype(F32)
    onset = jnp.concatenate([onset[0:1], onset[1:2]] * 2, axis=1)
    signal = mute(mm(inverse_ref[...], spectra), onset)
    field_ref[...] = jnp.transpose(signal)[: LANES // 2].reshape(field_ref.shape)


def emit_kernel(field_ref, out_ref):
    out_ref[...] = field_ref[...]


def vmem(count):
    return [pl.BlockSpec(memory_space=pltpu.VMEM) for _ in range(count)]


def hbm(count):
    return [pl.BlockSpec(memory_space=pltpu.HBM) for _ in range(count)]


def call(kernel, name, out_shape, in_specs, scratch=(), work=1.0e9, out_specs=None):
    if out_specs is None:
        many = isinstance(out_shape, (tuple, list))
        out_specs = vmem(len(out_shape)) if many else vmem(1)[0]
    return pl.pallas_call(
        kernel,
        name=name,
        out_shape=out_shape,
        in_specs=in_specs,
        out_specs=out_specs,
        scratch_shapes=list(scratch),
        compiler_params=pltpu.CompilerParams(vmem_limit_bytes=40 << 20),
        cost_estimate=pl.CostEstimate(flops=int(work), bytes_accessed=1 << 20, transcendentals=0),
    )


def emit(field):
    return call(
        emit_kernel, "emit", jax.ShapeDtypeStruct(field.shape, field.dtype), vmem(1), work=0.3e9
    )(field)


def exchange(value, axis, distance):
    count = lax.axis_size(axis)
    return lax.ppermute(value, axis, [(place, place ^ distance) for place in range(count)])


def add_rounded(left, right):
    return (left.astype(F32) + right.astype(F32)).astype(BF16)


def body(traces, shift_index, deconv, focal_start, onset_source, onset_receiver):
    shot_count = lax.axis_size("shot")
    rcv_count = lax.axis_size("rcv")
    sources, receivers, _ = traces.shape
    focal_total = focal_start.shape[0]
    pairs = focal_total // 2
    assert onset_source.shape[0] == 2 and pairs == rcv_count
    assert focal_total == shot_count and 4 * sources == LANES and receivers == LANES
    gain = 1.0 / math.sqrt(NT * receivers * rcv_count)
    tables = make_tables(sources)
    shape = jax.ShapeDtypeStruct
    half = sources // 2
    sets = focal_total // (LANES // half // 2)
    vector = shape((NG, focal_total, 2 * GROUP, 2 * receivers), BF16)
    half_matrix = shape((NG, half // 2, 2 * GROUP, 2 * receivers), BF16)
    half_sums = shape((sets * NF, LANES), BF16)
    half_kept = pltpu.VMEM((NG // 2 * focal_total * 2 * GROUP, sources * GROUP), BF16)
    half_delays = pltpu.VMEM((half // 2, 2 * NF, LANES), BF16)
    assert sets % 2 == 0 and half * 8 == LANES

    def buffer(value):
        return pltpu.VMEM(value.shape, value.dtype)

    inputs = (
        traces, shift_index, deconv, focal_start, onset_source,
        tables["forward"], tables["taps"], tables["gather_half"],
    )
    small = (shift_index, deconv, onset_source) + inputs[5:]
    first, first_sum, focal_own, start, *loaded = call(
        functools.partial(first_kernel, gain),
        "first",
        [
            half_matrix,
            half_sums,
            shape((receivers, NT), BF16),
            vector,
        ]
        + [shape(value.shape, value.dtype) for value in small],
        hbm(len(inputs)),
        [
            half_kept,
            pltpu.VMEM((half, receivers, NT), BF16),
            buffer(focal_start),
            pltpu.SemaphoreType.DMA((2,)),
            pltpu.SemaphoreType.DMA((6,)),
            half_delays,
        ],
        work=4.0e9,
    )(*[pltpu.with_memory_space_constraint(value, pltpu.HBM) for value in inputs])
    forward = loaded[3]
    rest, rest_sum = call(
        functools.partial(rest_kernel, gain),
        "rest",
        (half_matrix, half_sums),
        vmem(8),
        [half_kept, half_delays],
        work=3.0e9,
    )(traces, *loaded, start)

    mine = [first_sum, rest_sum]
    other = [exchange(value, "rcv", 1) for value in mine]
    distance = 1
    while 2 * distance < rcv_count:
        distance *= 2
        mine = [add_rounded(left, right) for left, right in zip(mine, other)]
        other = [exchange(value, "rcv", distance) for value in mine]

    echo = shape((NG, 2, pairs, 2 * GROUP, half * GROUP), BF16)
    shared = (forward, tables["inverse"], tables["spread"])
    lower, field_half = call(
        mute_kernel,
        "mute",
        (echo, shape((2, half, NT), F32)),
        vmem(5),
        work=1.0e9,
    )(mine[0], other[0], *shared)

    keep, far, send, upgoing_first = call(
        adjoint_kernel,
        "adjoint",
        [
            shape((pairs, 2 * NF, receivers), BF16),
            shape((2 * NF, receivers), BF16),
            shape((pairs - 1, 2 * NF, receivers), BF16),
            shape((2, sources, NT), F32),
        ],
        vmem(9),
        [buffer(echo)],
        work=2.0e9,
    )(mine[1], other[1], *shared, lower, field_half, first, rest)

    far = exchange(far, "shot", 1)
    near = exchange(send, "shot", 1)
    parts = [exchange(add_rounded(keep[pairs - 1], far), "shot", 2 * (pairs - 1))]
    for distance in reversed(range(pairs - 1)):
        block = add_rounded(keep[distance], near[distance])
        parts.append(exchange(block, "shot", 2 * distance) if distance else block)

    downgoing, plus = call(
        downgoing_kernel,
        "downgoing",
        (
            shape((1, receivers, NT), F32),
            shape((NG, 2 * GROUP, receivers), BF16),
        ),
        vmem(pairs + 4),
    )(*parts, focal_own, onset_receiver, forward, tables["inverse"])

    near = [plus]
    for distance in range(1, pairs):
        near.append(exchange(plus, "shot", 2 * distance))
    far = [exchange(value, "shot", 1) for value in near]

    parts = call(
        functools.partial(second_kernel, pairs),
        "second",
        [shape((NF, LANES), BF16)] * pairs,
        vmem(2 * pairs + 3),
        [
            buffer(vector),
            pltpu.VMEM((NG * focal_total * 2 * GROUP, sources * GROUP), BF16),
        ],
    )(*near, *far, first, rest, tables["gather"])

    parts = [
        exchange(parts[distance], "rcv", distance) for distance in reversed(range(1, rcv_count))
    ] + [parts[0]]
    upgoing_second = call(
        final_kernel, "final", shape((2, sources, NT), F32), vmem(len(parts) + 2)
    )(*parts, loaded[2], tables["inverse"])
    return (emit(upgoing_first), emit(downgoing), upgoing_second)


def solution(mesh):
    placed = (
        P("shot", "rcv", None),
        P("shot", "rcv"),
        P("shot", None),
        P(None, "rcv", None),
        P("rcv", "shot"),
        P("shot", "rcv"),
    )
    return jax.shard_map(
        body,
        mesh=mesh,
        in_specs=placed,
        out_specs=(P("rcv", "shot", None), P("shot", "rcv", None), P("rcv", "shot", None)),
        check_vma=False,
    )
```

```python
import functools
import math

import jax
import jax.numpy as jnp
import numpy as np
from jax import lax
from jax.experimental import pallas as pl
from jax.experimental.pallas import tpu as pltpu
from jax.sharding import PartitionSpec as P

NT = 256
NF = 128
TAPS = 64
KSHIFT = 64
LANES = 128
GROUP = 8
NG = NF // GROUP

F32 = jnp.float32
BF16 = jnp.bfloat16
NN = (((1,), (0,)), ((), ()))
NT_DIMS = (((1,), (1,)), ((), ()))


def make_tables(source_local):
    sample = np.arange(NT)
    bins = np.arange(NF)
    angles = 2.0 * np.pi / NT * (bins[:, None] * sample[None, :] % NT)
    forward = np.concatenate([np.cos(angles), -np.sin(angles)], axis=0)
    weights = np.where(bins == 0, 1.0, 2.0) / NT
    inverse = (forward * np.concatenate([weights, weights])[:, None]).T
    tap = np.arange(TAPS, dtype=np.float64)
    fraction = np.arange(KSHIFT) * (TAPS / (4.0 * KSHIFT))
    offset = tap[None, :] - 0.375 * TAPS - fraction[:, None]
    window = 0.5 - 0.5 * np.cos(2.0 * np.pi * (tap + 0.5) / TAPS)
    tap_spec = forward[:, :TAPS] @ (np.sinc(offset) * window[None, :]).T
    return dict(
        forward=jnp.asarray(forward, F32).astype(BF16),
        inverse=jnp.asarray(inverse, F32).astype(BF16),
        taps=jnp.asarray(np.tile(tap_spec, (1, LANES // KSHIFT)), F32),
        gather=gather_table(source_local),
        gather_half=gather_table(source_local // 2, 2),
        spread=spread_table(source_local // 2),
    )


def gather_table(sources, count=1):
    source_of = np.arange(sources * GROUP) // GROUP
    pick = source_of[:, None] == np.arange(sources)[None, :]
    table = np.kron(np.eye(count), np.tile(pick, (1, LANES // sources)))
    return jnp.asarray(table, F32).astype(BF16)


def spread_table(sources):
    pick = (np.arange(sources * GROUP)[None, :] // GROUP == np.arange(sources)[:, None]).astype(
        np.float32
    )
    blocks = LANES // sources
    table = np.zeros((2, blocks // 2, blocks, sources, 2, sources * GROUP), np.float32)
    for core in range(2):
        for pair in range(blocks // 2):
            table[core, pair, 2 * pair + core, :, 0] = pick
            table[core, pair, 2 * pair + 1 - core, :, 1] = pick
    table = table.reshape(2, blocks // 2, LANES, 2 * sources * GROUP)
    return jnp.asarray(table, F32).astype(BF16)


def mm(left, right, dims=NN):
    return lax.dot_general(left, right, dims, preferred_element_type=F32)


def interleave(first, second):
    width = first.shape[-1]
    pair = jnp.stack(
        [first.reshape(NG, GROUP, width), second.reshape(NG, GROUP, width)], axis=1
    )
    return pair.reshape(NG, 2 * GROUP, width)


def same_bin(rows, lanes):
    row = lax.broadcasted_iota(jnp.int32, (rows, lanes), 0)
    lane = lax.broadcasted_iota(jnp.int32, (rows, lanes), 1)
    return (row % GROUP) == (lane % GROUP)


def store_vector(vector_ref, place, re, im):
    receivers = re.shape[-1]
    vector_ref[:, place, :, :receivers] = interleave(re, im).astype(BF16)
    vector_ref[:, place, :, receivers:] = interleave(-im, re).astype(BF16)


def unpack(spectra_ref):
    receivers = spectra_ref.shape[-1]
    values = spectra_ref[...].astype(F32).reshape(NG, 2, GROUP, receivers)
    return values[:, 0].reshape(NF, receivers), values[:, 1].reshape(NF, receivers)


def apply_matrix(matrix_refs, vector_refs, kept_ref, gather, core, store):
    fields = sum(ref.shape[1] for ref in vector_refs)
    rows = fields * 2 * GROUP
    half = matrix_refs[0].shape[1] * matrix_refs[0].shape[2]
    width = half * len(matrix_refs)
    blocks = LANES // (width // GROUP)
    members = blocks // 2
    sets = fields // members
    diagonal = same_bin(rows, width)
    block_of = lax.broadcasted_iota(jnp.int32, (sets, GROUP, LANES), 2) // (LANES // blocks)

    span = kept_ref.shape[1] // width

    for group in range(NG):
        vector = [ref[group].reshape(-1, ref.shape[-1]) for ref in vector_refs]
        vector = vector[0] if len(vector) == 1 else jnp.concatenate(vector, axis=0)
        matrix = [ref[group].reshape(half, ref.shape[-1]) for ref in matrix_refs]
        matrix = matrix[0] if len(matrix) == 1 else jnp.concatenate(matrix, axis=0)
        full = mm(vector, matrix, NT_DIMS)
        place, lane = group // span * rows, group % span * width
        kept_ref[place : place + rows, lane : lane + width] = jnp.where(
            diagonal, full, 0.0
        ).astype(BF16)

    for couple in range(NG // 2):
        count = 2 // span * rows
        spread = mm(kept_ref[couple * count : (couple + 1) * count, :], gather)
        both = []
        for one in range(2):
            place, lane = one // span * rows, one % span * LANES
            part = spread[place : place + rows, lane : lane + LANES]
            if len(vector_refs) == 2:
                part = part.reshape(2, sets, 2, GROUP, LANES)
                ours = block_of % 2 == core
                real = jnp.where(ours, part[0, :, 0], part[1, :, 0])
                imag = jnp.where(ours, part[0, :, 1], part[1, :, 1])
                value = jnp.where(block_of < 2, real, imag)
            else:
                part = part.reshape(sets, members, 2, GROUP, LANES)
                value = part[:, 0, 0]
                for block in range(1, blocks):
                    term = part[:, block % members, block // members]
                    value = jnp.where(block_of == block, term, value)
            both.append(value)
        store(couple * 2 * GROUP, jnp.concatenate(both, axis=1).astype(BF16))


def make_delays(first, count, forward_ref, deconv_ref, taps_ref, gain, delay_ref):
    deconv = deconv_ref[...]
    sources = deconv.shape[0]
    deconv_high = deconv.astype(BF16)
    deconv_low = (deconv - deconv_high.astype(F32)).astype(BF16)
    head = forward_ref[:, :TAPS]
    wave = (mm(head, deconv_high, NT_DIMS) + mm(head, deconv_low, NT_DIMS)) * gain
    wave_high = wave.astype(BF16)
    wave_low = (wave - wave_high.astype(F32)).astype(BF16)
    wave_both = jnp.concatenate([wave_high, wave_low], axis=1)
    taps = taps_ref[...]
    taps_re, taps_im = taps[:NF], taps[NF:]
    owner = lax.broadcasted_iota(jnp.int32, (2 * sources, 2 * LANES), 0) % sources
    place = lax.broadcasted_iota(jnp.int32, (2 * sources, 2 * LANES), 1) // KSHIFT
    for quad in range(count // 4):
        spread = mm(wave_both, (owner == place + (first + 4 * quad)).astype(F32).astype(BF16))
        for couple in range(2):
            lanes = slice(couple * LANES, (couple + 1) * LANES)
            wave_re, wave_im = spread[:NF, lanes], spread[NF:, lanes]
            delay_re = taps_re * wave_re - taps_im * wave_im
            delay_im = taps_re * wave_im + taps_im * wave_re
            delay_ref[2 * quad + couple] = jnp.concatenate([delay_re, delay_im], axis=0).astype(BF16)


def make_matrix(first, couple, forward, traces_ref, shift_ref, delay_ref, matrix_ref):
    receivers = shift_ref.shape[1]
    source = first + 2 * couple
    zeros = jnp.zeros((KSHIFT, receivers), F32)
    kinds = lax.broadcasted_iota(jnp.int32, (KSHIFT, receivers), 0)
    signals = traces_ref[2 * couple : 2 * couple + 2].reshape(2 * receivers, NT)
    raw = mm(forward, signals, NT_DIMS)
    hot = [
        (kinds == shift_ref[source + half : source + half + 1, :]).astype(F32)
        for half in range(2)
    ]
    hot = jnp.concatenate(
        [jnp.concatenate([hot[0], zeros], axis=1), jnp.concatenate([zeros, hot[1]], axis=1)],
        axis=0,
    ).astype(BF16)
    delay = mm(delay_ref[couple], hot)
    re = raw[:NF] * delay[:NF] - raw[NF:] * delay[NF:]
    im = raw[:NF] * delay[NF:] + raw[NF:] * delay[:NF]
    matrix_ref[:, couple, :, :receivers] = interleave(
        re[:, :receivers], re[:, receivers:]
    ).astype(BF16)
    matrix_ref[:, couple, :, receivers:] = interleave(
        im[:, :receivers], im[:, receivers:]
    ).astype(BF16)


def make_sums(first, rcv_index, matrix_ref, vector_ref, kept_ref, gather, onset_ref, sum_ref):
    half = 2 * matrix_ref.shape[1]
    sets = vector_ref.shape[1] // (LANES // half // 2)

    def store(row, value):
        for one in range(sets):
            sum_ref[one * NF + row : one * NF + row + 2 * GROUP, :] = value[one]

    apply_matrix([matrix_ref], [vector_ref], kept_ref, gather, None, store)
    own = onset_ref[...].astype(F32)[:, first : first + half]
    turns = LANES // (2 * half)
    own = jnp.concatenate([own[0:1], own[1:2]] * turns, axis=1)
    own = jnp.broadcast_to(own, (2 * GROUP, LANES))
    row = lax.broadcasted_iota(jnp.int32, own.shape, 0)
    lane = lax.broadcasted_iota(jnp.int32, own.shape, 1)
    spare = (row == 0) & (lane >= LANES // 2)
    for one in range(sets):
        block = turns // 2 + (rcv_index - one * (turns // 2))
        here = (rcv_index // (turns // 2) == one) & (lane // (2 * half) == block)
        rows = slice(one * NF, one * NF + 2 * GROUP)
        value = sum_ref[rows, :].astype(F32)
        sum_ref[rows, :] = jnp.where(spare, jnp.where(here, own, 0.0), value).astype(BF16)


def first_kernel(
    gain, traces_hbm, shift_hbm, deconv_hbm, focal_hbm, onset_hbm,
    forward_hbm, taps_hbm, gather_hbm, matrix_ref, sum_ref, own_ref, vector_ref,
    shift_ref, deconv_ref, onset_ref, forward_ref, taps_ref, gather_ref,
    kept_ref, traces_ref, focal_ref, large_sem, small_sem, delay_ref,
):
    half = traces_ref.shape[0]
    fields = focal_ref.shape[0]
    small = [
        pltpu.make_async_copy(source, target, small_sem.at[place])
        for place, (source, target) in enumerate(
            [
                (forward_hbm, forward_ref),
                (deconv_hbm, deconv_ref),
                (taps_hbm, taps_ref),
                (shift_hbm, shift_ref),
                (gather_hbm, gather_ref),
                (onset_hbm, onset_ref),
            ]
        )
    ]
    large = [
        pltpu.make_async_copy(focal_hbm, focal_ref, large_sem.at[0]),
        pltpu.make_async_copy(traces_hbm.at[pl.ds(0, half)], traces_ref, large_sem.at[1]),
    ]
    for copy in small[:3] + large + small[3:]:
        copy.start()
    for copy in small[:3]:
        copy.wait()
    make_delays(0, half, forward_ref, deconv_ref, taps_ref, gain, delay_ref)
    forward = forward_ref[...]
    large[0].wait()
    for place in range(0, fields, 2):
        signals = focal_ref[place : place + 2].reshape(-1, NT)
        receivers = signals.shape[0] // 2
        spectra = mm(forward, signals, NT_DIMS)
        for one in range(2):
            field = spectra[:, one * receivers : (one + 1) * receivers]
            store_vector(vector_ref, place + one, field[:NF], field[NF:])
    own_ref[...] = focal_ref[lax.axis_index("shot")]
    for copy in small[3:] + large[1:]:
        copy.wait()
    for couple in range(half // 2):
        make_matrix(0, couple, forward, traces_ref, shift_ref, delay_ref, matrix_ref)
    make_sums(
        0, lax.axis_index("rcv"), matrix_ref, vector_ref, kept_ref, gather_ref[...], onset_ref, sum_ref
    )


def rest_kernel(
    gain, traces_ref, shift_ref, deconv_ref, onset_ref, forward_ref, taps_ref,
    gather_ref, vector_ref, matrix_ref, sum_ref, kept_ref, delay_ref,
):
    half = traces_ref.shape[0] // 2
    make_delays(half, half, forward_ref, deconv_ref, taps_ref, gain, delay_ref)
    forward = forward_ref[...]
    upper = traces_ref.at[pl.ds(half, half)]
    for couple in range(half // 2):
        make_matrix(half, couple, forward, upper, shift_ref, delay_ref, matrix_ref)
    make_sums(
        half, lax.axis_index("rcv"), matrix_ref, vector_ref, kept_ref, gather_ref[...], onset_ref, sum_ref
    )


def split_halves(first, second):
    lane = lax.broadcasted_iota(jnp.int32, first.shape, 1)
    low = lane < LANES // 2
    re = jnp.where(low, first, pltpu.roll(second, LANES // 2, 1))
    im = jnp.where(low, pltpu.roll(first, LANES // 2, 1), second)
    return jnp.concatenate([re, im], axis=0)


def mute(signal, onset):
    sample = lax.broadcasted_iota(jnp.int32, signal.shape, 0)
    folded = jnp.minimum(sample, NT - sample).astype(F32)
    return jnp.where(folded < onset, signal, 0.0)


def mute_half(mine_ref, other_ref, forward, inverse, spread_ref, vector_ref):
    shot_index = lax.axis_index("shot")
    rcv_index = lax.axis_index("rcv")
    core = shot_index % 2
    chip = shot_index // 2
    width = vector_ref.shape[-1]
    half = width // GROUP
    blocks = LANES // half
    sets = mine_ref.shape[0] // NF
    turns = blocks // 2
    owned = jnp.zeros((NT, LANES), F32)
    diagonal = same_bin(2 * NF, 2 * width)
    for couple in range(sets // 2):
        rows = slice(2 * couple * NF, 2 * (couple + 1) * NF)
        total = mine_ref[rows, :].astype(F32) + other_ref[rows, :].astype(F32)
        spectra = split_halves(total[:NF], total[NF:])
        signal = mute(mm(inverse, spectra.astype(BF16)), spectra[NF : NF + 1, :])
        owned = jnp.where(rcv_index // turns == couple, signal, owned)
        echo = mm(forward, signal.astype(BF16)).astype(BF16)
        for pair in range(blocks // 2):
            slot = (couple * (blocks // 2) + pair) ^ chip
            wide = jnp.where(diagonal, mm(echo, spread_ref[core, pair]), 0.0)
            for part in range(2):
                rows = slice(part * NF, (part + 1) * NF)
                vector_ref[:, part, slot] = interleave(
                    wide[rows, :width], wide[rows, width:]
                ).astype(BF16)
    turn = (turns - rcv_index % turns) % turns
    owned = pltpu.roll(owned, turn * (2 * half), 1)
    return jnp.transpose(owned)[: 2 * half].reshape(2, half, NT)


def mute_kernel(
    mine_ref, other_ref, forward_ref, inverse_ref, spread_ref, vector_ref, field_ref
):
    field_ref[...] = mute_half(
        mine_ref, other_ref, forward_ref[...], inverse_ref[...], spread_ref, vector_ref
    )


def adjoint_kernel(
    mine_ref, other_ref, forward_ref, inverse_ref, spread_ref,
    lower_ref, field_half_ref, first_ref, rest_ref, *refs
):
    keep_ref, far_ref, send_ref, field_ref, upper_ref = refs
    pairs = keep_ref.shape[0]
    receivers = first_ref.shape[-1] // 2
    width = lower_ref.shape[-1]
    half = width // GROUP
    field_ref[:, :half] = field_half_ref[...]
    field_ref[:, half:] = mute_half(
        mine_ref, other_ref, forward_ref[...], inverse_ref[...], spread_ref, upper_ref
    )

    def one(group):
        rows = 2 * pairs * 2 * GROUP
        vector = jnp.concatenate(
            [ref[group].reshape(rows, width) for ref in (lower_ref, upper_ref)], axis=1
        )
        matrix = jnp.concatenate(
            [ref[group].reshape(width, 2 * receivers) for ref in (first_ref, rest_ref)], axis=0
        )
        full = mm(vector, matrix).reshape(2, pairs, 2, GROUP, 2 * receivers)
        re = full[0, ..., :receivers] + full[1, ..., receivers:]
        im = full[1, ..., :receivers] - full[0, ..., receivers:]
        return re, im

    for couple in range(NG // 2):
        even = one(2 * couple)
        odd = one(2 * couple + 1)
        for part in range(2):
            both = jnp.concatenate([even[part], odd[part]], axis=2).astype(BF16)
            row = part * NF + couple * 2 * GROUP
            keep_ref[:, row : row + 2 * GROUP, :] = both[:, 0]
            far_ref[row : row + 2 * GROUP, :] = both[pairs - 1, 1]
            send_ref[:, row : row + 2 * GROUP, :] = both[: pairs - 1, 1]


def downgoing_kernel(*refs):
    parts = refs[:-6]
    focal_ref, onset_ref, forward_ref, inverse_ref, field_ref, plus_ref = refs[-6:]
    total = parts[0][...].astype(F32)
    for part in parts[1:]:
        total = total + part[...].astype(F32)
    onset = onset_ref[...].astype(F32)
    signal = mute(mm(inverse_ref[...], total.astype(BF16)), onset)
    field = focal_ref[...].astype(F32) + jnp.transpose(signal)
    field_ref[0] = field
    spectra = mm(forward_ref[...], field.astype(BF16), NT_DIMS)
    plus_ref[...] = interleave(spectra[:NF], spectra[NF:]).astype(BF16)


def place_fields(field_refs, vector_ref):
    chip = lax.axis_index("shot") // 2
    for distance, field_ref in enumerate(field_refs):
        slot = (chip ^ distance) ^ lax.axis_index("rcv")
        store_vector(vector_ref, slot, *unpack(field_ref))


def near_kernel(*refs):
    place_fields(refs[:-1], refs[-1])


def second_kernel(pairs, *refs):
    first_ref, rest_ref, gather_ref, near_ref = refs[pairs : pairs + 4]
    sum_refs = refs[pairs + 4 : -2]
    far_ref, kept_ref = refs[-2:]
    place_fields(refs[:pairs], far_ref)

    def store(row, value):
        for slot in range(pairs):
            sum_refs[slot][row : row + 2 * GROUP, :] = value[slot]

    core = lax.axis_index("shot") % 2
    apply_matrix(
        [first_ref, rest_ref], [near_ref, far_ref], kept_ref, gather_ref[...], core, store
    )


def final_kernel(*refs):
    parts = refs[:-3]
    onset_ref, inverse_ref, field_ref = refs[-3:]
    total = parts[0][...].astype(F32)
    for part in parts[1:]:
        total = total + part[...].astype(F32)
    spectra = split_halves(total, total).astype(BF16)
    onset = onset_ref[...].astype(F32)
    onset = jnp.concatenate([onset[0:1], onset[1:2]] * 2, axis=1)
    signal = mute(mm(inverse_ref[...], spectra), onset)
    field_ref[...] = jnp.transpose(signal)[: LANES // 2].reshape(field_ref.shape)


def emit_kernel(field_ref, out_ref):
    out_ref[...] = field_ref[...]


def vmem(count):
    return [pl.BlockSpec(memory_space=pltpu.VMEM) for _ in range(count)]


def hbm(count):
    return [pl.BlockSpec(memory_space=pltpu.HBM) for _ in range(count)]


def call(kernel, name, out_shape, in_specs, scratch=(), work=1.0e9, out_specs=None):
    if out_specs is None:
        many = isinstance(out_shape, (tuple, list))
        out_specs = vmem(len(out_shape)) if many else vmem(1)[0]
    return pl.pallas_call(
        kernel,
        name=name,
        out_shape=out_shape,
        in_specs=in_specs,
        out_specs=out_specs,
        scratch_shapes=list(scratch),
        compiler_params=pltpu.CompilerParams(vmem_limit_bytes=40 << 20),
        cost_estimate=pl.CostEstimate(flops=int(work), bytes_accessed=1 << 20, transcendentals=0),
    )


def emit(field):
    return call(
        emit_kernel, "emit", jax.ShapeDtypeStruct(field.shape, field.dtype), vmem(1), work=0.3e9
    )(field)


def exchange(value, axis, distance):
    count = lax.axis_size(axis)
    return lax.ppermute(value, axis, [(place, place ^ distance) for place in range(count)])


def add_rounded(left, right):
    return (left.astype(F32) + right.astype(F32)).astype(BF16)


def body(traces, shift_index, deconv, focal_start, onset_source, onset_receiver):
    shot_count = lax.axis_size("shot")
    rcv_count = lax.axis_size("rcv")
    sources, receivers, _ = traces.shape
    focal_total = focal_start.shape[0]
    pairs = focal_total // 2
    assert onset_source.shape[0] == 2 and pairs == rcv_count
    assert focal_total == shot_count and 4 * sources == LANES and receivers == LANES
    gain = 1.0 / math.sqrt(NT * receivers * rcv_count)
    tables = make_tables(sources)
    shape = jax.ShapeDtypeStruct
    half = sources // 2
    sets = focal_total // (LANES // half // 2)
    vector = shape((NG, focal_total, 2 * GROUP, 2 * receivers), BF16)
    half_matrix = shape((NG, half // 2, 2 * GROUP, 2 * receivers), BF16)
    half_sums = shape((sets * NF, LANES), BF16)
    half_kept = pltpu.VMEM((NG // 2 * focal_total * 2 * GROUP, sources * GROUP), BF16)
    half_delays = pltpu.VMEM((half // 2, 2 * NF, LANES), BF16)
    assert sets % 2 == 0 and half * 8 == LANES

    def buffer(value):
        return pltpu.VMEM(value.shape, value.dtype)

    inputs = (
        traces, shift_index, deconv, focal_start, onset_source,
        tables["forward"], tables["taps"], tables["gather_half"],
    )
    small = (shift_index, deconv, onset_source) + inputs[5:]
    first, first_sum, focal_own, start, *loaded = call(
        functools.partial(first_kernel, gain),
        "first",
        [
            half_matrix,
            half_sums,
            shape((receivers, NT), BF16),
            vector,
        ]
        + [shape(value.shape, value.dtype) for value in small],
        hbm(len(inputs)),
        [
            half_kept,
            pltpu.VMEM((half, receivers, NT), BF16),
            buffer(focal_start),
            pltpu.SemaphoreType.DMA((2,)),
            pltpu.SemaphoreType.DMA((6,)),
            half_delays,
        ],
        work=4.0e9,
    )(*[pltpu.with_memory_space_constraint(value, pltpu.HBM) for value in inputs])
    forward = loaded[3]
    rest, rest_sum = call(
        functools.partial(rest_kernel, gain),
        "rest",
        (half_matrix, half_sums),
        vmem(8),
        [half_kept, half_delays],
        work=3.0e9,
    )(traces, *loaded, start)

    distances = [1 << step for step in range(rcv_count.bit_length() - 1)]
    routes = [(distances, distances), (distances, distances[::-1])]

    def hop(value, step, route):
        pairs_of = [
            (shot * rcv_count + rcv, shot * rcv_count + (rcv ^ route[shot % 2][step]))
            for shot in range(shot_count)
            for rcv in range(rcv_count)
        ]
        return lax.ppermute(value, ("shot", "rcv"), pairs_of)

    mine = [first_sum, rest_sum]
    other = [hop(value, 0, route) for value, route in zip(mine, routes)]
    for step in range(1, len(distances)):
        mine = [add_rounded(left, right) for left, right in zip(mine, other)]
        other = [hop(value, step, route) for value, route in zip(mine, routes)]

    echo = shape((NG, 2, pairs, 2 * GROUP, half * GROUP), BF16)
    shared = (forward, tables["inverse"], tables["spread"])
    lower, field_half = call(
        mute_kernel,
        "mute",
        (echo, shape((2, half, NT), F32)),
        vmem(5),
        work=1.0e9,
    )(mine[0], other[0], *shared)

    keep, far, send, upgoing_first = call(
        adjoint_kernel,
        "adjoint",
        [
            shape((pairs, 2 * NF, receivers), BF16),
            shape((2 * NF, receivers), BF16),
            shape((pairs - 1, 2 * NF, receivers), BF16),
            shape((2, sources, NT), F32),
        ],
        vmem(9),
        [buffer(echo)],
        work=2.0e9,
    )(mine[1], other[1], *shared, lower, field_half, first, rest)

    far = exchange(far, "shot", 1)
    near = exchange(send, "shot", 1)
    parts = [exchange(add_rounded(keep[pairs - 1], far), "shot", 2 * (pairs - 1))]
    for distance in reversed(range(pairs - 1)):
        block = add_rounded(keep[distance], near[distance])
        parts.append(exchange(block, "shot", 2 * distance) if distance else block)

    downgoing, plus = call(
        downgoing_kernel,
        "downgoing",
        (
            shape((1, receivers, NT), F32),
            shape((NG, 2 * GROUP, receivers), BF16),
        ),
        vmem(pairs + 4),
    )(*parts, focal_own, onset_receiver, forward, tables["inverse"])

    near = [plus]
    for distance in range(1, pairs):
        near.append(exchange(plus, "shot", 2 * distance))
    far = [exchange(value, "shot", 1) for value in near]

    half_vector = shape((NG, pairs, 2 * GROUP, 2 * receivers), BF16)
    near_vector = call(near_kernel, "near", half_vector, vmem(pairs), work=0.3e9)(*near)
    parts = call(
        functools.partial(second_kernel, pairs),
        "second",
        [shape((NF, LANES), BF16)] * pairs,
        vmem(pairs + 4),
        [
            buffer(half_vector),
            pltpu.VMEM((NG * focal_total * 2 * GROUP, sources * GROUP), BF16),
        ],
    )(*far, first, rest, tables["gather"], near_vector)

    parts = [
        exchange(parts[distance], "rcv", distance) for distance in reversed(range(1, rcv_count))
    ] + [parts[0]]
    upgoing_second = call(
        final_kernel, "final", shape((2, sources, NT), F32), vmem(len(parts) + 2)
    )(*parts, loaded[2], tables["inverse"])
    return (emit(upgoing_first), emit(downgoing), upgoing_second)


def solution(mesh):
    placed = (
        P("shot", "rcv", None),
        P("shot", "rcv"),
        P("shot", None),
        P(None, "rcv", None),
        P("rcv", "shot"),
        P("shot", "rcv"),
    )
    return jax.shard_map(
        body,
        mesh=mesh,
        in_specs=placed,
        out_specs=(P("rcv", "shot", None), P("shot", "rcv", None), P("rcv", "shot", None)),
        check_vma=False,
    )
```

```python
import functools
import math

import jax
import jax.numpy as jnp
import numpy as np
from jax import lax
from jax.experimental import pallas as pl
from jax.experimental.pallas import tpu as pltpu
from jax.sharding import PartitionSpec as P

NT = 256
NF = 128
TAPS = 64
KSHIFT = 64
LANES = 128
GROUP = 8
NG = NF // GROUP

F32 = jnp.float32
BF16 = jnp.bfloat16
NN = (((1,), (0,)), ((), ()))
NT_DIMS = (((1,), (1,)), ((), ()))


def make_tables(source_local):
    sample = np.arange(NT)
    bins = np.arange(NF)
    angles = 2.0 * np.pi / NT * (bins[:, None] * sample[None, :] % NT)
    forward = np.concatenate([np.cos(angles), -np.sin(angles)], axis=0)
    weights = np.where(bins == 0, 1.0, 2.0) / NT
    inverse = (forward * np.concatenate([weights, weights])[:, None]).T
    tap = np.arange(TAPS, dtype=np.float64)
    fraction = np.arange(KSHIFT) * (TAPS / (4.0 * KSHIFT))
    offset = tap[None, :] - 0.375 * TAPS - fraction[:, None]
    window = 0.5 - 0.5 * np.cos(2.0 * np.pi * (tap + 0.5) / TAPS)
    tap_spec = forward[:, :TAPS] @ (np.sinc(offset) * window[None, :]).T
    return dict(
        forward=jnp.asarray(forward, F32).astype(BF16),
        inverse=jnp.asarray(inverse, F32).astype(BF16),
        taps=jnp.asarray(np.tile(tap_spec, (1, LANES // KSHIFT)), F32),
        gather=gather_table(source_local),
        gather_half=gather_table(source_local // 2, 2),
        spread=spread_table(source_local // 2),
    )


def gather_table(sources, count=1):
    source_of = np.arange(sources * GROUP) // GROUP
    pick = source_of[:, None] == np.arange(sources)[None, :]
    table = np.kron(np.eye(count), np.tile(pick, (1, LANES // sources)))
    return jnp.asarray(table, F32).astype(BF16)


def spread_table(sources):
    pick = (np.arange(sources * GROUP)[None, :] // GROUP == np.arange(sources)[:, None]).astype(
        np.float32
    )
    blocks = LANES // sources
    table = np.zeros((2, blocks // 2, blocks, sources, 2, sources * GROUP), np.float32)
    for core in range(2):
        for pair in range(blocks // 2):
            table[core, pair, 2 * pair + core, :, 0] = pick
            table[core, pair, 2 * pair + 1 - core, :, 1] = pick
    table = table.reshape(2, blocks // 2, LANES, 2 * sources * GROUP)
    return jnp.asarray(table, F32).astype(BF16)


def mm(left, right, dims=NN):
    return lax.dot_general(left, right, dims, preferred_element_type=F32)


def interleave(first, second):
    width = first.shape[-1]
    pair = jnp.stack(
        [first.reshape(NG, GROUP, width), second.reshape(NG, GROUP, width)], axis=1
    )
    return pair.reshape(NG, 2 * GROUP, width)


def same_bin(rows, lanes):
    row = lax.broadcasted_iota(jnp.int32, (rows, lanes), 0)
    lane = lax.broadcasted_iota(jnp.int32, (rows, lanes), 1)
    return (row % GROUP) == (lane % GROUP)


def store_vector(vector_ref, place, re, im):
    receivers = re.shape[-1]
    vector_ref[:, place, :, :receivers] = interleave(re, im).astype(BF16)
    vector_ref[:, place, :, receivers:] = interleave(-im, re).astype(BF16)


def unpack(spectra_ref):
    receivers = spectra_ref.shape[-1]
    values = spectra_ref[...].astype(F32).reshape(NG, 2, GROUP, receivers)
    return values[:, 0].reshape(NF, receivers), values[:, 1].reshape(NF, receivers)


def apply_matrix(matrix_refs, vector_refs, kept_ref, gather, core, store):
    fields = sum(ref.shape[1] for ref in vector_refs)
    rows = fields * 2 * GROUP
    half = matrix_refs[0].shape[1] * matrix_refs[0].shape[2]
    width = half * len(matrix_refs)
    blocks = LANES // (width // GROUP)
    members = blocks // 2
    sets = fields // members
    diagonal = same_bin(rows, width)
    block_of = lax.broadcasted_iota(jnp.int32, (sets, GROUP, LANES), 2) // (LANES // blocks)

    span = kept_ref.shape[1] // width

    for group in range(NG):
        vector = [ref[group].reshape(-1, ref.shape[-1]) for ref in vector_refs]
        vector = vector[0] if len(vector) == 1 else jnp.concatenate(vector, axis=0)
        matrix = [ref[group].reshape(half, ref.shape[-1]) for ref in matrix_refs]
        matrix = matrix[0] if len(matrix) == 1 else jnp.concatenate(matrix, axis=0)
        full = mm(vector, matrix, NT_DIMS)
        place, lane = group // span * rows, group % span * width
        kept_ref[place : place + rows, lane : lane + width] = jnp.where(
            diagonal, full, 0.0
        ).astype(BF16)

    for couple in range(NG // 2):
        count = 2 // span * rows
        spread = mm(kept_ref[couple * count : (couple + 1) * count, :], gather)
        both = []
        for one in range(2):
            place, lane = one // span * rows, one % span * LANES
            part = spread[place : place + rows, lane : lane + LANES]
            if len(vector_refs) == 2:
                part = part.reshape(2, sets, 2, GROUP, LANES)
                ours = block_of % 2 == core
                real = jnp.where(ours, part[0, :, 0], part[1, :, 0])
                imag = jnp.where(ours, part[0, :, 1], part[1, :, 1])
                value = jnp.where(block_of < 2, real, imag)
            else:
                part = part.reshape(sets, members, 2, GROUP, LANES)
                value = part[:, 0, 0]
                for block in range(1, blocks):
                    term = part[:, block % members, block // members]
                    value = jnp.where(block_of == block, term, value)
            both.append(value)
        store(couple * 2 * GROUP, jnp.concatenate(both, axis=1).astype(BF16))


def make_delays(first, count, forward_ref, deconv_ref, taps_ref, gain, delay_ref):
    deconv = deconv_ref[...]
    sources = deconv.shape[0]
    deconv_high = deconv.astype(BF16)
    deconv_low = (deconv - deconv_high.astype(F32)).astype(BF16)
    head = forward_ref[:, :TAPS]
    wave = (mm(head, deconv_high, NT_DIMS) + mm(head, deconv_low, NT_DIMS)) * gain
    wave_high = wave.astype(BF16)
    wave_low = (wave - wave_high.astype(F32)).astype(BF16)
    wave_both = jnp.concatenate([wave_high, wave_low], axis=1)
    taps = taps_ref[...]
    taps_re, taps_im = taps[:NF], taps[NF:]
    owner = lax.broadcasted_iota(jnp.int32, (2 * sources, 2 * LANES), 0) % sources
    place = lax.broadcasted_iota(jnp.int32, (2 * sources, 2 * LANES), 1) // KSHIFT
    for quad in range(count // 4):
        spread = mm(wave_both, (owner == place + (first + 4 * quad)).astype(F32).astype(BF16))
        for couple in range(2):
            lanes = slice(couple * LANES, (couple + 1) * LANES)
            wave_re, wave_im = spread[:NF, lanes], spread[NF:, lanes]
            delay_re = taps_re * wave_re - taps_im * wave_im
            delay_im = taps_re * wave_im + taps_im * wave_re
            delay_ref[2 * quad + couple] = jnp.concatenate([delay_re, delay_im], axis=0).astype(BF16)


def make_matrix(first, couple, forward, traces_ref, shift_ref, delay_ref, matrix_ref):
    receivers = shift_ref.shape[1]
    source = first + 2 * couple
    zeros = jnp.zeros((KSHIFT, receivers), F32)
    kinds = lax.broadcasted_iota(jnp.int32, (KSHIFT, receivers), 0)
    signals = traces_ref[2 * couple : 2 * couple + 2].reshape(2 * receivers, NT)
    raw = mm(forward, signals, NT_DIMS)
    hot = [
        (kinds == shift_ref[source + half : source + half + 1, :]).astype(F32)
        for half in range(2)
    ]
    hot = jnp.concatenate(
        [jnp.concatenate([hot[0], zeros], axis=1), jnp.concatenate([zeros, hot[1]], axis=1)],
        axis=0,
    ).astype(BF16)
    delay = mm(delay_ref[couple], hot)
    re = raw[:NF] * delay[:NF] - raw[NF:] * delay[NF:]
    im = raw[:NF] * delay[NF:] + raw[NF:] * delay[:NF]
    matrix_ref[:, couple, :, :receivers] = interleave(
        re[:, :receivers], re[:, receivers:]
    ).astype(BF16)
    matrix_ref[:, couple, :, receivers:] = interleave(
        im[:, :receivers], im[:, receivers:]
    ).astype(BF16)


def make_sums(first, rcv_index, matrix_ref, vector_ref, kept_ref, gather, onset_ref, sum_ref):
    half = 2 * matrix_ref.shape[1]
    sets = vector_ref.shape[1] // (LANES // half // 2)

    def store(row, value):
        for one in range(sets):
            sum_ref[one * NF + row : one * NF + row + 2 * GROUP, :] = value[one]

    apply_matrix([matrix_ref], [vector_ref], kept_ref, gather, None, store)
    own = onset_ref[...].astype(F32)[:, first : first + half]
    turns = LANES // (2 * half)
    own = jnp.concatenate([own[0:1], own[1:2]] * turns, axis=1)
    own = jnp.broadcast_to(own, (2 * GROUP, LANES))
    row = lax.broadcasted_iota(jnp.int32, own.shape, 0)
    lane = lax.broadcasted_iota(jnp.int32, own.shape, 1)
    spare = (row == 0) & (lane >= LANES // 2)
    for one in range(sets):
        block = turns // 2 + (rcv_index - one * (turns // 2))
        here = (rcv_index // (turns // 2) == one) & (lane // (2 * half) == block)
        rows = slice(one * NF, one * NF + 2 * GROUP)
        value = sum_ref[rows, :].astype(F32)
        sum_ref[rows, :] = jnp.where(spare, jnp.where(here, own, 0.0), value).astype(BF16)


def first_kernel(
    gain, traces_hbm, shift_hbm, deconv_hbm, focal_hbm, onset_hbm,
    forward_hbm, taps_hbm, gather_hbm, matrix_ref, sum_ref, own_ref, vector_ref,
    shift_ref, deconv_ref, onset_ref, forward_ref, taps_ref, gather_ref,
    kept_ref, traces_ref, focal_ref, large_sem, small_sem, delay_ref,
):
    half = traces_ref.shape[0]
    fields = focal_ref.shape[0]
    small = [
        pltpu.make_async_copy(source, target, small_sem.at[place])
        for place, (source, target) in enumerate(
            [
                (forward_hbm, forward_ref),
                (deconv_hbm, deconv_ref),
                (taps_hbm, taps_ref),
                (shift_hbm, shift_ref),
                (gather_hbm, gather_ref),
                (onset_hbm, onset_ref),
            ]
        )
    ]
    large = [
        pltpu.make_async_copy(focal_hbm, focal_ref, large_sem.at[0]),
        pltpu.make_async_copy(traces_hbm.at[pl.ds(0, half)], traces_ref, large_sem.at[1]),
    ]
    for copy in small[:3] + large + small[3:]:
        copy.start()
    for copy in small[:3]:
        copy.wait()
    make_delays(0, half, forward_ref, deconv_ref, taps_ref, gain, delay_ref)
    forward = forward_ref[...]
    large[0].wait()
    for place in range(0, fields, 2):
        signals = focal_ref[place : place + 2].reshape(-1, NT)
        receivers = signals.shape[0] // 2
        spectra = mm(forward, signals, NT_DIMS)
        for one in range(2):
            field = spectra[:, one * receivers : (one + 1) * receivers]
            store_vector(vector_ref, place + one, field[:NF], field[NF:])
    own_ref[...] = focal_ref[lax.axis_index("shot")]
    for copy in small[3:] + large[1:]:
        copy.wait()
    for couple in range(half // 2):
        make_matrix(0, couple, forward, traces_ref, shift_ref, delay_ref, matrix_ref)
    make_sums(
        0, lax.axis_index("rcv"), matrix_ref, vector_ref, kept_ref, gather_ref[...], onset_ref, sum_ref
    )


def rest_kernel(
    gain, traces_ref, shift_ref, deconv_ref, onset_ref, forward_ref, taps_ref,
    gather_ref, vector_ref, matrix_ref, sum_ref, kept_ref, delay_ref,
):
    half = traces_ref.shape[0] // 2
    make_delays(half, half, forward_ref, deconv_ref, taps_ref, gain, delay_ref)
    forward = forward_ref[...]
    upper = traces_ref.at[pl.ds(half, half)]
    for couple in range(half // 2):
        make_matrix(half, couple, forward, upper, shift_ref, delay_ref, matrix_ref)
    make_sums(
        half, lax.axis_index("rcv"), matrix_ref, vector_ref, kept_ref, gather_ref[...], onset_ref, sum_ref
    )


def split_halves(first, second):
    lane = lax.broadcasted_iota(jnp.int32, first.shape, 1)
    low = lane < LANES // 2
    re = jnp.where(low, first, pltpu.roll(second, LANES // 2, 1))
    im = jnp.where(low, pltpu.roll(first, LANES // 2, 1), second)
    return jnp.concatenate([re, im], axis=0)


def mute(signal, onset):
    sample = lax.broadcasted_iota(jnp.int32, signal.shape, 0)
    folded = jnp.minimum(sample, NT - sample).astype(F32)
    return jnp.where(folded < onset, signal, 0.0)


def mute_half(mine_ref, other_ref, forward, inverse, spread_ref, vector_ref):
    shot_index = lax.axis_index("shot")
    rcv_index = lax.axis_index("rcv")
    core = shot_index % 2
    chip = shot_index // 2
    width = vector_ref.shape[-1]
    half = width // GROUP
    blocks = LANES // half
    sets = mine_ref.shape[0] // NF
    turns = blocks // 2
    owned = jnp.zeros((NT, LANES), F32)
    diagonal = same_bin(2 * NF, 2 * width)
    for couple in range(sets // 2):
        rows = slice(2 * couple * NF, 2 * (couple + 1) * NF)
        total = mine_ref[rows, :].astype(F32) + other_ref[rows, :].astype(F32)
        spectra = split_halves(total[:NF], total[NF:])
        signal = mute(mm(inverse, spectra.astype(BF16)), spectra[NF : NF + 1, :])
        owned = jnp.where(rcv_index // turns == couple, signal, owned)
        echo = mm(forward, signal.astype(BF16)).astype(BF16)
        for pair in range(blocks // 2):
            slot = (couple * (blocks // 2) + pair) ^ chip
            wide = jnp.where(diagonal, mm(echo, spread_ref[core, pair]), 0.0)
            for part in range(2):
                rows = slice(part * NF, (part + 1) * NF)
                vector_ref[:, part, slot] = interleave(
                    wide[rows, :width], wide[rows, width:]
                ).astype(BF16)
    turn = (turns - rcv_index % turns) % turns
    owned = pltpu.roll(owned, turn * (2 * half), 1)
    return jnp.transpose(owned)[: 2 * half].reshape(2, half, NT)


def mute_kernel(
    mine_ref, other_ref, forward_ref, inverse_ref, spread_ref, vector_ref, field_ref
):
    field_ref[...] = mute_half(
        mine_ref, other_ref, forward_ref[...], inverse_ref[...], spread_ref, vector_ref
    )


def adjoint_kernel(
    mine_ref, other_ref, forward_ref, inverse_ref, spread_ref,
    lower_ref, field_half_ref, first_ref, rest_ref, *refs
):
    keep_ref, far_ref, send_ref, field_ref, upper_ref = refs
    pairs = keep_ref.shape[0]
    receivers = first_ref.shape[-1] // 2
    width = lower_ref.shape[-1]
    half = width // GROUP
    field_ref[:, :half] = field_half_ref[...]
    field_ref[:, half:] = mute_half(
        mine_ref, other_ref, forward_ref[...], inverse_ref[...], spread_ref, upper_ref
    )

    def one(group):
        rows = 2 * pairs * 2 * GROUP
        vector = jnp.concatenate(
            [ref[group].reshape(rows, width) for ref in (lower_ref, upper_ref)], axis=1
        )
        matrix = jnp.concatenate(
            [ref[group].reshape(width, 2 * receivers) for ref in (first_ref, rest_ref)], axis=0
        )
        full = mm(vector, matrix).reshape(2, pairs, 2, GROUP, 2 * receivers)
        re = full[0, ..., :receivers] + full[1, ..., receivers:]
        im = full[1, ..., :receivers] - full[0, ..., receivers:]
        return re, im

    for couple in range(NG // 2):
        even = one(2 * couple)
        odd = one(2 * couple + 1)
        for part in range(2):
            both = jnp.concatenate([even[part], odd[part]], axis=2).astype(BF16)
            row = part * NF + couple * 2 * GROUP
            keep_ref[:, row : row + 2 * GROUP, :] = both[:, 0]
            far_ref[row : row + 2 * GROUP, :] = both[pairs - 1, 1]
            send_ref[:, row : row + 2 * GROUP, :] = both[: pairs - 1, 1]


def downgoing_kernel(*refs):
    parts = refs[:-6]
    focal_ref, onset_ref, forward_ref, inverse_ref, field_ref, plus_ref = refs[-6:]
    total = parts[0][...].astype(F32)
    for part in parts[1:]:
        total = total + part[...].astype(F32)
    onset = onset_ref[...].astype(F32)
    signal = mute(mm(inverse_ref[...], total.astype(BF16)), onset)
    field = focal_ref[...].astype(F32) + jnp.transpose(signal)
    field_ref[0] = field
    spectra = mm(forward_ref[...], field.astype(BF16), NT_DIMS)
    plus_ref[...] = interleave(spectra[:NF], spectra[NF:]).astype(BF16)


def place_fields(field_refs, vector_ref):
    chip = lax.axis_index("shot") // 2
    for distance, field_ref in enumerate(field_refs):
        slot = (chip ^ distance) ^ lax.axis_index("rcv")
        swapped = (slot & ~3) | ((slot & 1) << 1) | ((slot >> 1) & 1)
        slot = jnp.where(lax.axis_index("shot") % 2 == 0, slot, swapped)
        store_vector(vector_ref, slot, *unpack(field_ref))


def near_kernel(*refs):
    place_fields(refs[:-1], refs[-1])


def second_kernel(pairs, *refs):
    first_ref, rest_ref, gather_ref, near_ref = refs[pairs : pairs + 4]
    sum_refs = refs[pairs + 4 : -2]
    far_ref, kept_ref = refs[-2:]
    place_fields(refs[:pairs], far_ref)

    def store(row, value):
        for slot in range(pairs):
            sum_refs[slot][row : row + 2 * GROUP, :] = value[slot]

    core = lax.axis_index("shot") % 2
    apply_matrix(
        [first_ref, rest_ref], [near_ref, far_ref], kept_ref, gather_ref[...], core, store
    )


def final_kernel(*refs):
    parts = refs[:-3]
    onset_ref, inverse_ref, field_ref = refs[-3:]
    total = parts[0][...].astype(F32)
    for part in parts[1:]:
        total = total + part[...].astype(F32)
    spectra = split_halves(total, total).astype(BF16)
    onset = onset_ref[...].astype(F32)
    onset = jnp.concatenate([onset[0:1], onset[1:2]] * 2, axis=1)
    signal = mute(mm(inverse_ref[...], spectra), onset)
    field_ref[...] = jnp.transpose(signal)[: LANES // 2].reshape(field_ref.shape)


def emit_kernel(field_ref, out_ref):
    out_ref[...] = field_ref[...]


def vmem(count):
    return [pl.BlockSpec(memory_space=pltpu.VMEM) for _ in range(count)]


def hbm(count):
    return [pl.BlockSpec(memory_space=pltpu.HBM) for _ in range(count)]


def call(kernel, name, out_shape, in_specs, scratch=(), work=1.0e9, out_specs=None):
    if out_specs is None:
        many = isinstance(out_shape, (tuple, list))
        out_specs = vmem(len(out_shape)) if many else vmem(1)[0]
    return pl.pallas_call(
        kernel,
        name=name,
        out_shape=out_shape,
        in_specs=in_specs,
        out_specs=out_specs,
        scratch_shapes=list(scratch),
        compiler_params=pltpu.CompilerParams(vmem_limit_bytes=40 << 20),
        cost_estimate=pl.CostEstimate(flops=int(work), bytes_accessed=1 << 20, transcendentals=0),
    )


def emit(field):
    return call(
        emit_kernel, "emit", jax.ShapeDtypeStruct(field.shape, field.dtype), vmem(1), work=0.3e9
    )(field)


def exchange(value, axis, distance):
    count = lax.axis_size(axis)
    return lax.ppermute(value, axis, [(place, place ^ distance) for place in range(count)])


def add_rounded(left, right):
    return (left.astype(F32) + right.astype(F32)).astype(BF16)


def body(traces, shift_index, deconv, focal_start, onset_source, onset_receiver):
    shot_count = lax.axis_size("shot")
    rcv_count = lax.axis_size("rcv")
    sources, receivers, _ = traces.shape
    focal_total = focal_start.shape[0]
    pairs = focal_total // 2
    assert onset_source.shape[0] == 2 and pairs == rcv_count
    assert focal_total == shot_count and 4 * sources == LANES and receivers == LANES
    gain = 1.0 / math.sqrt(NT * receivers * rcv_count)
    tables = make_tables(sources)
    shape = jax.ShapeDtypeStruct
    half = sources // 2
    sets = focal_total // (LANES // half // 2)
    vector = shape((NG, focal_total, 2 * GROUP, 2 * receivers), BF16)
    half_matrix = shape((NG, half // 2, 2 * GROUP, 2 * receivers), BF16)
    half_sums = shape((sets * NF, LANES), BF16)
    half_kept = pltpu.VMEM((NG // 2 * focal_total * 2 * GROUP, sources * GROUP), BF16)
    half_delays = pltpu.VMEM((half // 2, 2 * NF, LANES), BF16)
    assert sets % 2 == 0 and half * 8 == LANES

    def buffer(value):
        return pltpu.VMEM(value.shape, value.dtype)

    inputs = (
        traces, shift_index, deconv, focal_start, onset_source,
        tables["forward"], tables["taps"], tables["gather_half"],
    )
    small = (shift_index, deconv, onset_source) + inputs[5:]
    first, first_sum, focal_own, start, *loaded = call(
        functools.partial(first_kernel, gain),
        "first",
        [
            half_matrix,
            half_sums,
            shape((receivers, NT), BF16),
            vector,
        ]
        + [shape(value.shape, value.dtype) for value in small],
        hbm(len(inputs)),
        [
            half_kept,
            pltpu.VMEM((half, receivers, NT), BF16),
            buffer(focal_start),
            pltpu.SemaphoreType.DMA((2,)),
            pltpu.SemaphoreType.DMA((6,)),
            half_delays,
        ],
        work=4.0e9,
    )(*[pltpu.with_memory_space_constraint(value, pltpu.HBM) for value in inputs])
    forward = loaded[3]
    rest, rest_sum = call(
        functools.partial(rest_kernel, gain),
        "rest",
        (half_matrix, half_sums),
        vmem(8),
        [half_kept, half_delays],
        work=3.0e9,
    )(traces, *loaded, start)

    distances = [1 << step for step in range(rcv_count.bit_length() - 1)]
    routes = [(distances, distances), (distances, distances[::-1])]

    def hop(value, step, route):
        pairs_of = [
            (shot * rcv_count + rcv, shot * rcv_count + (rcv ^ route[shot % 2][step]))
            for shot in range(shot_count)
            for rcv in range(rcv_count)
        ]
        return lax.ppermute(value, ("shot", "rcv"), pairs_of)

    mine = [first_sum, rest_sum]
    other = [hop(value, 0, route) for value, route in zip(mine, routes)]
    for step in range(1, len(distances)):
        mine = [add_rounded(left, right) for left, right in zip(mine, other)]
        other = [hop(value, step, route) for value, route in zip(mine, routes)]

    echo = shape((NG, 2, pairs, 2 * GROUP, half * GROUP), BF16)
    shared = (forward, tables["inverse"], tables["spread"])
    lower, field_half = call(
        mute_kernel,
        "mute",
        (echo, shape((2, half, NT), F32)),
        vmem(5),
        work=1.0e9,
    )(mine[0], other[0], *shared)

    keep, far, send, upgoing_first = call(
        adjoint_kernel,
        "adjoint",
        [
            shape((pairs, 2 * NF, receivers), BF16),
            shape((2 * NF, receivers), BF16),
            shape((pairs - 1, 2 * NF, receivers), BF16),
            shape((2, sources, NT), F32),
        ],
        vmem(9),
        [buffer(echo)],
        work=2.0e9,
    )(mine[1], other[1], *shared, lower, field_half, first, rest)

    far = exchange(far, "shot", 1)
    near = exchange(send, "shot", 1)
    parts = [exchange(add_rounded(keep[pairs - 1], far), "shot", 2 * (pairs - 1))]
    for distance in reversed(range(pairs - 1)):
        block = add_rounded(keep[distance], near[distance])
        parts.append(exchange(block, "shot", 2 * distance) if distance else block)

    downgoing, plus = call(
        downgoing_kernel,
        "downgoing",
        (
            shape((1, receivers, NT), F32),
            shape((NG, 2 * GROUP, receivers), BF16),
        ),
        vmem(pairs + 4),
    )(*parts, focal_own, onset_receiver, forward, tables["inverse"])

    near = [plus]
    for distance in range(1, pairs):
        near.append(exchange(plus, "shot", 2 * distance))
    far = [exchange(value, "shot", 1) for value in near]

    def scatter(value, distance):
        swapped = (distance & ~3) | ((distance & 1) << 1) | ((distance >> 1) & 1)
        routes = [
            (shot * rcv_count + rcv, shot * rcv_count + (rcv ^ (swapped if shot % 2 else distance)))
            for shot in range(shot_count)
            for rcv in range(rcv_count)
        ]
        return lax.ppermute(value, ("shot", "rcv"), routes)

    half_vector = shape((NG, pairs, 2 * GROUP, 2 * receivers), BF16)
    near_vector = call(near_kernel, "near", half_vector, vmem(pairs), work=0.3e9)(*near)
    parts = call(
        functools.partial(second_kernel, pairs),
        "second",
        [shape((NF, LANES), BF16)] * pairs,
        vmem(pairs + 4),
        [
            buffer(half_vector),
            pltpu.VMEM((NG * focal_total * 2 * GROUP, sources * GROUP), BF16),
        ],
    )(*far, first, rest, tables["gather"], near_vector)

    parts = [
        scatter(parts[distance], distance) for distance in reversed(range(1, rcv_count))
    ] + [parts[0]]
    upgoing_second = call(
        final_kernel, "final", shape((2, sources, NT), F32), vmem(len(parts) + 2)
    )(*parts, loaded[2], tables["inverse"])
    return (emit(upgoing_first), emit(downgoing), upgoing_second)


def solution(mesh):
    placed = (
        P("shot", "rcv", None),
        P("shot", "rcv"),
        P("shot", None),
        P(None, "rcv", None),
        P("rcv", "shot"),
        P("shot", "rcv"),
    )
    return jax.shard_map(
        body,
        mesh=mesh,
        in_specs=placed,
        out_specs=(P("rcv", "shot", None), P("shot", "rcv", None), P("rcv", "shot", None)),
        check_vma=False,
    )
```

```python
import functools
import math

import jax
import jax.numpy as jnp
import numpy as np
from jax import lax
from jax.experimental import pallas as pl
from jax.experimental.pallas import tpu as pltpu
from jax.sharding import PartitionSpec as P

NT = 256
NF = 128
TAPS = 64
KSHIFT = 64
LANES = 128
GROUP = 8
NG = NF // GROUP

F32 = jnp.float32
BF16 = jnp.bfloat16
NN = (((1,), (0,)), ((), ()))
NT_DIMS = (((1,), (1,)), ((), ()))


def make_tables(source_local):
    sample = np.arange(NT)
    bins = np.arange(NF)
    angles = 2.0 * np.pi / NT * (bins[:, None] * sample[None, :] % NT)
    forward = np.concatenate([np.cos(angles), -np.sin(angles)], axis=0)
    weights = np.where(bins == 0, 1.0, 2.0) / NT
    inverse = (forward * np.concatenate([weights, weights])[:, None]).T
    tap = np.arange(TAPS, dtype=np.float64)
    fraction = np.arange(KSHIFT) * (TAPS / (4.0 * KSHIFT))
    offset = tap[None, :] - 0.375 * TAPS - fraction[:, None]
    window = 0.5 - 0.5 * np.cos(2.0 * np.pi * (tap + 0.5) / TAPS)
    tap_spec = forward[:, :TAPS] @ (np.sinc(offset) * window[None, :]).T
    return dict(
        forward=jnp.asarray(forward, F32).astype(BF16),
        inverse=jnp.asarray(inverse, F32).astype(BF16),
        taps=jnp.asarray(np.tile(tap_spec, (1, LANES // KSHIFT)), F32),
        gather=gather_table(source_local),
        gather_half=gather_table(source_local // 2, 2),
        spread=spread_table(source_local // 2),
    )


def gather_table(sources, count=1):
    source_of = np.arange(sources * GROUP) // GROUP
    pick = source_of[:, None] == np.arange(sources)[None, :]
    table = np.kron(np.eye(count), np.tile(pick, (1, LANES // sources)))
    return jnp.asarray(table, F32).astype(BF16)


def spread_table(sources):
    pick = (np.arange(sources * GROUP)[None, :] // GROUP == np.arange(sources)[:, None]).astype(
        np.float32
    )
    blocks = LANES // sources
    table = np.zeros((2, blocks // 2, blocks, sources, 2, sources * GROUP), np.float32)
    for core in range(2):
        for pair in range(blocks // 2):
            table[core, pair, 2 * pair + core, :, 0] = pick
            table[core, pair, 2 * pair + 1 - core, :, 1] = pick
    table = table.reshape(2, blocks // 2, LANES, 2 * sources * GROUP)
    return jnp.asarray(table, F32).astype(BF16)


def mm(left, right, dims=NN):
    return lax.dot_general(left, right, dims, preferred_element_type=F32)


def interleave(first, second):
    width = first.shape[-1]
    pair = jnp.stack(
        [first.reshape(NG, GROUP, width), second.reshape(NG, GROUP, width)], axis=1
    )
    return pair.reshape(NG, 2 * GROUP, width)


def same_bin(rows, lanes):
    row = lax.broadcasted_iota(jnp.int32, (rows, lanes), 0)
    lane = lax.broadcasted_iota(jnp.int32, (rows, lanes), 1)
    return (row % GROUP) == (lane % GROUP)


def store_vector(vector_ref, place, re, im):
    receivers = re.shape[-1]
    vector_ref[:, place, :, :receivers] = interleave(re, im).astype(BF16)
    vector_ref[:, place, :, receivers:] = interleave(-im, re).astype(BF16)


def unpack(spectra_ref):
    receivers = spectra_ref.shape[-1]
    values = spectra_ref[...].astype(F32).reshape(NG, 2, GROUP, receivers)
    return values[:, 0].reshape(NF, receivers), values[:, 1].reshape(NF, receivers)


def apply_matrix(matrix_refs, vector_refs, kept_ref, gather, core, store):
    fields = sum(ref.shape[1] for ref in vector_refs)
    rows = fields * 2 * GROUP
    half = matrix_refs[0].shape[1] * matrix_refs[0].shape[2]
    width = half * len(matrix_refs)
    blocks = LANES // (width // GROUP)
    members = blocks // 2
    sets = fields // members
    diagonal = same_bin(rows, width)
    block_of = lax.broadcasted_iota(jnp.int32, (sets, GROUP, LANES), 2) // (LANES // blocks)

    span = kept_ref.shape[1] // width

    for group in range(NG):
        vector = [ref[group].reshape(-1, ref.shape[-1]) for ref in vector_refs]
        vector = vector[0] if len(vector) == 1 else jnp.concatenate(vector, axis=0)
        matrix = [ref[group].reshape(half, ref.shape[-1]) for ref in matrix_refs]
        matrix = matrix[0] if len(matrix) == 1 else jnp.concatenate(matrix, axis=0)
        full = mm(vector, matrix, NT_DIMS)
        place, lane = group // span * rows, group % span * width
        kept_ref[place : place + rows, lane : lane + width] = jnp.where(
            diagonal, full, 0.0
        ).astype(BF16)

    for couple in range(NG // 2):
        count = 2 // span * rows
        spread = mm(kept_ref[couple * count : (couple + 1) * count, :], gather)
        both = []
        for one in range(2):
            place, lane = one // span * rows, one % span * LANES
            part = spread[place : place + rows, lane : lane + LANES]
            if len(vector_refs) == 2:
                part = part.reshape(2, sets, 2, GROUP, LANES)
                ours = block_of % 2 == core
                real = jnp.where(ours, part[0, :, 0], part[1, :, 0])
                imag = jnp.where(ours, part[0, :, 1], part[1, :, 1])
                value = jnp.where(block_of < 2, real, imag)
            else:
                part = part.reshape(sets, members, 2, GROUP, LANES)
                value = part[:, 0, 0]
                for block in range(1, blocks):
                    term = part[:, block % members, block // members]
                    value = jnp.where(block_of == block, term, value)
            both.append(value)
        store(couple * 2 * GROUP, jnp.concatenate(both, axis=1).astype(BF16))


def make_delays(first, count, forward_ref, deconv_ref, taps_ref, gain, delay_ref):
    deconv = deconv_ref[...]
    sources = deconv.shape[0]
    deconv_high = deconv.astype(BF16)
    deconv_low = (deconv - deconv_high.astype(F32)).astype(BF16)
    head = forward_ref[:, :TAPS]
    wave = (mm(head, deconv_high, NT_DIMS) + mm(head, deconv_low, NT_DIMS)) * gain
    wave_high = wave.astype(BF16)
    wave_low = (wave - wave_high.astype(F32)).astype(BF16)
    wave_both = jnp.concatenate([wave_high, wave_low], axis=1)
    taps = taps_ref[...]
    taps_re, taps_im = taps[:NF], taps[NF:]
    owner = lax.broadcasted_iota(jnp.int32, (2 * sources, 2 * LANES), 0) % sources
    place = lax.broadcasted_iota(jnp.int32, (2 * sources, 2 * LANES), 1) // KSHIFT
    for quad in range(count // 4):
        spread = mm(wave_both, (owner == place + (first + 4 * quad)).astype(F32).astype(BF16))
        for couple in range(2):
            lanes = slice(couple * LANES, (couple + 1) * LANES)
            wave_re, wave_im = spread[:NF, lanes], spread[NF:, lanes]
            delay_re = taps_re * wave_re - taps_im * wave_im
            delay_im = taps_re * wave_im + taps_im * wave_re
            delay_ref[2 * quad + couple] = jnp.concatenate([delay_re, delay_im], axis=0).astype(BF16)


def make_matrix(first, couple, forward, traces_ref, shift_ref, delay_ref, matrix_ref):
    receivers = shift_ref.shape[1]
    source = first + 2 * couple
    zeros = jnp.zeros((KSHIFT, receivers), F32)
    kinds = lax.broadcasted_iota(jnp.int32, (KSHIFT, receivers), 0)
    signals = traces_ref[2 * couple : 2 * couple + 2].reshape(2 * receivers, NT)
    raw = mm(forward, signals, NT_DIMS)
    hot = [
        (kinds == shift_ref[source + half : source + half + 1, :]).astype(F32)
        for half in range(2)
    ]
    hot = jnp.concatenate(
        [jnp.concatenate([hot[0], zeros], axis=1), jnp.concatenate([zeros, hot[1]], axis=1)],
        axis=0,
    ).astype(BF16)
    delay = mm(delay_ref[couple], hot)
    re = raw[:NF] * delay[:NF] - raw[NF:] * delay[NF:]
    im = raw[:NF] * delay[NF:] + raw[NF:] * delay[:NF]
    matrix_ref[:, couple, :, :receivers] = interleave(
        re[:, :receivers], re[:, receivers:]
    ).astype(BF16)
    matrix_ref[:, couple, :, receivers:] = interleave(
        im[:, :receivers], im[:, receivers:]
    ).astype(BF16)


def make_sums(first, rcv_index, matrix_ref, vector_ref, kept_ref, gather, onset_ref, sum_ref):
    half = 2 * matrix_ref.shape[1]
    sets = vector_ref.shape[1] // (LANES // half // 2)

    def store(row, value):
        for one in range(sets):
            sum_ref[one * NF + row : one * NF + row + 2 * GROUP, :] = value[one]

    apply_matrix([matrix_ref], [vector_ref], kept_ref, gather, None, store)
    own = onset_ref[...].astype(F32)[:, first : first + half]
    turns = LANES // (2 * half)
    own = jnp.concatenate([own[0:1], own[1:2]] * turns, axis=1)
    own = jnp.broadcast_to(own, (2 * GROUP, LANES))
    row = lax.broadcasted_iota(jnp.int32, own.shape, 0)
    lane = lax.broadcasted_iota(jnp.int32, own.shape, 1)
    spare = (row == 0) & (lane >= LANES // 2)
    for one in range(sets):
        block = turns // 2 + (rcv_index - one * (turns // 2))
        here = (rcv_index // (turns // 2) == one) & (lane // (2 * half) == block)
        rows = slice(one * NF, one * NF + 2 * GROUP)
        value = sum_ref[rows, :].astype(F32)
        sum_ref[rows, :] = jnp.where(spare, jnp.where(here, own, 0.0), value).astype(BF16)


def first_kernel(
    gain, traces_hbm, shift_hbm, deconv_hbm, focal_hbm, onset_hbm,
    forward_hbm, taps_hbm, gather_hbm, matrix_ref, sum_ref, own_ref, vector_ref,
    shift_ref, deconv_ref, onset_ref, forward_ref, taps_ref, gather_ref,
    kept_ref, traces_ref, focal_ref, large_sem, small_sem, delay_ref,
):
    half = traces_ref.shape[0]
    fields = focal_ref.shape[0]
    small = [
        pltpu.make_async_copy(source, target, small_sem.at[place])
        for place, (source, target) in enumerate(
            [
                (forward_hbm, forward_ref),
                (deconv_hbm, deconv_ref),
                (taps_hbm, taps_ref),
                (shift_hbm, shift_ref),
                (gather_hbm, gather_ref),
                (onset_hbm, onset_ref),
            ]
        )
    ]
    large = [
        pltpu.make_async_copy(focal_hbm, focal_ref, large_sem.at[0]),
        pltpu.make_async_copy(traces_hbm.at[pl.ds(0, half)], traces_ref, large_sem.at[1]),
    ]
    for copy in small[:3] + large + small[3:]:
        copy.start()
    for copy in small[:3]:
        copy.wait()
    make_delays(0, half, forward_ref, deconv_ref, taps_ref, gain, delay_ref)
    forward = forward_ref[...]
    large[0].wait()
    for place in range(0, fields, 2):
        signals = focal_ref[place : place + 2].reshape(-1, NT)
        receivers = signals.shape[0] // 2
        spectra = mm(forward, signals, NT_DIMS)
        for one in range(2):
            field = spectra[:, one * receivers : (one + 1) * receivers]
            store_vector(vector_ref, place + one, field[:NF], field[NF:])
    own_ref[...] = focal_ref[lax.axis_index("shot")]
    for copy in small[3:] + large[1:]:
        copy.wait()
    for couple in range(half // 2):
        make_matrix(0, couple, forward, traces_ref, shift_ref, delay_ref, matrix_ref)
    make_sums(
        0, lax.axis_index("rcv"), matrix_ref, vector_ref, kept_ref, gather_ref[...], onset_ref, sum_ref
    )


def rest_kernel(
    gain, traces_ref, shift_ref, deconv_ref, onset_ref, forward_ref, taps_ref,
    gather_ref, vector_ref, matrix_ref, sum_ref, kept_ref, delay_ref,
):
    half = traces_ref.shape[0] // 2
    make_delays(half, half, forward_ref, deconv_ref, taps_ref, gain, delay_ref)
    forward = forward_ref[...]
    upper = traces_ref.at[pl.ds(half, half)]
    for couple in range(half // 2):
        make_matrix(half, couple, forward, upper, shift_ref, delay_ref, matrix_ref)
    make_sums(
        half, lax.axis_index("rcv"), matrix_ref, vector_ref, kept_ref, gather_ref[...], onset_ref, sum_ref
    )


def split_halves(first, second):
    lane = lax.broadcasted_iota(jnp.int32, first.shape, 1)
    low = lane < LANES // 2
    re = jnp.where(low, first, pltpu.roll(second, LANES // 2, 1))
    im = jnp.where(low, pltpu.roll(first, LANES // 2, 1), second)
    return jnp.concatenate([re, im], axis=0)


def mute(signal, onset):
    sample = lax.broadcasted_iota(jnp.int32, signal.shape, 0)
    folded = jnp.minimum(sample, NT - sample).astype(F32)
    return jnp.where(folded < onset, signal, 0.0)


def mute_half(mine_ref, other_ref, forward, inverse, spread_ref, vector_ref):
    shot_index = lax.axis_index("shot")
    rcv_index = lax.axis_index("rcv")
    core = shot_index % 2
    chip = shot_index // 2
    width = vector_ref.shape[-1]
    half = width // GROUP
    blocks = LANES // half
    sets = mine_ref.shape[0] // NF
    turns = blocks // 2
    owned = jnp.zeros((NT, LANES), F32)
    diagonal = same_bin(2 * NF, 2 * width)
    for couple in range(sets // 2):
        rows = slice(2 * couple * NF, 2 * (couple + 1) * NF)
        total = mine_ref[rows, :].astype(F32) + other_ref[rows, :].astype(F32)
        spectra = split_halves(total[:NF], total[NF:])
        signal = mute(mm(inverse, spectra.astype(BF16)), spectra[NF : NF + 1, :])
        owned = jnp.where(rcv_index // turns == couple, signal, owned)
        echo = mm(forward, signal.astype(BF16)).astype(BF16)
        for pair in range(blocks // 2):
            slot = (couple * (blocks // 2) + pair) ^ chip
            wide = jnp.where(diagonal, mm(echo, spread_ref[core, pair]), 0.0)
            for part in range(2):
                rows = slice(part * NF, (part + 1) * NF)
                vector_ref[:, part, slot] = interleave(
                    wide[rows, :width], wide[rows, width:]
                ).astype(BF16)
    turn = (turns - rcv_index % turns) % turns
    owned = pltpu.roll(owned, turn * (2 * half), 1)
    return jnp.transpose(owned)[: 2 * half].reshape(2, half, NT)


def mute_kernel(
    mine_ref, other_ref, forward_ref, inverse_ref, spread_ref, vector_ref, field_ref
):
    field_ref[...] = mute_half(
        mine_ref, other_ref, forward_ref[...], inverse_ref[...], spread_ref, vector_ref
    )


def adjoint_kernel(
    mine_ref, other_ref, forward_ref, inverse_ref, spread_ref,
    lower_ref, field_half_ref, first_ref, rest_ref, *refs
):
    keep_ref, far_ref, send_ref, field_ref, upper_ref = refs
    pairs = keep_ref.shape[0]
    receivers = first_ref.shape[-1] // 2
    width = lower_ref.shape[-1]
    half = width // GROUP
    field_ref[:, :half] = field_half_ref[...]
    field_ref[:, half:] = mute_half(
        mine_ref, other_ref, forward_ref[...], inverse_ref[...], spread_ref, upper_ref
    )

    def one(group):
        rows = 2 * pairs * 2 * GROUP
        vector = jnp.concatenate(
            [ref[group].reshape(rows, width) for ref in (lower_ref, upper_ref)], axis=1
        )
        matrix = jnp.concatenate(
            [ref[group].reshape(width, 2 * receivers) for ref in (first_ref, rest_ref)], axis=0
        )
        full = mm(vector, matrix).reshape(2, pairs, 2, GROUP, 2 * receivers)
        re = full[0, ..., :receivers] + full[1, ..., receivers:]
        im = full[1, ..., :receivers] - full[0, ..., receivers:]
        return re, im

    for couple in range(NG // 2):
        even = one(2 * couple)
        odd = one(2 * couple + 1)
        for part in range(2):
            both = jnp.concatenate([even[part], odd[part]], axis=2).astype(BF16)
            row = part * NF + couple * 2 * GROUP
            keep_ref[:, row : row + 2 * GROUP, :] = both[:, 0]
            far_ref[row : row + 2 * GROUP, :] = both[pairs - 1, 1]
            send_ref[:, row : row + 2 * GROUP, :] = both[: pairs - 1, 1]


def downgoing_kernel(*refs):
    parts = refs[:-6]
    focal_ref, onset_ref, forward_ref, inverse_ref, field_ref, plus_ref = refs[-6:]
    total = parts[0][...].astype(F32)
    for part in parts[1:]:
        total = total + part[...].astype(F32)
    onset = onset_ref[...].astype(F32)
    signal = mute(mm(inverse_ref[...], total.astype(BF16)), onset)
    field = focal_ref[...].astype(F32) + jnp.transpose(signal)
    field_ref[0] = field
    spectra = mm(forward_ref[...], field.astype(BF16), NT_DIMS)
    plus_ref[...] = interleave(spectra[:NF], spectra[NF:]).astype(BF16)


def turned(distance):
    return (distance & ~3) | ((distance & 1) << 1) | ((distance >> 1) & 1)


def place_fields(field_refs, vector_ref, core):
    chip = lax.axis_index("shot") // 2
    for distance, field_ref in enumerate(field_refs):
        away = jnp.where(core == 0, distance, turned(distance))
        slot = (chip ^ away) ^ lax.axis_index("rcv")
        store_vector(vector_ref, slot, *unpack(field_ref))


def near_kernel(*refs):
    place_fields(refs[:-1], refs[-1], lax.axis_index("shot") % 2)


def second_kernel(pairs, *refs):
    first_ref, rest_ref, gather_ref, near_ref = refs[pairs : pairs + 4]
    sum_refs = refs[pairs + 4 : -2]
    far_ref, kept_ref = refs[-2:]
    core = lax.axis_index("shot") % 2
    place_fields(refs[:pairs], far_ref, 1 - core)

    def store(row, value):
        for slot in range(pairs):
            sum_refs[slot][row : row + 2 * GROUP, :] = value[slot]

    core = lax.axis_index("shot") % 2
    apply_matrix(
        [first_ref, rest_ref], [near_ref, far_ref], kept_ref, gather_ref[...], core, store
    )


def final_kernel(*refs):
    parts = refs[:-3]
    onset_ref, inverse_ref, field_ref = refs[-3:]
    total = parts[0][...].astype(F32)
    for part in parts[1:]:
        total = total + part[...].astype(F32)
    spectra = split_halves(total, total).astype(BF16)
    onset = onset_ref[...].astype(F32)
    onset = jnp.concatenate([onset[0:1], onset[1:2]] * 2, axis=1)
    signal = mute(mm(inverse_ref[...], spectra), onset)
    field_ref[...] = jnp.transpose(signal)[: LANES // 2].reshape(field_ref.shape)


def emit_kernel(field_ref, out_ref):
    out_ref[...] = field_ref[...]


def vmem(count):
    return [pl.BlockSpec(memory_space=pltpu.VMEM) for _ in range(count)]


def hbm(count):
    return [pl.BlockSpec(memory_space=pltpu.HBM) for _ in range(count)]


def call(kernel, name, out_shape, in_specs, scratch=(), work=1.0e9, out_specs=None):
    if out_specs is None:
        many = isinstance(out_shape, (tuple, list))
        out_specs = vmem(len(out_shape)) if many else vmem(1)[0]
    return pl.pallas_call(
        kernel,
        name=name,
        out_shape=out_shape,
        in_specs=in_specs,
        out_specs=out_specs,
        scratch_shapes=list(scratch),
        compiler_params=pltpu.CompilerParams(vmem_limit_bytes=40 << 20),
        cost_estimate=pl.CostEstimate(flops=int(work), bytes_accessed=1 << 20, transcendentals=0),
    )


def emit(field):
    return call(
        emit_kernel, "emit", jax.ShapeDtypeStruct(field.shape, field.dtype), vmem(1), work=0.3e9
    )(field)


def exchange(value, axis, distance):
    count = lax.axis_size(axis)
    return lax.ppermute(value, axis, [(place, place ^ distance) for place in range(count)])


def add_rounded(left, right):
    return (left.astype(F32) + right.astype(F32)).astype(BF16)


def body(traces, shift_index, deconv, focal_start, onset_source, onset_receiver):
    shot_count = lax.axis_size("shot")
    rcv_count = lax.axis_size("rcv")
    sources, receivers, _ = traces.shape
    focal_total = focal_start.shape[0]
    pairs = focal_total // 2
    assert onset_source.shape[0] == 2 and pairs == rcv_count
    assert focal_total == shot_count and 4 * sources == LANES and receivers == LANES
    gain = 1.0 / math.sqrt(NT * receivers * rcv_count)
    tables = make_tables(sources)
    shape = jax.ShapeDtypeStruct
    half = sources // 2
    sets = focal_total // (LANES // half // 2)
    vector = shape((NG, focal_total, 2 * GROUP, 2 * receivers), BF16)
    half_matrix = shape((NG, half // 2, 2 * GROUP, 2 * receivers), BF16)
    half_sums = shape((sets * NF, LANES), BF16)
    half_kept = pltpu.VMEM((NG // 2 * focal_total * 2 * GROUP, sources * GROUP), BF16)
    half_delays = pltpu.VMEM((half // 2, 2 * NF, LANES), BF16)
    assert sets % 2 == 0 and half * 8 == LANES

    def buffer(value):
        return pltpu.VMEM(value.shape, value.dtype)

    inputs = (
        traces, shift_index, deconv, focal_start, onset_source,
        tables["forward"], tables["taps"], tables["gather_half"],
    )
    small = (shift_index, deconv, onset_source) + inputs[5:]
    first, first_sum, focal_own, start, *loaded = call(
        functools.partial(first_kernel, gain),
        "first",
        [
            half_matrix,
            half_sums,
            shape((receivers, NT), BF16),
            vector,
        ]
        + [shape(value.shape, value.dtype) for value in small],
        hbm(len(inputs)),
        [
            half_kept,
            pltpu.VMEM((half, receivers, NT), BF16),
            buffer(focal_start),
            pltpu.SemaphoreType.DMA((2,)),
            pltpu.SemaphoreType.DMA((6,)),
            half_delays,
        ],
        work=4.0e9,
    )(*[pltpu.with_memory_space_constraint(value, pltpu.HBM) for value in inputs])
    forward = loaded[3]
    rest, rest_sum = call(
        functools.partial(rest_kernel, gain),
        "rest",
        (half_matrix, half_sums),
        vmem(8),
        [half_kept, half_delays],
        work=3.0e9,
    )(traces, *loaded, start)

    distances = [1 << step for step in range(rcv_count.bit_length() - 1)]
    routes = [(distances, distances), (distances, distances[::-1])]

    def hop(value, step, route):
        pairs_of = [
            (shot * rcv_count + rcv, shot * rcv_count + (rcv ^ route[shot % 2][step]))
            for shot in range(shot_count)
            for rcv in range(rcv_count)
        ]
        return lax.ppermute(value, ("shot", "rcv"), pairs_of)

    mine = [first_sum, rest_sum]
    other = [hop(value, 0, route) for value, route in zip(mine, routes)]
    for step in range(1, len(distances)):
        mine = [add_rounded(left, right) for left, right in zip(mine, other)]
        other = [hop(value, step, route) for value, route in zip(mine, routes)]

    echo = shape((NG, 2, pairs, 2 * GROUP, half * GROUP), BF16)
    shared = (forward, tables["inverse"], tables["spread"])
    lower, field_half = call(
        mute_kernel,
        "mute",
        (echo, shape((2, half, NT), F32)),
        vmem(5),
        work=1.0e9,
    )(mine[0], other[0], *shared)

    keep, far, send, upgoing_first = call(
        adjoint_kernel,
        "adjoint",
        [
            shape((pairs, 2 * NF, receivers), BF16),
            shape((2 * NF, receivers), BF16),
            shape((pairs - 1, 2 * NF, receivers), BF16),
            shape((2, sources, NT), F32),
        ],
        vmem(9),
        [buffer(echo)],
        work=2.0e9,
    )(mine[1], other[1], *shared, lower, field_half, first, rest)

    far = exchange(far, "shot", 1)
    near = exchange(send, "shot", 1)
    parts = [exchange(add_rounded(keep[pairs - 1], far), "shot", 2 * (pairs - 1))]
    for distance in reversed(range(pairs - 1)):
        block = add_rounded(keep[distance], near[distance])
        parts.append(exchange(block, "shot", 2 * distance) if distance else block)

    downgoing, plus = call(
        downgoing_kernel,
        "downgoing",
        (
            shape((1, receivers, NT), F32),
            shape((NG, 2 * GROUP, receivers), BF16),
        ),
        vmem(pairs + 4),
    )(*parts, focal_own, onset_receiver, forward, tables["inverse"])

    near = [plus]
    for distance in range(1, pairs):
        routes = [
            (place, place ^ (2 * (turned(distance) if place % 2 else distance)))
            for place in range(shot_count)
        ]
        near.append(lax.ppermute(plus, "shot", routes))
    far = [exchange(value, "shot", 1) for value in near]

    half_vector = shape((NG, pairs, 2 * GROUP, 2 * receivers), BF16)
    near_vector = call(near_kernel, "near", half_vector, vmem(pairs), work=0.3e9)(*near)
    parts = call(
        functools.partial(second_kernel, pairs),
        "second",
        [shape((NF, LANES), BF16)] * pairs,
        vmem(pairs + 4),
        [
            buffer(half_vector),
            pltpu.VMEM((NG * focal_total * 2 * GROUP, sources * GROUP), BF16),
        ],
    )(*far, first, rest, tables["gather"], near_vector)

    parts = [
        exchange(parts[distance], "rcv", distance) for distance in reversed(range(1, rcv_count))
    ] + [parts[0]]
    upgoing_second = call(
        final_kernel, "final", shape((2, sources, NT), F32), vmem(len(parts) + 2)
    )(*parts, loaded[2], tables["inverse"])
    return (emit(upgoing_first), emit(downgoing), upgoing_second)


def solution(mesh):
    placed = (
        P("shot", "rcv", None),
        P("shot", "rcv"),
        P("shot", None),
        P(None, "rcv", None),
        P("rcv", "shot"),
        P("shot", "rcv"),
    )
    return jax.shard_map(
        body,
        mesh=mesh,
        in_specs=placed,
        out_specs=(P("rcv", "shot", None), P("shot", "rcv", None), P("rcv", "shot", None)),
        check_vma=False,
    )
```
